32 devices in a mesh: group: 2 (over y), tp: 8 (over z, x), pair: 2 (over core).
Axes of the slice: x: 2, y: 2, z: 4, core: 2. Of those that a mesh axis runs over, the one named last changes fastest.
Arguments:
- hidden_in: bfloat16 [1024, 8192], P(('group', 'pair'), 'tp'), parts along dimension 0, may hold values from -2.5 to 2.5
- norm_gain: float32 [8192], replicated, may hold values from 0.1 to 1.9
- query_weight: bfloat16 [8192, 8192], P('tp', 'pair'), may hold values from -5 to 5
- key_weight: bfloat16 [1024, 8192], P('tp', 'pair'), may hold values from -1 to 1
- value_weight: bfloat16 [1024, 8192], P('tp', 'pair'), may hold values from -0.0625 to 0.0625
- output_weight: bfloat16 [8192, 8192], P('tp', 'pair'), may hold values from -0.0625 to 0.0625
- lengths: int32 [4, 4], P(('group', 'pair')), parts along dimension 0, may hold values from 1 to 128, 256 in all within a row
Outputs:
- layer_out: bfloat16 [1024, 8192], P(('group', 'pair'), 'tp'), parts along dimension 0
The draws below stay inside these ranges and needn't reach their ends.
There are 2 independent parts, one for each index of `group`. The reference program is written for one: setup_inputs(seed, part) draws one part's arguments, and reference() takes and returns one part's arrays. A program takes and returns all parts, laid end to end along the dimension named above; an argument that names none is the same for every part. Nothing has to cross between parts.
Inputs may be any that keep to these rules, and one draw needn't show every extreme that they name: The 4 lengths of a prompt block sum to 256; one of them equals 128.
All inputs are finite; a program needn't handle non-finite values.
Results may differ from the reference program's by a relative error of at most 0.007.
Values may be sent and summed in bfloat16 or wider, within the bound.
No kernel may reach another device: no remote copies, remote signals or barrier semaphores. Data moves between devices by JAX's collectives and lax.ppermute only.
A program may use at most 128 MiB of HBM per device.

```python
import math
import jax
import jax.numpy as jnp
import numpy as np
from jax import lax

D = 8192
HQ = 64
KVH = 8
HD = 128
STRETCH = 256
NREQ = 4
STRETCHES = 2
TOKENS = 512


def key_base(key):
    fresh = jax.random.fold_in(key, 7)
    return jnp.clip(jax.random.normal(fresh, (KVH * HD, D), jnp.float32), -6.0, 6.0) * D ** (-0.5)


def draw_key_weight(key, part):
    return key_base(key).astype(jnp.bfloat16)


def draw_query_weight(key, part):
    noise = jnp.clip(jax.random.normal(jax.random.fold_in(key, 13), (HQ * HD, D), jnp.float32), -6.0, 6.0) * D ** (-0.5)
    return noise.astype(jnp.bfloat16)


def level_of(rng, extent, split, smallest, top_value):
    gain = 1.0
    for axis_at, shards_of in split:
        draws = jax.random.uniform(jax.random.fold_in(jax.random.fold_in(rng, 6), axis_at), (shards_of,), jnp.float32, smallest / len(split), top_value / len(split))
        gain = gain * jnp.repeat(jnp.exp(draws), extent[axis_at] // shards_of).reshape((-1,) + (1,) * (len(extent) - 1 - axis_at))
    return gain


def length_profile(number_of, total, limit, lean):
    portions = [(1 << 20) // math.isqrt(standing ** lean) + 1 for standing in range(2, number_of + 1)]
    spare, given = total - limit - (number_of - 1), [1] * (number_of - 1)
    while spare > 0:
        movable = [i for i in range(number_of - 1) if given[i] < limit]
        mass, remaining = sum([portions[i] for i in movable]), spare
        for i in movable:
            more = min(limit - given[i], max(1, remaining * portions[i] // mass), spare)
            given[i] = given[i] + more
            spare = spare - more
    return np.array([limit] + given)


def ragged(key, count, total, reach, skew):
    if count == 2:
        one = jax.random.randint(key, (), max(1, total - reach), min(reach, total - 1) + 1)
        return jnp.stack([one, total - one])
    sizes = jnp.asarray(length_profile(count, total, reach, skew), jnp.int32)
    pairs = (count - 1) // 2
    giver, taker = sizes[1:1 + 2 * pairs:2], sizes[2:2 + 2 * pairs:2]
    margin = jnp.minimum(giver - 1, reach - taker)
    shifted = jax.random.randint(jax.random.fold_in(key, 1), (pairs,), 0, 1 << 20) % (margin + 1)
    sizes = sizes.at[1:1 + 2 * pairs:2].set(giver - shifted).at[2:2 + 2 * pairs:2].set(taker + shifted)
    return sizes[jax.random.permutation(jax.random.fold_in(key, 2), count)]


def normal_values(own_key, extent, scale, limit, cuts=(), kind=jnp.bfloat16):
    result = jax.random.normal(own_key, extent, jnp.float32) * scale
    if len(cuts) > 0:
        result = level_of(own_key, extent, cuts, -0.22, 0.18) * result
    return jnp.clip(result, min=-limit, max=limit).astype(kind)


def setup_inputs(seed: int = 0, part: int = 0) -> dict:
    keys = jax.random.split(jax.random.key(seed), 8)
    part_keys = jax.random.split(jax.random.fold_in(keys[7], part), 8)
    return {
        "hidden_in": normal_values(part_keys[0], (TOKENS, D), 0.3, 2.5, ((0, 2), (1, 8))),
        "norm_gain": jnp.clip(1.0 + 0.18 * jax.random.normal(keys[1], (D,), jnp.float32), 0.1, 1.9),
        "query_weight": draw_query_weight(jax.random.fold_in(keys[7], 71), part),
        "key_weight": draw_key_weight(jax.random.fold_in(keys[7], 71), part),
        "value_weight": normal_values(keys[4], (KVH * HD, D), D ** -0.5, 0.0625, ((0, 8), (1, 2))),
        "output_weight": normal_values(keys[5], (D, HQ * HD), (HQ * HD) ** -0.5, 0.0625, ((0, 8), (1, 2))),
        "lengths": jax.vmap(lambda own: ragged(own, NREQ, STRETCH, STRETCH // 2, 2))(jax.random.split(part_keys[6], STRETCHES)).reshape((STRETCHES, NREQ)).astype(jnp.int32),
    }


THETA = 500000.0

def token_layout(lengths):
    lengths = lengths.astype(jnp.int32)
    ends = jnp.cumsum(lengths, axis=1)
    offsets = jnp.arange(STRETCH, dtype=jnp.int32)
    finished = ends[:, None, :] <= offsets[None, :, None]
    request = lax.optimization_barrier(jnp.sum(finished.astype(jnp.int32), axis=2))
    position = offsets[None, :] - lax.optimization_barrier(jnp.sum(jnp.where(finished, lengths[:, None, :], 0), axis=2))
    return (request, position)

def scaled_freq(dims):
    freq = jnp.exp(dims.astype(jnp.float32) * (-math.log(THETA) / HD))
    wavelen = 2.0 * math.pi / freq
    smooth = (8192.0 / wavelen - 1.0) / 3.0
    middle = (1.0 - smooth) * freq / 8.0 + smooth * freq
    return jnp.where(wavelen < 2048.0, freq, jnp.where(wavelen > 8192.0, freq / 8.0, middle))

def rotary(projected, position, dims):
    freq = scaled_freq(dims[0::2])
    angle = position.astype(jnp.float32)[:, None] * freq[None, :]
    cosine = jnp.cos(angle)
    sine = jnp.sin(angle)
    first = projected[:, 0::2]
    second = projected[:, 1::2]
    turned = jnp.stack([first * cosine - second * sine, first * sine + second * cosine], axis=-1)
    return turned.reshape(projected.shape)

def attend(query, key, value, request, stretches, heads, groups):
    repeat = heads // groups
    query_blocks = query.astype(jnp.float32).reshape(stretches, STRETCH, groups, repeat, HD)
    key_blocks = key.astype(jnp.float32).reshape(stretches, STRETCH, groups, HD)
    value_blocks = value.astype(jnp.float32).reshape(stretches, STRETCH, groups, HD)
    scores = jnp.einsum('cqgrd,ckgd->cgrqk', query_blocks, key_blocks) * (1.0 / math.sqrt(HD))
    offsets = jnp.arange(STRETCH, dtype=jnp.int32)
    keep = (request[:, :, None] == request[:, None, :]) & (offsets[:, None] >= offsets[None, :])[None]
    scores = jnp.where(keep[:, None, None], scores, -1e+30)
    top = lax.optimization_barrier(jnp.max(scores, axis=-1, keepdims=True))
    weights = jnp.exp(scores - top)
    probs = (weights / lax.optimization_barrier(jnp.sum(weights, axis=-1, keepdims=True))).astype(jnp.bfloat16)
    attended = jnp.einsum('cgrqk,ckgd->cqgrd', probs.astype(jnp.float32), value_blocks)
    return attended.reshape(stretches * STRETCH, heads * HD).astype(jnp.bfloat16)

def contract(left, right):
    return lax.dot_general(left, right, (((1,), (1,)), ((), ())), preferred_element_type=jnp.float32)

def reference(hidden_in, norm_gain, query_weight, key_weight, value_weight, output_weight, lengths):
    stretches = lengths.shape[0]
    request, position = token_layout(lengths)
    position = position.reshape(-1)
    stream = hidden_in.astype(jnp.float32)
    mean_square = lax.optimization_barrier(jnp.mean(stream * stream, axis=1, keepdims=True))
    normed = (stream * lax.rsqrt(mean_square + 1e-05) * norm_gain.astype(jnp.float32)[None, :]).astype(jnp.bfloat16)
    query_dims = jnp.arange(HQ * HD, dtype=jnp.int32) % HD
    key_dims = jnp.arange(KVH * HD, dtype=jnp.int32) % HD
    query = rotary(contract(normed, query_weight), position, query_dims).astype(jnp.bfloat16)
    key = rotary(contract(normed, key_weight), position, key_dims).astype(jnp.bfloat16)
    value = contract(normed, value_weight).astype(jnp.bfloat16)
    attended = attend(query, key, value, request, stretches, HQ, KVH)
    projected = contract(attended, output_weight)
    return (stream + projected).astype(jnp.bfloat16)
```

```python
import math

import jax
import jax.numpy as jnp
from jax import lax
from jax.experimental import pallas as pl
from jax.experimental.pallas import tpu as pltpu
from jax.sharding import PartitionSpec as P

HQ = 64
KVH = 8
HD = 128
STRETCH = 256


THETA = 500000.0


def shortened(shard):

    def short(part):
        return part.astype(jnp.bfloat16) if part.dtype == jnp.float32 else part

    return jax.tree.map(short, shard)


def partner(shard, axis, apart):
    return lax.ppermute(shard, axis, [(i, i ^ 1 << apart) for i in range(lax.axis_size(axis))])


def token_layout(lengths):
    ends = jnp.cumsum(lengths, axis=1)
    offsets = jnp.arange(STRETCH, dtype=jnp.int32)
    finished = ends[:, None, :] <= offsets[None, :, None]
    request = jnp.sum(finished.astype(jnp.int32), axis=2)
    position = offsets[None, :] - jnp.sum(jnp.where(finished, lengths[:, None, :], 0), axis=2)
    return (request, position)


def scaled_freq(dims):
    freq = jnp.exp(dims.astype(jnp.float32) * (-math.log(THETA) / HD))
    wavelen = 2.0 * math.pi / freq
    smooth = (8192.0 / wavelen - 1.0) / 3.0
    middle = (1.0 - smooth) * freq / 8.0 + smooth * freq
    return jnp.where(wavelen < 2048.0, freq, jnp.where(wavelen > 8192.0, freq / 8.0, middle))


def rotary(projected, position, dims):
    freq = scaled_freq(dims[0::2])
    angle = position.astype(jnp.float32)[:, None] * freq[None, :]
    cosine = jnp.cos(angle)
    sine = jnp.sin(angle)
    first = projected[:, 0::2]
    second = projected[:, 1::2]
    turned = jnp.stack([first * cosine - second * sine, first * sine + second * cosine], axis=-1)
    return turned.reshape(projected.shape)


def attend(query, key, value, request, stretches, heads, groups):
    repeat = heads // groups
    query_blocks = query.reshape(stretches, STRETCH, groups, repeat, HD)
    key_blocks = key.reshape(stretches, STRETCH, groups, HD)
    value_blocks = value.reshape(stretches, STRETCH, groups, HD)
    scores = jnp.einsum(
        "cqgrd,ckgd->cgrqk", query_blocks, key_blocks, preferred_element_type=jnp.float32
    ) * (1.0 / math.sqrt(HD))
    offsets = jnp.arange(STRETCH, dtype=jnp.int32)
    keep = (request[:, :, None] == request[:, None, :]) & (offsets[:, None] >= offsets[None, :])[
        None
    ]
    scores = jnp.where(keep[:, None, None], scores, -1e30)
    top = jnp.max(scores, axis=-1, keepdims=True)
    weights = jnp.exp(scores - top)
    probs = (weights / jnp.sum(weights, axis=-1, keepdims=True)).astype(jnp.bfloat16)
    attended = jnp.einsum(
        "cgrqk,ckgd->cqgrd", probs, value_blocks, preferred_element_type=jnp.float32
    )
    return attended.reshape(stretches * STRETCH, heads * HD).astype(jnp.bfloat16)


def contract(left, right):
    return lax.dot_general(
        left, right, (((1,), (1,)), ((), ())), preferred_element_type=jnp.float32
    )


def bit_count(number):
    return number.bit_length() - 1


def assemble(parts, needed_bits, device, axis):
    for bit_index in range(max(needed_bits)):
        moving = [piece for piece, needed in zip(parts, needed_bits) if bit_index < needed]
        widths = [piece.shape[axis] for piece in moving]
        sent = jnp.concatenate(moving, axis=axis)
        arrived = partner(shortened(sent), "tp", bit_index).astype(sent.dtype)
        upper = device // 2**bit_index % 2 == 1
        cuts = []
        running = 0
        for width in widths[:-1]:
            running = running + width
            cuts.append(running)
        received = jnp.split(arrived, cuts, axis=axis)
        joined = []
        counter = 0
        for piece, needed in zip(parts, needed_bits):
            if bit_index < needed:
                other = received[counter]
                counter = counter + 1
                piece = jnp.where(
                    upper,
                    jnp.concatenate([other, piece], axis=axis),
                    jnp.concatenate([piece, other], axis=axis),
                )
            joined.append(piece)
        parts = joined
    return parts


def project(normed, query_rows, key_rows, value_rows, output_rows):
    query_full, key_full, value_full, output_full = (
        lax.all_gather(query_rows, "pair", axis=1, tiled=True),
        lax.all_gather(key_rows, "pair", axis=1, tiled=True),
        lax.all_gather(value_rows, "pair", axis=1, tiled=True),
        lax.all_gather(output_rows, "pair", axis=1, tiled=True),
    )
    query_pre = contract(normed, query_full)
    key_pre = contract(normed, key_full)
    value_pre = contract(normed, value_full)
    return (query_pre, key_pre, value_pre, output_full)


def general_body(hidden_in, norm_gain, query_weight, key_weight, value_weight, output_weight, lengths):
    tp_count = lax.axis_size("tp")
    device = lax.axis_index("tp")
    query_bits = bit_count(max(1, tp_count // HQ))
    group_bits = bit_count(max(1, tp_count // KVH))
    needed_bits = [query_bits, group_bits, group_bits]
    query_cols = query_weight.shape[0]
    stretches = lengths.shape[0]
    request, position = token_layout(lengths)
    position = position.reshape(-1)
    full_rows = lax.all_gather(hidden_in, "tp", axis=1, tiled=True)
    stream = full_rows.astype(jnp.float32)
    mean_square = jnp.mean(stream * stream, axis=1, keepdims=True)
    normed = (stream * lax.rsqrt(mean_square + 1e-05) * norm_gain[None, :]).astype(jnp.bfloat16)
    query_block, key_block, value_block = assemble(
        [query_weight, key_weight, value_weight], needed_bits, device, 0
    )
    query_pre, key_pre, value_pre, output_full = project(
        normed, query_block, key_block, value_block, output_weight
    )
    query_dims = jnp.arange(query_pre.shape[1], dtype=jnp.int32) % HD
    key_dims = jnp.arange(key_pre.shape[1], dtype=jnp.int32) % HD
    query = rotary(query_pre, position, query_dims).astype(jnp.bfloat16)
    key = rotary(key_pre, position, key_dims).astype(jnp.bfloat16)
    value = value_pre.astype(jnp.bfloat16)
    heads = query.shape[1] // HD
    groups = key.shape[1] // HD
    attended = attend(query, key, value, request, stretches, heads, groups)
    own_start = device * query_cols % (heads * HD)
    own_columns = lax.dynamic_slice_in_dim(attended, own_start, query_cols, 1)
    projected = contract(lax.all_gather(own_columns, "tp", axis=1, tiled=True), output_full)
    return (hidden_in.astype(jnp.float32) + projected).astype(jnp.bfloat16)


RING = 8
ROWS = STRETCH // 2
UNIT = 1024
CHUNK = 256
ORDER = (0, 1, -1, -2, 2, 3, -3, -4)


def ring_place(t):
    return t // 2 if t % 2 == 0 else RING - 1 - t // 2


def ring_member(place):
    return 2 * place if place < RING // 2 else 2 * RING - 1 - 2 * place


def ring_swap(later):
    pairs = []
    for t in range(RING):
        for p in range(2):
            place = ring_place(t)
            step = 1 if (place + p + later) % 2 == 0 else -1
            pairs.append((t * 2 + p, ring_member((place + step) % RING) * 2 + p))
    return pairs


def swapped(shard, later):
    return lax.ppermute(shard, ("tp", "pair"), ring_swap(later))


def gather_stream(own):
    first = swapped(own, 0)
    second = swapped(jnp.concatenate([own, first], axis=0), 1)
    third = swapped(second, 0)
    fourth = swapped(third, 1)
    return first, second, third, fourth


def unit_of(index):
    t = lax.axis_index("tp")
    place = jnp.where(t % 2 == 0, t // 2, RING - 1 - t // 2)
    step = 1 - 2 * ((place + lax.axis_index("pair")) % 2)
    offset = jnp.int32(ORDER[0])
    for k in range(1, len(ORDER)):
        offset = jnp.where(index == k, ORDER[k], offset)
    where = (place + offset * step + RING) % RING
    return jnp.where(where < RING // 2, 2 * where, 2 * RING - 1 - 2 * where)


def fetch(pairs, slot, sems, index):
    t = unit_of(index)
    mine = t // (RING // 2) == lax.axis_index("pair")
    cols = pl.ds(pl.multiple_of(t % (RING // 2) * UNIT, UNIT), UNIT)
    for n, (own, other, buf) in enumerate(pairs):

        @pl.when(mine)
        def _():
            pltpu.make_async_copy(own.at[:, cols], buf.at[slot], sems.at[n, slot]).start()

        @pl.when(jnp.logical_not(mine))
        def _():
            pltpu.make_async_copy(other.at[:, cols], buf.at[slot], sems.at[n, slot]).start()


def arrive(pairs, slot, sems):
    for n, (own, _, buf) in enumerate(pairs):
        pltpu.make_async_copy(own.at[:, pl.ds(0, UNIT)], buf.at[slot], sems.at[n, slot]).wait()


def scaled_unit(part, gain_ref, index):
    gain = gain_ref[pl.ds(unit_of(index), 1), :]
    stream = part.astype(jnp.float32)
    square = stream * stream
    sums = square[:, :128]
    for k in range(1, UNIT // 128):
        sums = sums + square[:, k * 128 : (k + 1) * 128]
    return (stream * gain).astype(jnp.bfloat16), sums


def add_units(xs, acc, pairs, sems, first, count, start):
    def unit_step(u, carry):
        slot = u % 2

        @pl.when(u + 1 < count)
        def _():
            fetch(pairs, (u + 1) % 2, sems, first + u + 1)

        arrive(pairs, slot, sems)
        x = xs[u]
        at = 0
        for _, _, buf in pairs:
            for row in range(0, buf.shape[1], CHUNK):
                size = min(CHUNK, buf.shape[1] - row)
                product = contract(x, buf[slot, row : row + size, :])
                n, lane = at // CHUNK, at % CHUNK
                if start:
                    old = acc[n, :, lane : lane + size]
                    acc[n, :, lane : lane + size] = jnp.where(u == 0, product, old + product)
                else:
                    acc[n, :, lane : lane + size] += product
                at += size
        return carry

    lax.fori_loop(0, count, unit_step, 0)


VM = pl.BlockSpec(memory_space=pltpu.VMEM)
ANY = pl.BlockSpec(memory_space=pl.ANY)
SM = pl.BlockSpec(memory_space=pltpu.SMEM)


def params(mib):
    return pltpu.CompilerParams(vmem_limit_bytes=mib * 2**20)


def cost(rows, units, width):
    return pl.CostEstimate(
        flops=2 * rows * units * UNIT * width,
        bytes_accessed=2 * units * UNIT * width + 4 * rows * width,
        transcendentals=0,
    )


def pair_buffers(widths):
    return [pltpu.VMEM((2, w, UNIT), jnp.bfloat16) for w in widths]


def early_kernel(own, a1, b1, a2, b2, gain, *refs):
    q0, q1, k0, k1, v0, v1, acc, sums, xs, qb, kb, vb, sems = refs
    pairs = ((q0, q1, qb), (k0, k1, kb), (v0, v1, vb))
    fetch(pairs, 0, sems, 0)
    parts = (
        (own[:ROWS, :], own[ROWS:, :]),
        (a1[...], b1[...]),
        (a2[:ROWS, :], b2[:ROWS, :]),
        (a2[ROWS:, :], b2[ROWS:, :]),
    )
    for n, halves in enumerate(parts):
        for s, part in enumerate(halves):
            rows = slice(s * ROWS, (s + 1) * ROWS)
            scaled, square = scaled_unit(part, gain, n)
            xs[n, rows, :] = scaled
            sums[rows, :] = square if n == 0 else sums[rows, :] + square
    add_units(xs, acc, pairs, sems, 0, 4, True)


def middle_kernel(a3, b3, gain, acc_in, sums_in, *refs):
    q0, q1, k0, k1, v0, v1, acc, sums, xs, qb, kb, vb, sems = refs
    pairs = ((q0, q1, qb), (k0, k1, kb), (v0, v1, vb))
    fetch(pairs, 0, sems, 4)
    for n in range(2):
        for s, ref in enumerate((a3, b3)):
            rows = slice(s * ROWS, (s + 1) * ROWS)
            scaled, square = scaled_unit(ref[n * ROWS : (n + 1) * ROWS, :], gain, 4 + n)
            xs[n, rows, :] = scaled
            sums[rows, :] = (sums_in if n == 0 else sums)[rows, :] + square
    acc[...] = acc_in[...]
    add_units(xs, acc, pairs, sems, 4, 2, False)


def turned_heads(part, cosine, sine):
    lane = lax.broadcasted_iota(jnp.int32, part.shape, 1)
    other = jnp.where(lane % 2 == 0, pltpu.roll(part, HD - 1, 1), pltpu.roll(part, 1, 1))
    return (part * cosine + other * sine).astype(jnp.bfloat16)


def last_kernel(half, *refs):
    lens, new, gain, acc_in, sums_in, cosine, sine = refs[:7]
    refs = refs[7:]
    if half:
        key_early, value_early = refs[:2]
        refs = refs[2:]
    q0, q1, k0, k1, v0, v1, attended, key_out, value_out, acc, xs, qb, kb, vb, sems = refs
    pairs = ((q0, q1, qb), (k0, k1, kb), (v0, v1, vb))
    fetch(pairs, 0, sems, 6)
    rows = slice(half * ROWS, (half + 1) * ROWS)
    squares = sums_in[rows, :]
    for n in range(2):
        scaled, square = scaled_unit(new[n * ROWS : (n + 1) * ROWS, :], gain, 6 + n)
        xs[n] = scaled
        squares = squares + square
    acc[...] = acc_in[:, rows, :]
    add_units(xs, acc, pairs, sems, 6, 2, False)
    factor = lax.rsqrt(jnp.sum(squares, axis=1, keepdims=True) / (RING * UNIT) + 1e-05)
    cos, sin = cosine[rows, :], sine[rows, :]
    heads = UNIT // HD
    key = turned_heads(acc[heads // 2, :, :HD] * factor, cos, sin)
    value = (acc[heads // 2, :, HD:] * factor).astype(jnp.bfloat16)
    key_out[...] = key
    value_out[...] = value
    if half:
        key = jnp.concatenate([key_early[...], key], axis=0)
        value = jnp.concatenate([value_early[...], value], axis=0)
    shape = (ROWS, (half + 1) * ROWS)
    row = lax.broadcasted_iota(jnp.int32, shape, 0) + half * ROWS
    col = lax.broadcasted_iota(jnp.int32, shape, 1)
    row_request = jnp.zeros(shape, jnp.int32)
    col_request = jnp.zeros(shape, jnp.int32)
    end = jnp.int32(0)
    for k in range(lens.shape[1]):
        end = end + lens[0, k]
        row_request += (row >= end).astype(jnp.int32)
        col_request += (col >= end).astype(jnp.int32)
    keep = (row_request == col_request) & (row >= col)
    for h in range(heads):
        lane = h % 2 * HD
        query = turned_heads(acc[h // 2, :, lane : lane + HD] * factor, cos, sin)
        scores = contract(query, key) * (1.0 / math.sqrt(HD))
        scores = jnp.where(keep, scores, -1e30)
        weights = jnp.exp(scores - jnp.max(scores, axis=1, keepdims=True))
        probs = (weights / jnp.sum(weights, axis=1, keepdims=True)).astype(jnp.bfloat16)
        out = jnp.dot(probs, value, preferred_element_type=jnp.float32)
        attended[:, h * HD : (h + 1) * HD] = out.astype(jnp.bfloat16)


def out_early_kernel(a0, b0, a1, b1, a2, b2, w0, w1, acc, xs, wb, sems):
    pairs = ((w0, w1, wb),)
    fetch(pairs, 0, sems, 0)
    for s, refs in enumerate(((a0, a1, a2), (b0, b1, b2))):
        rows = slice(s * ROWS, (s + 1) * ROWS)
        xs[0, rows, :] = refs[0][...]
        xs[1, rows, :] = refs[1][...]
        xs[2, rows, :] = refs[2][:ROWS, :]
        xs[3, rows, :] = refs[2][ROWS:, :]
    add_units(xs, acc, pairs, sems, 0, 4, True)


def out_middle_kernel(a3, b3, acc_in, w0, w1, acc, xs, wb, sems):
    pairs = ((w0, w1, wb),)
    fetch(pairs, 0, sems, 4)
    for s, ref in enumerate((a3, b3)):
        rows = slice(s * ROWS, (s + 1) * ROWS)
        xs[0, rows, :] = ref[:ROWS, :]
        xs[1, rows, :] = ref[ROWS:, :]
    acc[...] = acc_in[...]
    add_units(xs, acc, pairs, sems, 4, 2, False)


def out_last_kernel(half, new, hidden, acc_in, w0, w1, *refs):
    if half:
        refs = refs[1:]
    out, acc, xs, wb, sems = refs
    pairs = ((w0, w1, wb),)
    fetch(pairs, 0, sems, 6)
    xs[0] = new[:ROWS, :]
    xs[1] = new[ROWS:, :]
    acc[...] = acc_in[...]
    add_units(xs, acc, pairs, sems, 6, 2, False)
    for n in range(UNIT // CHUNK):
        cols = slice(n * CHUNK, (n + 1) * CHUNK)
        out[:, cols] = (hidden[:, cols].astype(jnp.float32) + acc[n]).astype(jnp.bfloat16)


def ring_body(hidden_in, norm_gain, query_weight, key_weight, value_weight, output_weight, lengths):
    f32, bf16 = jnp.float32, jnp.bfloat16
    qkv = query_weight.shape[0] + key_weight.shape[0] + value_weight.shape[0]
    widths = [query_weight.shape[0], key_weight.shape[0], value_weight.shape[0]]
    other_query, other_key, other_value = (
        partner(w, "pair", 0) for w in (query_weight, key_weight, value_weight)
    )
    weights = (query_weight, other_query, key_weight, other_key, value_weight, other_value)
    a0, b0 = hidden_in[:ROWS], hidden_in[ROWS:]
    a1, a2, a3, a4 = gather_stream(a0)
    b1, b2, b3, b4 = gather_stream(b0)
    gain = norm_gain.reshape(RING, UNIT)
    _, position = token_layout(lengths)
    lane = jnp.arange(HD, dtype=jnp.int32)
    angle = position.reshape(-1).astype(f32)[:, None] * scaled_freq(lane - lane % 2)[None, :]
    cosine = jnp.cos(angle)
    sine = jnp.sin(angle) * jnp.where(lane % 2 == 0, -1.0, 1.0)[None, :]

    acc_shape = (qkv // CHUNK, STRETCH, CHUNK)
    sums_shape = jax.ShapeDtypeStruct((STRETCH, 128), f32)
    sems = pltpu.SemaphoreType.DMA((3, 2))
    acc, sums = pl.pallas_call(
        early_kernel,
        out_shape=(jax.ShapeDtypeStruct(acc_shape, f32), sums_shape),
        in_specs=[VM] * 6 + [ANY] * 6,
        out_specs=(VM, VM),
        scratch_shapes=[pltpu.VMEM((4, STRETCH, UNIT), bf16), *pair_buffers(widths), sems],
        compiler_params=params(24),
        cost_estimate=cost(STRETCH, 4, qkv),
        name="early",
    )(hidden_in, a1, b1, a2, b2, gain, *weights)
    acc, sums = pl.pallas_call(
        middle_kernel,
        out_shape=(jax.ShapeDtypeStruct(acc_shape, f32), sums_shape),
        in_specs=[VM] * 5 + [ANY] * 6,
        out_specs=(VM, VM),
        scratch_shapes=[pltpu.VMEM((2, STRETCH, UNIT), bf16), *pair_buffers(widths), sems],
        compiler_params=params(24),
        cost_estimate=cost(STRETCH, 2, qkv),
        name="middle",
    )(a3, b3, gain, acc, sums, *weights)

    def last(half, new, early):
        kv = jax.ShapeDtypeStruct((ROWS, HD), bf16)
        return pl.pallas_call(
            lambda *refs: last_kernel(half, *refs),
            out_shape=(jax.ShapeDtypeStruct((ROWS, UNIT), bf16), kv, kv),
            in_specs=[SM] + [VM] * (6 + len(early)) + [ANY] * 6,
            out_specs=(VM, VM, VM),
            scratch_shapes=[
                pltpu.VMEM((qkv // CHUNK, ROWS, CHUNK), f32),
                pltpu.VMEM((2, ROWS, UNIT), bf16),
                *pair_buffers(widths),
                sems,
            ],
            compiler_params=params(24),
            cost_estimate=cost(ROWS, 4, qkv),
            name=f"last{half}",
        )(lengths, new, gain, acc, sums, cosine, sine, *early, *weights)

    att_a, key_a, value_a = last(0, a4, ())
    att_b, _, _ = last(1, b4, (key_a, value_a))

    other_output = partner(output_weight, "pair", 0)
    a1, a2, a3, a4 = gather_stream(att_a)
    b1, b2, b3, b4 = gather_stream(att_b)
    width = output_weight.shape[0]
    acc_shape = (width // CHUNK, STRETCH, CHUNK)
    sems = pltpu.SemaphoreType.DMA((1, 2))
    acc = pl.pallas_call(
        out_early_kernel,
        out_shape=jax.ShapeDtypeStruct(acc_shape, f32),
        in_specs=[VM] * 6 + [ANY] * 2,
        out_specs=VM,
        scratch_shapes=[pltpu.VMEM((4, STRETCH, UNIT), bf16), *pair_buffers([width]), sems],
        compiler_params=params(20),
        cost_estimate=cost(STRETCH, 4, width),
        name="out_early",
    )(att_a, att_b, a1, b1, a2, b2, output_weight, other_output)
    acc = pl.pallas_call(
        out_middle_kernel,
        out_shape=jax.ShapeDtypeStruct(acc_shape, f32),
        in_specs=[VM] * 3 + [ANY] * 2,
        out_specs=VM,
        scratch_shapes=[pltpu.VMEM((2, STRETCH, UNIT), bf16), *pair_buffers([width]), sems],
        compiler_params=params(20),
        cost_estimate=cost(STRETCH, 2, width),
        name="out_middle",
    )(a3, b3, acc, output_weight, other_output)

    def out_last(half, new, *partial):
        part = pl.BlockSpec((ROWS, UNIT), lambda i: (half, 0))
        return pl.pallas_call(
            lambda *refs: out_last_kernel(half, *refs),
            grid=(1,),
            out_shape=jax.ShapeDtypeStruct((STRETCH, UNIT), bf16),
            in_specs=[
                VM,
                part,
                pl.BlockSpec((width // CHUNK, ROWS, CHUNK), lambda i: (0, half, 0)),
            ]
            + [ANY] * (2 + half),
            out_specs=part,
            scratch_shapes=[
                pltpu.VMEM((width // CHUNK, ROWS, CHUNK), f32),
                pltpu.VMEM((2, ROWS, UNIT), bf16),
                *pair_buffers([width]),
                sems,
            ],
            input_output_aliases={5: 0} if half else {},
            compiler_params=params(20),
            cost_estimate=cost(ROWS, 4, width),
            name=f"out_last{half}",
        )(new, hidden_in, acc, output_weight, other_output, *partial)

    return out_last(1, b4, out_last(0, a4))


def fits_ring(mesh):
    return dict(mesh.shape)["tp"] == RING and dict(mesh.shape)["pair"] == 2


def solution(mesh):
    placed = (
        P(("group", "pair"), "tp"),
        P(),
        P("tp", "pair"),
        P("tp", "pair"),
        P("tp", "pair"),
        P("tp", "pair"),
        P(("group", "pair"), None),
    )
    body = ring_body if fits_ring(mesh) else general_body
    return jax.shard_map(
        body, mesh=mesh, in_specs=placed, out_specs=P(("group", "pair"), "tp"), check_vma=False
    )
```

```python
import math

import jax
import jax.numpy as jnp
from jax import lax
from jax.experimental import pallas as pl
from jax.experimental.pallas import tpu as pltpu
from jax.sharding import PartitionSpec as P

HQ = 64
KVH = 8
HD = 128
STRETCH = 256


THETA = 500000.0


def shortened(shard):

    def short(part):
        return part.astype(jnp.bfloat16) if part.dtype == jnp.float32 else part

    return jax.tree.map(short, shard)


def partner(shard, axis, apart):
    return lax.ppermute(shard, axis, [(i, i ^ 1 << apart) for i in range(lax.axis_size(axis))])


def token_layout(lengths):
    ends = jnp.cumsum(lengths, axis=1)
    offsets = jnp.arange(STRETCH, dtype=jnp.int32)
    finished = ends[:, None, :] <= offsets[None, :, None]
    request = jnp.sum(finished.astype(jnp.int32), axis=2)
    position = offsets[None, :] - jnp.sum(jnp.where(finished, lengths[:, None, :], 0), axis=2)
    return (request, position)


def scaled_freq(dims):
    freq = jnp.exp(dims.astype(jnp.float32) * (-math.log(THETA) / HD))
    wavelen = 2.0 * math.pi / freq
    smooth = (8192.0 / wavelen - 1.0) / 3.0
    middle = (1.0 - smooth) * freq / 8.0 + smooth * freq
    return jnp.where(wavelen < 2048.0, freq, jnp.where(wavelen > 8192.0, freq / 8.0, middle))


def rotary(projected, position, dims):
    freq = scaled_freq(dims[0::2])
    angle = position.astype(jnp.float32)[:, None] * freq[None, :]
    cosine = jnp.cos(angle)
    sine = jnp.sin(angle)
    first = projected[:, 0::2]
    second = projected[:, 1::2]
    turned = jnp.stack([first * cosine - second * sine, first * sine + second * cosine], axis=-1)
    return turned.reshape(projected.shape)


def attend(query, key, value, request, stretches, heads, groups):
    repeat = heads // groups
    query_blocks = query.reshape(stretches, STRETCH, groups, repeat, HD)
    key_blocks = key.reshape(stretches, STRETCH, groups, HD)
    value_blocks = value.reshape(stretches, STRETCH, groups, HD)
    scores = jnp.einsum(
        "cqgrd,ckgd->cgrqk", query_blocks, key_blocks, preferred_element_type=jnp.float32
    ) * (1.0 / math.sqrt(HD))
    offsets = jnp.arange(STRETCH, dtype=jnp.int32)
    keep = (request[:, :, None] == request[:, None, :]) & (offsets[:, None] >= offsets[None, :])[
        None
    ]
    scores = jnp.where(keep[:, None, None], scores, -1e30)
    top = jnp.max(scores, axis=-1, keepdims=True)
    weights = jnp.exp(scores - top)
    probs = (weights / jnp.sum(weights, axis=-1, keepdims=True)).astype(jnp.bfloat16)
    attended = jnp.einsum(
        "cgrqk,ckgd->cqgrd", probs, value_blocks, preferred_element_type=jnp.float32
    )
    return attended.reshape(stretches * STRETCH, heads * HD).astype(jnp.bfloat16)


def contract(left, right):
    return lax.dot_general(
        left, right, (((1,), (1,)), ((), ())), preferred_element_type=jnp.float32
    )


def bit_count(number):
    return number.bit_length() - 1


def assemble(parts, needed_bits, device, axis):
    for bit_index in range(max(needed_bits)):
        moving = [piece for piece, needed in zip(parts, needed_bits) if bit_index < needed]
        widths = [piece.shape[axis] for piece in moving]
        sent = jnp.concatenate(moving, axis=axis)
        arrived = partner(shortened(sent), "tp", bit_index).astype(sent.dtype)
        upper = device // 2**bit_index % 2 == 1
        cuts = []
        running = 0
        for width in widths[:-1]:
            running = running + width
            cuts.append(running)
        received = jnp.split(arrived, cuts, axis=axis)
        joined = []
        counter = 0
        for piece, needed in zip(parts, needed_bits):
            if bit_index < needed:
                other = received[counter]
                counter = counter + 1
                piece = jnp.where(
                    upper,
                    jnp.concatenate([other, piece], axis=axis),
                    jnp.concatenate([piece, other], axis=axis),
                )
            joined.append(piece)
        parts = joined
    return parts


def project(normed, query_rows, key_rows, value_rows, output_rows):
    query_full, key_full, value_full, output_full = (
        lax.all_gather(query_rows, "pair", axis=1, tiled=True),
        lax.all_gather(key_rows, "pair", axis=1, tiled=True),
        lax.all_gather(value_rows, "pair", axis=1, tiled=True),
        lax.all_gather(output_rows, "pair", axis=1, tiled=True),
    )
    query_pre = contract(normed, query_full)
    key_pre = contract(normed, key_full)
    value_pre = contract(normed, value_full)
    return (query_pre, key_pre, value_pre, output_full)


def general_body(hidden_in, norm_gain, query_weight, key_weight, value_weight, output_weight, lengths):
    tp_count = lax.axis_size("tp")
    device = lax.axis_index("tp")
    query_bits = bit_count(max(1, tp_count // HQ))
    group_bits = bit_count(max(1, tp_count // KVH))
    needed_bits = [query_bits, group_bits, group_bits]
    query_cols = query_weight.shape[0]
    stretches = lengths.shape[0]
    request, position = token_layout(lengths)
    position = position.reshape(-1)
    full_rows = lax.all_gather(hidden_in, "tp", axis=1, tiled=True)
    stream = full_rows.astype(jnp.float32)
    mean_square = jnp.mean(stream * stream, axis=1, keepdims=True)
    normed = (stream * lax.rsqrt(mean_square + 1e-05) * norm_gain[None, :]).astype(jnp.bfloat16)
    query_block, key_block, value_block = assemble(
        [query_weight, key_weight, value_weight], needed_bits, device, 0
    )
    query_pre, key_pre, value_pre, output_full = project(
        normed, query_block, key_block, value_block, output_weight
    )
    query_dims = jnp.arange(query_pre.shape[1], dtype=jnp.int32) % HD
    key_dims = jnp.arange(key_pre.shape[1], dtype=jnp.int32) % HD
    query = rotary(query_pre, position, query_dims).astype(jnp.bfloat16)
    key = rotary(key_pre, position, key_dims).astype(jnp.bfloat16)
    value = value_pre.astype(jnp.bfloat16)
    heads = query.shape[1] // HD
    groups = key.shape[1] // HD
    attended = attend(query, key, value, request, stretches, heads, groups)
    own_start = device * query_cols % (heads * HD)
    own_columns = lax.dynamic_slice_in_dim(attended, own_start, query_cols, 1)
    projected = contract(lax.all_gather(own_columns, "tp", axis=1, tiled=True), output_full)
    return (hidden_in.astype(jnp.float32) + projected).astype(jnp.bfloat16)


RING = 8
ROWS = STRETCH // 2
UNIT = 1024
CHUNK = 256
ORDER = (0, 1, -1, -2, 2, 3, -3, -4)


def ring_place(t):
    return t // 2 if t % 2 == 0 else RING - 1 - t // 2


def ring_member(place):
    return 2 * place if place < RING // 2 else 2 * RING - 1 - 2 * place


def ring_swap(later):
    pairs = []
    for t in range(RING):
        for p in range(2):
            place = ring_place(t)
            step = 1 if (place + p + later) % 2 == 0 else -1
            pairs.append((t * 2 + p, ring_member((place + step) % RING) * 2 + p))
    return pairs


def swapped(shard, later):
    return lax.ppermute(shard, ("tp", "pair"), ring_swap(later))


def unit_of(index):
    t = lax.axis_index("tp")
    place = jnp.where(t % 2 == 0, t // 2, RING - 1 - t // 2)
    step = 1 - 2 * ((place + lax.axis_index("pair")) % 2)
    offset = jnp.int32(ORDER[0])
    for k in range(1, len(ORDER)):
        offset = jnp.where(index == k, ORDER[k], offset)
    where = (place + offset * step + RING) % RING
    return jnp.where(where < RING // 2, 2 * where, 2 * RING - 1 - 2 * where)


def columns_of(index):
    t = unit_of(index)
    mine = t // (RING // 2) == lax.axis_index("pair")
    return mine, pl.ds(pl.multiple_of(t % (RING // 2) * UNIT, UNIT), UNIT)


def copy_either(own, other, rows, index, target, sem):
    mine, cols = columns_of(index)

    @pl.when(mine)
    def _():
        pltpu.make_async_copy(own.at[rows, cols], target, sem).start()

    @pl.when(jnp.logical_not(mine))
    def _():
        pltpu.make_async_copy(other.at[rows, cols], target, sem).start()


def start_block(weights, h, index, target, sem):
    first = 0
    for own, other in weights:
        blocks = own.shape[0] // HALF

        @pl.when((h >= first) & (h < first + blocks))
        def _():
            rows = pl.ds(pl.multiple_of((h - first) * HALF, HALF), HALF)
            copy_either(own, other, rows, index, target, sem)

        first += blocks


def start_chunk(weights, chunk, slot, buf, sems, first, count):
    for part in range(CHUNK // HALF):
        for u in range(count):
            target = buf.at[slot, pl.ds(part * HALF, HALF), pl.ds(u * UNIT, UNIT)]
            start_block(weights, chunk * (CHUNK // HALF) + part, first + u, target, sems.at[slot, part, u])


def wait_chunk(weights, slot, buf, sems, count):
    for part in range(CHUNK // HALF):
        for u in range(count):
            target = buf.at[slot, pl.ds(part * HALF, HALF), pl.ds(u * UNIT, UNIT)]
            source = weights[0][0].at[pl.ds(0, HALF), pl.ds(0, UNIT)]
            pltpu.make_async_copy(source, target, sems.at[slot, part, u]).wait()


def contract_units(xs, acc, weights, buf, sems, first, count, acc_in=None):
    chunks = acc.shape[0]

    def chunk_step(n, carry):
        slot = n % 2

        @pl.when(n + 1 < chunks)
        def _():
            start_chunk(weights, n + 1, (n + 1) % 2, buf, sems, first, count)

        wait_chunk(weights, slot, buf, sems, count)
        product = contract(xs[...], buf[slot])
        acc[n] = product if acc_in is None else acc_in[n] + product
        return carry

    lax.fori_loop(0, chunks, chunk_step, 0)


def prefetch(weights, target, sems, first, count, go):
    for u in range(count):
        at = 0
        for n, (own, other) in enumerate(weights):
            rows = own.shape[0]
            where = target.at[pl.ds(at, rows), pl.ds(u * UNIT, UNIT)]
            if go:
                copy_either(own, other, pl.ds(0, rows), first + u, where, sems.at[n, u])
            else:
                source = own.at[:, pl.ds(0, UNIT)]
                pltpu.make_async_copy(source, where, sems.at[n, u]).wait()
            at += rows


def normed_unit(part, factor, gain_ref, index):
    base = unit_of(index) * (UNIT // 128)
    stream = part.astype(jnp.float32)
    lanes = []
    for k in range(UNIT // 128):
        gain = gain_ref[pl.ds(base + k, 1), :]
        lanes.append((stream[:, k * 128 : (k + 1) * 128] * factor * gain).astype(jnp.bfloat16))
    return lanes


def place_unit(xs, rows, n, part, factor, gain, index):
    for k, lane in enumerate(normed_unit(part, factor, gain, index)):
        at = n * UNIT + k * 128
        xs[rows, at : at + 128] = lane


HALF = 128
VM = pl.BlockSpec(memory_space=pltpu.VMEM)
HBM = pl.BlockSpec(memory_space=pltpu.HBM)
SM = pl.BlockSpec(memory_space=pltpu.SMEM)


def params(mib):
    return pltpu.CompilerParams(vmem_limit_bytes=mib * 2**20)


def cost(rows, units, width):
    return pl.CostEstimate(
        flops=2 * rows * units * UNIT * width,
        bytes_accessed=2 * units * UNIT * width + 4 * rows * width,
        transcendentals=0,
    )


def paired(refs):
    return tuple((refs[n], refs[n + 1]) for n in range(0, len(refs), 2))


def chunk_scratch(count):
    return [
        pltpu.VMEM((STRETCH, count * UNIT), jnp.bfloat16),
        pltpu.VMEM((2, CHUNK, count * UNIT), jnp.bfloat16),
        pltpu.SemaphoreType.DMA((2, CHUNK // HALF, count)),
    ]


def stream_rows(s):
    return slice(s * ROWS, (s + 1) * ROWS)


def early_kernel(a0, b0, a1, b1, a2, b2, gain, factor, *refs):
    *weights, acc, xs, buf, sems = refs
    weights = paired(weights)
    start_chunk(weights, 0, 0, buf, sems, 0, 4)
    for s, (own, first, second) in enumerate(((a0, a1, a2), (b0, b1, b2))):
        rows = stream_rows(s)
        scale = factor[rows, :]
        place_unit(xs, rows, 0, own[...], scale, gain, 0)
        place_unit(xs, rows, 1, first[...], scale, gain, 1)
        place_unit(xs, rows, 2, second[:ROWS, :], scale, gain, 2)
        place_unit(xs, rows, 3, second[ROWS:, :], scale, gain, 3)
    contract_units(xs, acc, weights, buf, sems, 0, 4)


def middle_kernel(a3, b3, gain, factor, acc_in, *refs):
    *weights, acc, late, xs, buf, sems, late_sems = refs
    weights = paired(weights)
    start_chunk(weights, 0, 0, buf, sems, 4, 2)
    for s, ref in enumerate((a3, b3)):
        for n in range(2):
            part = ref[n * ROWS : (n + 1) * ROWS, :]
            place_unit(xs, stream_rows(s), n, part, factor[stream_rows(s), :], gain, 4 + n)
    prefetch(weights, late, late_sems, 6, 2, True)
    contract_units(xs, acc, weights, buf, sems, 4, 2, acc_in)
    prefetch(weights, late, late_sems, 6, 2, False)


def turned_heads(part, cosine, sine):
    lane = lax.broadcasted_iota(jnp.int32, part.shape, 1)
    other = jnp.where(lane % 2 == 0, pltpu.roll(part, HD - 1, 1), pltpu.roll(part, 1, 1))
    return (part * cosine + other * sine).astype(jnp.bfloat16)


def last_kernel(half, lens, new, gain, factor, acc_in, late, cosine, sine, *refs):
    if half:
        key_early, value_early = refs[:2]
        refs = refs[2:]
    attended, key_out, value_out, xs = refs
    rows = stream_rows(half)
    for n in range(2):
        part = new[n * ROWS : (n + 1) * ROWS, :]
        place_unit(xs, slice(0, ROWS), n, part, factor[rows, :], gain, 6 + n)
    chunks = acc_in.shape[0]

    def projected(n):
        product = contract(xs[...], late[n * CHUNK : (n + 1) * CHUNK, :])
        return acc_in[n, rows, :] + product

    cos, sin = cosine[rows, :], sine[rows, :]
    both = projected(chunks - 1)
    key = turned_heads(both[:, :HD], cos, sin)
    value = both[:, HD:].astype(jnp.bfloat16)
    key_out[...] = key
    value_out[...] = value
    if half:
        key = jnp.concatenate([key_early[...], key], axis=0)
        value = jnp.concatenate([value_early[...], value], axis=0)
    shape = (ROWS, (half + 1) * ROWS)
    row = lax.broadcasted_iota(jnp.int32, shape, 0) + half * ROWS
    col = lax.broadcasted_iota(jnp.int32, shape, 1)
    row_request = jnp.zeros(shape, jnp.int32)
    col_request = jnp.zeros(shape, jnp.int32)
    end = jnp.int32(0)
    for k in range(lens.shape[1]):
        end = end + lens[0, k]
        row_request += (row >= end).astype(jnp.int32)
        col_request += (col >= end).astype(jnp.int32)
    keep = (row_request == col_request) & (row >= col)
    for n in range(chunks - 1):
        both = projected(n)
        for lane in range(0, CHUNK, HD):
            query = turned_heads(both[:, lane : lane + HD], cos, sin)
            scores = contract(query, key) * (1.0 / math.sqrt(HD))
            scores = jnp.where(keep, scores, -1e30)
            weights = jnp.exp(scores - jnp.max(scores, axis=1, keepdims=True))
            probs = (weights / jnp.sum(weights, axis=1, keepdims=True)).astype(jnp.bfloat16)
            out = jnp.dot(probs, value, preferred_element_type=jnp.float32)
            at = n * CHUNK + lane
            attended[:, at : at + HD] = out.astype(jnp.bfloat16)


def out_early_kernel(a0, b0, a1, b1, a2, b2, w0, w1, acc, xs, buf, sems):
    weights = ((w0, w1),)
    start_chunk(weights, 0, 0, buf, sems, 0, 4)
    for s, (own, first, second) in enumerate(((a0, a1, a2), (b0, b1, b2))):
        rows = stream_rows(s)
        xs[rows, 0:UNIT] = own[...]
        xs[rows, UNIT : 2 * UNIT] = first[...]
        xs[rows, 2 * UNIT : 3 * UNIT] = second[:ROWS, :]
        xs[rows, 3 * UNIT :] = second[ROWS:, :]
    contract_units(xs, acc, weights, buf, sems, 0, 4)


def out_middle_kernel(a3, b3, acc_in, w0, w1, acc, late, xs, buf, sems, late_sems):
    weights = ((w0, w1),)
    start_chunk(weights, 0, 0, buf, sems, 4, 2)
    for s, ref in enumerate((a3, b3)):
        xs[stream_rows(s), :UNIT] = ref[:ROWS, :]
        xs[stream_rows(s), UNIT:] = ref[ROWS:, :]
    prefetch(weights, late, late_sems, 6, 2, True)
    contract_units(xs, acc, weights, buf, sems, 4, 2, acc_in)
    prefetch(weights, late, late_sems, 6, 2, False)


def out_last_kernel(half, new, hidden, acc_in, late, *refs):
    out = refs[-1]
    rows = stream_rows(half)
    for n in range(acc_in.shape[0]):
        cols = slice(n * CHUNK, (n + 1) * CHUNK)
        total = acc_in[n, rows, :]
        for u in range(2):
            part = new[u * ROWS : (u + 1) * ROWS, :]
            total = total + contract(part, late[cols, u * UNIT : (u + 1) * UNIT])
        out[:, cols] = (hidden[:, cols].astype(jnp.float32) + total).astype(jnp.bfloat16)


def summed_over_tp(value):
    for bit in (2, 1, 4):
        pairs = [(t * 2 + p, (t ^ bit) * 2 + p) for t in range(RING) for p in range(2)]
        value = value + lax.ppermute(value, ("tp", "pair"), pairs)
    return value


def in_hbm(value):
    return pltpu.with_memory_space_constraint(value, pltpu.HBM)


def after(value, *others):
    return lax.optimization_barrier((value, *others))


def ring_body(hidden_in, norm_gain, query_weight, key_weight, value_weight, output_weight, lengths):
    f32, bf16 = jnp.float32, jnp.bfloat16
    a0, b0 = hidden_in[:ROWS], hidden_in[ROWS:]
    a1, b1 = swapped(a0, 0), swapped(b0, 0)
    weights = []
    for w in (key_weight, value_weight, query_weight):
        weights = [in_hbm(w), in_hbm(partner(w, "pair", 0))] + weights
    weights = weights[:2] + weights[4:] + weights[2:4]
    qkv = sum(w.shape[0] for w in weights[::2])
    stream = hidden_in.astype(f32)
    squares = jnp.sum(stream * stream, axis=1).reshape(2, 128)
    factor = lax.rsqrt(summed_over_tp(squares) / (RING * UNIT) + 1e-05)
    factor = jnp.broadcast_to(factor.reshape(STRETCH, 1), (STRETCH, 128))
    a2 = swapped(jnp.concatenate([a0, a1], axis=0), 1)
    b2 = swapped(jnp.concatenate([b0, b1], axis=0), 1)
    gain = norm_gain.reshape(RING * UNIT // 128, 128)
    _, position = token_layout(lengths)
    lane = jnp.arange(HD, dtype=jnp.int32)
    angle = position.reshape(-1).astype(f32)[:, None] * scaled_freq(lane - lane % 2)[None, :]
    cosine = jnp.cos(angle)
    sine = jnp.sin(angle) * jnp.where(lane % 2 == 0, -1.0, 1.0)[None, :]
    a3, b3 = swapped(a2, 0), swapped(b2, 0)

    chunks = qkv // CHUNK
    acc_shape = jax.ShapeDtypeStruct((chunks, STRETCH, CHUNK), f32)
    acc = pl.pallas_call(
        early_kernel,
        out_shape=acc_shape,
        in_specs=[VM] * 8 + [HBM] * 6,
        out_specs=VM,
        scratch_shapes=chunk_scratch(4),
        compiler_params=params(16),
        cost_estimate=cost(STRETCH, 4, qkv),
        name="early",
    )(a0, b0, a1, b1, a2, b2, gain, factor, *weights)
    a3, acc = after(a3, acc)
    a4, b4 = swapped(a3, 1), swapped(b3, 1)
    acc, late = pl.pallas_call(
        middle_kernel,
        out_shape=(acc_shape, jax.ShapeDtypeStruct((qkv, 2 * UNIT), bf16)),
        in_specs=[VM] * 5 + [HBM] * 6,
        out_specs=(VM, VM),
        scratch_shapes=chunk_scratch(2) + [pltpu.SemaphoreType.DMA((3, 2))],
        compiler_params=params(20),
        cost_estimate=cost(STRETCH, 2, qkv),
        name="middle",
    )(a3, b3, gain, factor, acc, *weights)

    def last(half, new, early):
        kv = jax.ShapeDtypeStruct((ROWS, HD), bf16)
        return pl.pallas_call(
            lambda *refs: last_kernel(half, *refs),
            out_shape=(jax.ShapeDtypeStruct((ROWS, UNIT), bf16), kv, kv),
            in_specs=[SM] + [VM] * (7 + len(early)),
            out_specs=(VM, VM, VM),
            scratch_shapes=[pltpu.VMEM((ROWS, 2 * UNIT), bf16)],
            compiler_params=params(16),
            cost_estimate=cost(ROWS, 4, qkv),
            name=f"last{half}",
        )(lengths, new, gain, factor, acc, late, cosine, sine, *early)

    a0, key_a, value_a = last(0, a4, ())
    b0, _, _ = last(1, b4, (key_a, value_a))

    other_output = in_hbm(partner(output_weight, "pair", 0))
    output_weight = in_hbm(output_weight)
    a1, b1 = swapped(a0, 0), swapped(b0, 0)
    a2 = swapped(jnp.concatenate([a0, a1], axis=0), 1)
    b2 = swapped(jnp.concatenate([b0, b1], axis=0), 1)
    a3, b3 = swapped(a2, 0), swapped(b2, 0)
    width = output_weight.shape[0]
    acc_shape = jax.ShapeDtypeStruct((width // CHUNK, STRETCH, CHUNK), f32)
    acc = pl.pallas_call(
        out_early_kernel,
        out_shape=acc_shape,
        in_specs=[VM] * 6 + [HBM] * 2,
        out_specs=VM,
        scratch_shapes=chunk_scratch(4),
        compiler_params=params(16),
        cost_estimate=cost(STRETCH, 4, width),
        name="out_early",
    )(a0, b0, a1, b1, a2, b2, output_weight, other_output)
    a3, acc = after(a3, acc)
    a4, b4 = swapped(a3, 1), swapped(b3, 1)
    acc, late = pl.pallas_call(
        out_middle_kernel,
        out_shape=(acc_shape, jax.ShapeDtypeStruct((width, 2 * UNIT), bf16)),
        in_specs=[VM] * 3 + [HBM] * 2,
        out_specs=(VM, VM),
        scratch_shapes=chunk_scratch(2) + [pltpu.SemaphoreType.DMA((1, 2))],
        compiler_params=params(20),
        cost_estimate=cost(STRETCH, 2, width),
        name="out_middle",
    )(a3, b3, acc, output_weight, other_output)

    def out_last(half, new, *partial):
        part = pl.BlockSpec((ROWS, UNIT), lambda i: (half, 0))
        return pl.pallas_call(
            lambda *refs: out_last_kernel(half, *refs),
            grid=(1,),
            out_shape=jax.ShapeDtypeStruct((STRETCH, UNIT), bf16),
            in_specs=[VM, part, VM, VM] + [HBM] * half,
            out_specs=part,
            input_output_aliases={4: 0} if half else {},
            compiler_params=params(16),
            cost_estimate=cost(ROWS, 4, width),
            name=f"out_last{half}",
        )(new, hidden_in, acc, late, *partial)

    return out_last(1, b4, out_last(0, a4))


def fits_ring(mesh):
    return dict(mesh.shape)["tp"] == RING and dict(mesh.shape)["pair"] == 2


def solution(mesh):
    placed = (
        P(("group", "pair"), "tp"),
        P(),
        P("tp", "pair"),
        P("tp", "pair"),
        P("tp", "pair"),
        P("tp", "pair"),
        P(("group", "pair"), None),
    )
    body = ring_body if fits_ring(mesh) else general_body
    return jax.shard_map(
        body, mesh=mesh, in_specs=placed, out_specs=P(("group", "pair"), "tp"), check_vma=False
    )
```

```python
import math

import jax
import jax.numpy as jnp
from jax import lax
from jax.experimental import pallas as pl
from jax.experimental.pallas import tpu as pltpu

from jax.sharding import PartitionSpec as P

HQ = 64
KVH = 8
HD = 128
STRETCH = 256


THETA = 500000.0


def shortened(shard):

    def short(part):
        return part.astype(jnp.bfloat16) if part.dtype == jnp.float32 else part

    return jax.tree.map(short, shard)


def partner(shard, axis, apart):
    return lax.ppermute(shard, axis, [(i, i ^ 1 << apart) for i in range(lax.axis_size(axis))])


def token_layout(lengths):
    ends = jnp.cumsum(lengths, axis=1)
    offsets = jnp.arange(STRETCH, dtype=jnp.int32)
    finished = ends[:, None, :] <= offsets[None, :, None]
    request = jnp.sum(finished.astype(jnp.int32), axis=2)
    position = offsets[None, :] - jnp.sum(jnp.where(finished, lengths[:, None, :], 0), axis=2)
    return (request, position)


def scaled_freq(dims):
    freq = jnp.exp(dims.astype(jnp.float32) * (-math.log(THETA) / HD))
    wavelen = 2.0 * math.pi / freq
    smooth = (8192.0 / wavelen - 1.0) / 3.0
    middle = (1.0 - smooth) * freq / 8.0 + smooth * freq
    return jnp.where(wavelen < 2048.0, freq, jnp.where(wavelen > 8192.0, freq / 8.0, middle))


def rotary(projected, position, dims):
    freq = scaled_freq(dims[0::2])
    angle = position.astype(jnp.float32)[:, None] * freq[None, :]
    cosine = jnp.cos(angle)
    sine = jnp.sin(angle)
    first = projected[:, 0::2]
    second = projected[:, 1::2]
    turned = jnp.stack([first * cosine - second * sine, first * sine + second * cosine], axis=-1)
    return turned.reshape(projected.shape)


def attend(query, key, value, request, stretches, heads, groups):
    repeat = heads // groups
    query_blocks = query.reshape(stretches, STRETCH, groups, repeat, HD)
    key_blocks = key.reshape(stretches, STRETCH, groups, HD)
    value_blocks = value.reshape(stretches, STRETCH, groups, HD)
    scores = jnp.einsum(
        "cqgrd,ckgd->cgrqk", query_blocks, key_blocks, preferred_element_type=jnp.float32
    ) * (1.0 / math.sqrt(HD))
    offsets = jnp.arange(STRETCH, dtype=jnp.int32)
    keep = (request[:, :, None] == request[:, None, :]) & (offsets[:, None] >= offsets[None, :])[
        None
    ]
    scores = jnp.where(keep[:, None, None], scores, -1e30)
    top = jnp.max(scores, axis=-1, keepdims=True)
    weights = jnp.exp(scores - top)
    probs = (weights / jnp.sum(weights, axis=-1, keepdims=True)).astype(jnp.bfloat16)
    attended = jnp.einsum(
        "cgrqk,ckgd->cqgrd", probs, value_blocks, preferred_element_type=jnp.float32
    )
    return attended.reshape(stretches * STRETCH, heads * HD).astype(jnp.bfloat16)


def contract(left, right):
    return lax.dot_general(
        left, right, (((1,), (1,)), ((), ())), preferred_element_type=jnp.float32
    )


def bit_count(number):
    return number.bit_length() - 1


def assemble(parts, needed_bits, device, axis):
    for bit_index in range(max(needed_bits)):
        moving = [piece for piece, needed in zip(parts, needed_bits) if bit_index < needed]
        widths = [piece.shape[axis] for piece in moving]
        sent = jnp.concatenate(moving, axis=axis)
        arrived = partner(shortened(sent), "tp", bit_index).astype(sent.dtype)
        upper = device // 2**bit_index % 2 == 1
        cuts = []
        running = 0
        for width in widths[:-1]:
            running = running + width
            cuts.append(running)
        received = jnp.split(arrived, cuts, axis=axis)
        joined = []
        counter = 0
        for piece, needed in zip(parts, needed_bits):
            if bit_index < needed:
                other = received[counter]
                counter = counter + 1
                piece = jnp.where(
                    upper,
                    jnp.concatenate([other, piece], axis=axis),
                    jnp.concatenate([piece, other], axis=axis),
                )
            joined.append(piece)
        parts = joined
    return parts


def project(normed, query_rows, key_rows, value_rows, output_rows):
    query_full, key_full, value_full, output_full = (
        lax.all_gather(query_rows, "pair", axis=1, tiled=True),
        lax.all_gather(key_rows, "pair", axis=1, tiled=True),
        lax.all_gather(value_rows, "pair", axis=1, tiled=True),
        lax.all_gather(output_rows, "pair", axis=1, tiled=True),
    )
    query_pre = contract(normed, query_full)
    key_pre = contract(normed, key_full)
    value_pre = contract(normed, value_full)
    return (query_pre, key_pre, value_pre, output_full)


def general_body(hidden_in, norm_gain, query_weight, key_weight, value_weight, output_weight, lengths):
    tp_count = lax.axis_size("tp")
    device = lax.axis_index("tp")
    query_bits = bit_count(max(1, tp_count // HQ))
    group_bits = bit_count(max(1, tp_count // KVH))
    needed_bits = [query_bits, group_bits, group_bits]
    query_cols = query_weight.shape[0]
    stretches = lengths.shape[0]
    request, position = token_layout(lengths)
    position = position.reshape(-1)
    full_rows = lax.all_gather(hidden_in, "tp", axis=1, tiled=True)
    stream = full_rows.astype(jnp.float32)
    mean_square = jnp.mean(stream * stream, axis=1, keepdims=True)
    normed = (stream * lax.rsqrt(mean_square + 1e-05) * norm_gain[None, :]).astype(jnp.bfloat16)
    query_block, key_block, value_block = assemble(
        [query_weight, key_weight, value_weight], needed_bits, device, 0
    )
    query_pre, key_pre, value_pre, output_full = project(
        normed, query_block, key_block, value_block, output_weight
    )
    query_dims = jnp.arange(query_pre.shape[1], dtype=jnp.int32) % HD
    key_dims = jnp.arange(key_pre.shape[1], dtype=jnp.int32) % HD
    query = rotary(query_pre, position, query_dims).astype(jnp.bfloat16)
    key = rotary(key_pre, position, key_dims).astype(jnp.bfloat16)
    value = value_pre.astype(jnp.bfloat16)
    heads = query.shape[1] // HD
    groups = key.shape[1] // HD
    attended = attend(query, key, value, request, stretches, heads, groups)
    own_start = device * query_cols % (heads * HD)
    own_columns = lax.dynamic_slice_in_dim(attended, own_start, query_cols, 1)
    projected = contract(lax.all_gather(own_columns, "tp", axis=1, tiled=True), output_full)
    return (hidden_in.astype(jnp.float32) + projected).astype(jnp.bfloat16)


RING = 8
ROWS = STRETCH // 2
UNIT = 1024
ORDER = (0, 1, -1, -2, 2, 3, -3, -4)


def ring_place(t):
    return t // 2 if t % 2 == 0 else RING - 1 - t // 2


def ring_member(place):
    return 2 * place if place < RING // 2 else 2 * RING - 1 - 2 * place


def ring_swap(later):
    pairs = []
    for t in range(RING):
        for p in range(2):
            place = ring_place(t)
            step = 1 if (place + p + later) % 2 == 0 else -1
            pairs.append((t * 2 + p, ring_member((place + step) % RING) * 2 + p))
    return pairs


def swapped(shard, later):
    return lax.ppermute(shard, ("tp", "pair"), ring_swap(later))


def unit_of(index):
    t = lax.axis_index("tp")
    place = jnp.where(t % 2 == 0, t // 2, RING - 1 - t // 2)
    step = 1 - 2 * ((place + lax.axis_index("pair")) % 2)
    offset = jnp.int32(ORDER[0])
    for k in range(1, len(ORDER)):
        offset = jnp.where(index == k, ORDER[k], offset)
    where = (place + offset * step + RING) % RING
    return jnp.where(where < RING // 2, 2 * where, 2 * RING - 1 - 2 * where)


def columns_of(index):
    t = unit_of(index)
    mine = t // (RING // 2) == lax.axis_index("pair")
    return mine, pl.ds(pl.multiple_of(t % (RING // 2) * UNIT, UNIT), UNIT)


def copy_either(own, other, rows, index, target, sem):
    mine, cols = columns_of(index)

    @pl.when(mine)
    def _():
        pltpu.make_async_copy(own.at[rows, cols], target, sem).start()

    @pl.when(jnp.logical_not(mine))
    def _():
        pltpu.make_async_copy(other.at[rows, cols], target, sem).start()


def contract_units(xs, acc, weights, buf, sems, count):
    for u in range(count):
        prefetch(weights, buf, sems, 0, u, False)
        columns = slice(u * UNIT, (u + 1) * UNIT)
        product = contract(xs[:, columns], buf[:, columns])
        acc[...] = product if u == 0 else acc[...] + product


def prefetch(weights, target, sems, first, u, go):
    at = 0
    for n, (own, other) in enumerate(weights):
        rows = own.shape[0]
        where = target.at[pl.ds(at, rows), pl.ds(u * UNIT, UNIT)]
        if go:
            copy_either(own, other, pl.ds(0, rows), first + u, where, sems.at[n, u])
        else:
            source = own.at[:, pl.ds(0, UNIT)]
            pltpu.make_async_copy(source, where, sems.at[n, u]).wait()
        at += rows


def normed_unit(part, factor, gain_ref, index):
    base = unit_of(index) * (UNIT // 128)
    stream = part.astype(jnp.float32)
    lanes = []
    for k in range(UNIT // 128):
        gain = gain_ref[pl.ds(base + k, 1), :]
        lanes.append((stream[:, k * 128 : (k + 1) * 128] * factor * gain).astype(jnp.bfloat16))
    return lanes


def place_unit(xs, rows, n, part, factor, gain, index):
    for k, lane in enumerate(normed_unit(part, factor, gain, index)):
        at = n * UNIT + k * 128
        xs[rows, at : at + 128] = lane


VM = pl.BlockSpec(memory_space=pltpu.VMEM)
HBM = pl.BlockSpec(memory_space=pl.ANY)
SM = pl.BlockSpec(memory_space=pltpu.SMEM)


def params(mib):
    return pltpu.CompilerParams(vmem_limit_bytes=mib * 2**20)


def cost(rows, units, width):
    return pl.CostEstimate(
        flops=2 * rows * units * UNIT * width,
        bytes_accessed=2 * units * UNIT * width + 4 * rows * width,
        transcendentals=0,
    )


def paired(refs):
    return tuple((refs[n], refs[n + 1]) for n in range(0, len(refs), 2))


def unit_scratch(count, width, kinds):
    return [
        pltpu.VMEM((STRETCH, count * UNIT), jnp.bfloat16),
        pltpu.VMEM((width, count * UNIT), jnp.bfloat16),
        pltpu.SemaphoreType.DMA((kinds, count)),
        pltpu.SemaphoreType.DMA((kinds, count)),
    ]


def stream_rows(s):
    return slice(s * ROWS, (s + 1) * ROWS)


def early_kernel(a0, b0, a1, b1, a2, b2, gain, factor, *refs):
    *weights, acc, late, xs, buf, sems, late_sems = refs
    weights = paired(weights)
    for u in range(4):
        prefetch(weights, buf, sems, 0, u, True)
    for u in range(4):
        prefetch(weights, late, late_sems, 4, u, True)
    for s, (own, first, second) in enumerate(((a0, a1, a2), (b0, b1, b2))):
        rows = stream_rows(s)
        scale = factor[rows, :]
        place_unit(xs, rows, 0, own[...], scale, gain, 0)
        place_unit(xs, rows, 1, first[...], scale, gain, 1)
        place_unit(xs, rows, 2, second[:ROWS, :], scale, gain, 2)
        place_unit(xs, rows, 3, second[ROWS:, :], scale, gain, 3)
    contract_units(xs, acc, weights, buf, sems, 4)
    for u in range(4):
        prefetch(weights, late, late_sems, 4, u, False)


def middle_kernel(a3, b3, gain, factor, acc_in, late, acc, xs):
    for s, ref in enumerate((a3, b3)):
        for n in range(2):
            part = ref[n * ROWS : (n + 1) * ROWS, :]
            place_unit(xs, stream_rows(s), n, part, factor[stream_rows(s), :], gain, 4 + n)
    acc[...] = acc_in[...] + contract(xs[...], late[:, : 2 * UNIT])


def turned_heads(part, cosine, sine):
    lane = lax.broadcasted_iota(jnp.int32, part.shape, 1)
    other = jnp.where(lane % 2 == 0, pltpu.roll(part, HD - 1, 1), pltpu.roll(part, 1, 1))
    return (part * cosine + other * sine).astype(jnp.bfloat16)


def last_kernel(half, lens, new, gain, factor, acc_in, late, cosine, sine, *refs):
    if half:
        key_early, value_early = refs[:2]
        refs = refs[2:]
    attended, key_out, value_out, xs, acc = refs
    rows = stream_rows(half)
    for n in range(2):
        part = new[n * ROWS : (n + 1) * ROWS, :]
        place_unit(xs, slice(0, ROWS), n, part, factor[rows, :], gain, 6 + n)
    acc[...] = acc_in[rows, :] + contract(xs[...], late[:, 2 * UNIT :])
    heads = UNIT // HD
    cos, sin = cosine[rows, :], sine[rows, :]
    key = turned_heads(acc[:, UNIT : UNIT + HD], cos, sin)
    value = acc[:, UNIT + HD :].astype(jnp.bfloat16)
    key_out[...] = key
    value_out[...] = value
    if half:
        key = jnp.concatenate([key_early[...], key], axis=0)
        value = jnp.concatenate([value_early[...], value], axis=0)
    shape = (ROWS, (half + 1) * ROWS)
    row = lax.broadcasted_iota(jnp.int32, shape, 0) + half * ROWS
    col = lax.broadcasted_iota(jnp.int32, shape, 1)
    row_request = jnp.zeros(shape, jnp.int32)
    col_request = jnp.zeros(shape, jnp.int32)
    end = jnp.int32(0)
    for k in range(lens.shape[1]):
        end = end + lens[0, k]
        row_request += (row >= end).astype(jnp.int32)
        col_request += (col >= end).astype(jnp.int32)
    keep = (row_request == col_request) & (row >= col)
    queries = [turned_heads(acc[:, h * HD : (h + 1) * HD], cos, sin) for h in range(heads)]
    scores = contract(jnp.concatenate(queries, axis=0), key) * (1.0 / math.sqrt(HD))
    scores = jnp.where(keep[None], scores.reshape(heads, *shape), -1e30)
    weights = jnp.exp(scores - jnp.max(scores, axis=2, keepdims=True))
    probs = (weights / jnp.sum(weights, axis=2, keepdims=True)).astype(jnp.bfloat16)
    probs = probs.reshape(heads * ROWS, shape[1])
    out = jnp.dot(probs, value, preferred_element_type=jnp.float32).astype(jnp.bfloat16)
    for h in range(heads):
        attended[:, h * HD : (h + 1) * HD] = out[h * ROWS : (h + 1) * ROWS, :]


def out_early_kernel(a0, b0, a1, b1, a2, b2, w0, w1, acc, late, xs, buf, sems, late_sems):
    weights = ((w0, w1),)
    for u in range(4):
        prefetch(weights, buf, sems, 0, u, True)
    for u in range(4):
        prefetch(weights, late, late_sems, 4, u, True)
    for s, (own, first, second) in enumerate(((a0, a1, a2), (b0, b1, b2))):
        rows = stream_rows(s)
        xs[rows, 0:UNIT] = own[...]
        xs[rows, UNIT : 2 * UNIT] = first[...]
        xs[rows, 2 * UNIT : 3 * UNIT] = second[:ROWS, :]
        xs[rows, 3 * UNIT :] = second[ROWS:, :]
    contract_units(xs, acc, weights, buf, sems, 4)
    for u in range(4):
        prefetch(weights, late, late_sems, 4, u, False)


def out_middle_kernel(a3, b3, acc_in, late, acc, xs):
    for s, ref in enumerate((a3, b3)):
        xs[stream_rows(s), :UNIT] = ref[:ROWS, :]
        xs[stream_rows(s), UNIT:] = ref[ROWS:, :]
    acc[...] = acc_in[...] + contract(xs[...], late[:, : 2 * UNIT])


def out_last_kernel(half, new, hidden, acc_in, late, *refs):
    out = refs[-1]
    total = acc_in[stream_rows(half), :]
    for u in range(2):
        part = new[u * ROWS : (u + 1) * ROWS, :]
        total = total + contract(part, late[:, (u + 2) * UNIT : (u + 3) * UNIT])
    out[...] = (hidden[...].astype(jnp.float32) + total).astype(jnp.bfloat16)


def summed_over_tp(value):
    for bits in ((1, 2), (2, 1), (4, 4)):
        pairs = [(t * 2 + p, (t ^ bits[p]) * 2 + p) for t in range(RING) for p in range(2)]
        value = value + lax.ppermute(value, ("tp", "pair"), pairs)
    return value


def kernel_call(kernel, **options):
    return pl.pallas_call(kernel, **options)


def in_hbm(value):
    return pltpu.with_memory_space_constraint(value, pltpu.HBM)


def in_vmem(value):
    return pltpu.with_memory_space_constraint(value, pltpu.VMEM)


def after(value, *others):
    return lax.optimization_barrier((value, *others))


def ring_body(*args):
    return ring_layer(*args)


def ring_layer(hidden_in, norm_gain, query_weight, key_weight, value_weight, output_weight, lengths):
    f32, bf16 = jnp.float32, jnp.bfloat16
    a0, b0 = hidden_in[:ROWS], hidden_in[ROWS:]
    a1, b1 = swapped(a0, 0), swapped(b0, 0)
    weights = []
    for w in (key_weight, value_weight, query_weight):
        weights = [in_hbm(w), in_vmem(partner(w, "pair", 0))] + weights
    weights = weights[:2] + weights[4:] + weights[2:4]
    qkv = sum(w.shape[0] for w in weights[::2])
    stream = hidden_in.astype(f32)
    squares = jnp.sum(stream * stream, axis=1).reshape(2, 128)
    factor = lax.rsqrt(summed_over_tp(squares) / (RING * UNIT) + 1e-05)
    factor = jnp.broadcast_to(factor.reshape(STRETCH, 1), (STRETCH, 128))
    a2 = swapped(jnp.concatenate([a0, a1], axis=0), 1)
    b2 = swapped(jnp.concatenate([b0, b1], axis=0), 1)
    gain = norm_gain.reshape(RING * UNIT // 128, 128)
    _, position = token_layout(lengths)
    lane = jnp.arange(HD, dtype=jnp.int32)
    angle = position.reshape(-1).astype(f32)[:, None] * scaled_freq(lane - lane % 2)[None, :]
    cosine = jnp.cos(angle)
    sine = jnp.sin(angle) * jnp.where(lane % 2 == 0, -1.0, 1.0)[None, :]
    a3, b3 = swapped(a2, 0), swapped(b2, 0)

    factor, cosine, sine, lengths = after(factor, cosine, sine, lengths)
    acc_shape = jax.ShapeDtypeStruct((STRETCH, qkv), f32)
    acc, late = kernel_call(
        early_kernel,
        out_shape=(acc_shape, jax.ShapeDtypeStruct((qkv, 4 * UNIT), bf16)),
        in_specs=[VM] * 8 + [HBM, VM] * 3,
        out_specs=(VM, VM),
        scratch_shapes=unit_scratch(4, qkv, 3),
        compiler_params=params(24),
        cost_estimate=cost(STRETCH, 4, qkv),
    )(a0, b0, a1, b1, a2, b2, gain, factor, *weights)
    a3, acc = after(a3, acc)
    a4, b4 = swapped(a3, 1), swapped(b3, 1)
    acc = kernel_call(
        middle_kernel,
        out_shape=acc_shape,
        in_specs=[VM] * 6,
        out_specs=VM,
        scratch_shapes=[pltpu.VMEM((STRETCH, 2 * UNIT), bf16)],
        compiler_params=params(16),
        cost_estimate=cost(STRETCH, 2, qkv),
    )(a3, b3, gain, factor, acc, late)

    def last(half, new, early):
        kv = jax.ShapeDtypeStruct((ROWS, HD), bf16)
        return kernel_call(
            lambda *refs: last_kernel(half, *refs),
            out_shape=(jax.ShapeDtypeStruct((ROWS, UNIT), bf16), kv, kv),
            in_specs=[SM] + [VM] * (7 + len(early)),
            out_specs=(VM, VM, VM),
            scratch_shapes=[pltpu.VMEM((ROWS, 2 * UNIT), bf16), pltpu.VMEM((ROWS, qkv), f32)],
            compiler_params=params(20),
            cost_estimate=cost(ROWS, 4, qkv),
        )(lengths, new, gain, factor, acc, late, cosine, sine, *early)

    a0, key_a, value_a = last(0, a4, ())
    b0, _, _ = last(1, b4, (key_a, value_a))

    other_output = in_vmem(partner(output_weight, "pair", 0))
    output_weight = in_hbm(output_weight)
    a1, b1 = swapped(a0, 0), swapped(b0, 0)
    a2 = swapped(jnp.concatenate([a0, a1], axis=0), 1)
    b2 = swapped(jnp.concatenate([b0, b1], axis=0), 1)
    a3, b3 = swapped(a2, 0), swapped(b2, 0)
    width = output_weight.shape[0]
    acc_shape = jax.ShapeDtypeStruct((STRETCH, width), f32)
    acc, late = kernel_call(
        out_early_kernel,
        out_shape=(acc_shape, jax.ShapeDtypeStruct((width, 4 * UNIT), bf16)),
        in_specs=[VM] * 6 + [HBM, VM],
        out_specs=(VM, VM),
        scratch_shapes=unit_scratch(4, width, 1),
        compiler_params=params(22),
        cost_estimate=cost(STRETCH, 4, width),
    )(a0, b0, a1, b1, a2, b2, output_weight, other_output)
    a3, acc = after(a3, acc)
    a4, b4 = swapped(a3, 1), swapped(b3, 1)
    acc = kernel_call(
        out_middle_kernel,
        out_shape=acc_shape,
        in_specs=[VM] * 4,
        out_specs=VM,
        scratch_shapes=[pltpu.VMEM((STRETCH, 2 * UNIT), bf16)],
        compiler_params=params(16),
        cost_estimate=cost(STRETCH, 2, width),
    )(a3, b3, acc, late)

    def out_last(half, new, *partial):
        part = pl.BlockSpec((ROWS, UNIT), lambda i: (half, 0))
        return kernel_call(
            lambda *refs: out_last_kernel(half, *refs),
            grid=(1,),
            out_shape=jax.ShapeDtypeStruct((STRETCH, UNIT), bf16),
            in_specs=[VM, part, VM, VM] + [HBM] * half,
            out_specs=part,
            input_output_aliases={4: 0} if half else {},
            compiler_params=params(16),
            cost_estimate=cost(ROWS, 4, width),
        )(new, hidden_in, acc, late, *partial)

    return out_last(1, b4, out_last(0, a4))


def fits_ring(mesh):
    return dict(mesh.shape)["tp"] == RING and dict(mesh.shape)["pair"] == 2


def solution(mesh):
    placed = (
        P(("group", "pair"), "tp"),
        P(),
        P("tp", "pair"),
        P("tp", "pair"),
        P("tp", "pair"),
        P("tp", "pair"),
        P(("group", "pair"), None),
    )
    body = ring_body if fits_ring(mesh) else general_body
    return jax.shard_map(
        body, mesh=mesh, in_specs=placed, out_specs=P(("group", "pair"), "tp"), check_vma=False
    )
```

```python
import math

import jax
import jax.numpy as jnp
from jax import lax
from jax.experimental import pallas as pl
from jax.experimental.pallas import tpu as pltpu

from jax.sharding import PartitionSpec as P

HQ = 64
KVH = 8
HD = 128
STRETCH = 256


THETA = 500000.0


def shortened(shard):

    def short(part):
        return part.astype(jnp.bfloat16) if part.dtype == jnp.float32 else part

    return jax.tree.map(short, shard)


def partner(shard, axis, apart):
    return lax.ppermute(shard, axis, [(i, i ^ 1 << apart) for i in range(lax.axis_size(axis))])


def token_layout(lengths):
    ends = jnp.cumsum(lengths, axis=1)
    offsets = jnp.arange(STRETCH, dtype=jnp.int32)
    finished = ends[:, None, :] <= offsets[None, :, None]
    request = jnp.sum(finished.astype(jnp.int32), axis=2)
    position = offsets[None, :] - jnp.sum(jnp.where(finished, lengths[:, None, :], 0), axis=2)
    return (request, position)


def scaled_freq(dims):
    freq = jnp.exp(dims.astype(jnp.float32) * (-math.log(THETA) / HD))
    wavelen = 2.0 * math.pi / freq
    smooth = (8192.0 / wavelen - 1.0) / 3.0
    middle = (1.0 - smooth) * freq / 8.0 + smooth * freq
    return jnp.where(wavelen < 2048.0, freq, jnp.where(wavelen > 8192.0, freq / 8.0, middle))


def rotary(projected, position, dims):
    freq = scaled_freq(dims[0::2])
    angle = position.astype(jnp.float32)[:, None] * freq[None, :]
    cosine = jnp.cos(angle)
    sine = jnp.sin(angle)
    first = projected[:, 0::2]
    second = projected[:, 1::2]
    turned = jnp.stack([first * cosine - second * sine, first * sine + second * cosine], axis=-1)
    return turned.reshape(projected.shape)


def attend(query, key, value, request, stretches, heads, groups):
    repeat = heads // groups
    query_blocks = query.reshape(stretches, STRETCH, groups, repeat, HD)
    key_blocks = key.reshape(stretches, STRETCH, groups, HD)
    value_blocks = value.reshape(stretches, STRETCH, groups, HD)
    scores = jnp.einsum(
        "cqgrd,ckgd->cgrqk", query_blocks, key_blocks, preferred_element_type=jnp.float32
    ) * (1.0 / math.sqrt(HD))
    offsets = jnp.arange(STRETCH, dtype=jnp.int32)
    keep = (request[:, :, None] == request[:, None, :]) & (offsets[:, None] >= offsets[None, :])[
        None
    ]
    scores = jnp.where(keep[:, None, None], scores, -1e30)
    top = jnp.max(scores, axis=-1, keepdims=True)
    weights = jnp.exp(scores - top)
    probs = (weights / jnp.sum(weights, axis=-1, keepdims=True)).astype(jnp.bfloat16)
    attended = jnp.einsum(
        "cgrqk,ckgd->cqgrd", probs, value_blocks, preferred_element_type=jnp.float32
    )
    return attended.reshape(stretches * STRETCH, heads * HD).astype(jnp.bfloat16)


def contract(left, right):
    return lax.dot_general(
        left, right, (((1,), (1,)), ((), ())), preferred_element_type=jnp.float32
    )


def bit_count(number):
    return number.bit_length() - 1


def assemble(parts, needed_bits, device, axis):
    for bit_index in range(max(needed_bits)):
        moving = [piece for piece, needed in zip(parts, needed_bits) if bit_index < needed]
        widths = [piece.shape[axis] for piece in moving]
        sent = jnp.concatenate(moving, axis=axis)
        arrived = partner(shortened(sent), "tp", bit_index).astype(sent.dtype)
        upper = device // 2**bit_index % 2 == 1
        cuts = []
        running = 0
        for width in widths[:-1]:
            running = running + width
            cuts.append(running)
        received = jnp.split(arrived, cuts, axis=axis)
        joined = []
        counter = 0
        for piece, needed in zip(parts, needed_bits):
            if bit_index < needed:
                other = received[counter]
                counter = counter + 1
                piece = jnp.where(
                    upper,
                    jnp.concatenate([other, piece], axis=axis),
                    jnp.concatenate([piece, other], axis=axis),
                )
            joined.append(piece)
        parts = joined
    return parts


def project(normed, query_rows, key_rows, value_rows, output_rows):
    query_full, key_full, value_full, output_full = (
        lax.all_gather(query_rows, "pair", axis=1, tiled=True),
        lax.all_gather(key_rows, "pair", axis=1, tiled=True),
        lax.all_gather(value_rows, "pair", axis=1, tiled=True),
        lax.all_gather(output_rows, "pair", axis=1, tiled=True),
    )
    query_pre = contract(normed, query_full)
    key_pre = contract(normed, key_full)
    value_pre = contract(normed, value_full)
    return (query_pre, key_pre, value_pre, output_full)


def general_body(hidden_in, norm_gain, query_weight, key_weight, value_weight, output_weight, lengths):
    tp_count = lax.axis_size("tp")
    device = lax.axis_index("tp")
    query_bits = bit_count(max(1, tp_count // HQ))
    group_bits = bit_count(max(1, tp_count // KVH))
    needed_bits = [query_bits, group_bits, group_bits]
    query_cols = query_weight.shape[0]
    stretches = lengths.shape[0]
    request, position = token_layout(lengths)
    position = position.reshape(-1)
    full_rows = lax.all_gather(hidden_in, "tp", axis=1, tiled=True)
    stream = full_rows.astype(jnp.float32)
    mean_square = jnp.mean(stream * stream, axis=1, keepdims=True)
    normed = (stream * lax.rsqrt(mean_square + 1e-05) * norm_gain[None, :]).astype(jnp.bfloat16)
    query_block, key_block, value_block = assemble(
        [query_weight, key_weight, value_weight], needed_bits, device, 0
    )
    query_pre, key_pre, value_pre, output_full = project(
        normed, query_block, key_block, value_block, output_weight
    )
    query_dims = jnp.arange(query_pre.shape[1], dtype=jnp.int32) % HD
    key_dims = jnp.arange(key_pre.shape[1], dtype=jnp.int32) % HD
    query = rotary(query_pre, position, query_dims).astype(jnp.bfloat16)
    key = rotary(key_pre, position, key_dims).astype(jnp.bfloat16)
    value = value_pre.astype(jnp.bfloat16)
    heads = query.shape[1] // HD
    groups = key.shape[1] // HD
    attended = attend(query, key, value, request, stretches, heads, groups)
    own_start = device * query_cols % (heads * HD)
    own_columns = lax.dynamic_slice_in_dim(attended, own_start, query_cols, 1)
    projected = contract(lax.all_gather(own_columns, "tp", axis=1, tiled=True), output_full)
    return (hidden_in.astype(jnp.float32) + projected).astype(jnp.bfloat16)


RING = 8
ROWS = STRETCH // 2
UNIT = 1024
ORDER = (0, 1, -1, -2, 2, 3, -3, -4)


def ring_place(t):
    return t // 2 if t % 2 == 0 else RING - 1 - t // 2


def ring_member(place):
    return 2 * place if place < RING // 2 else 2 * RING - 1 - 2 * place


def ring_swap(later):
    pairs = []
    for t in range(RING):
        for p in range(2):
            place = ring_place(t)
            step = 1 if (place + p + later) % 2 == 0 else -1
            pairs.append((t * 2 + p, ring_member((place + step) % RING) * 2 + p))
    return pairs


def swapped(shard, later):
    return lax.ppermute(shard, ("tp", "pair"), ring_swap(later))


def unit_of(index):
    t = lax.axis_index("tp")
    place = jnp.where(t % 2 == 0, t // 2, RING - 1 - t // 2)
    step = 1 - 2 * ((place + lax.axis_index("pair")) % 2)
    offset = jnp.int32(ORDER[0])
    for k in range(1, len(ORDER)):
        offset = jnp.where(index == k, ORDER[k], offset)
    where = (place + offset * step + RING) % RING
    return jnp.where(where < RING // 2, 2 * where, 2 * RING - 1 - 2 * where)


def columns_of(index):
    t = unit_of(index)
    mine = t // (RING // 2) == lax.axis_index("pair")
    return mine, pl.ds(pl.multiple_of(t % (RING // 2) * UNIT, UNIT), UNIT)


def add_units(xs, acc, own, others, first, count):
    def unit_step(u, carry):
        mine, cols = columns_of(first + u)
        for here, parts in ((mine, (own,)), (jnp.logical_not(mine), others)):

            @pl.when(here)
            def _(parts=parts):
                at = 0
                for part in parts:
                    rows = part.shape[0]
                    acc[:, at : at + rows] += contract(xs[u], part[:, cols])
                    at += rows

        return carry

    lax.fori_loop(0, count, unit_step, 0)


def load_kernel(*refs):
    *sources, target, sems = refs
    copies = []
    at = 0
    for n, source in enumerate(sources):
        rows = source.shape[0]
        copies.append(pltpu.make_async_copy(source, target.at[pl.ds(at, rows), :], sems.at[n]))
        at += rows
    for copy in copies:
        copy.start()
    for copy in copies:
        copy.wait()


def normed_unit(part, factor, gain_ref, index):
    base = unit_of(index) * (UNIT // 128)
    stream = part.astype(jnp.float32)
    lanes = []
    for k in range(UNIT // 128):
        gain = gain_ref[pl.ds(base + k, 1), :]
        lanes.append((stream[:, k * 128 : (k + 1) * 128] * factor * gain).astype(jnp.bfloat16))
    return lanes


def place_unit(xs, rows, n, part, factor, gain, index):
    for k, lane in enumerate(normed_unit(part, factor, gain, index)):
        xs[n, rows, k * 128 : (k + 1) * 128] = lane


VM = pl.BlockSpec(memory_space=pltpu.VMEM)
HBM = pl.BlockSpec(memory_space=pl.ANY)
SM = pl.BlockSpec(memory_space=pltpu.SMEM)


def params(mib):
    return pltpu.CompilerParams(vmem_limit_bytes=mib * 2**20)


def cost(rows, units, width):
    return pl.CostEstimate(
        flops=2 * rows * units * UNIT * width,
        bytes_accessed=2 * units * UNIT * width + 4 * rows * width,
        transcendentals=0,
    )


def stream_rows(s):
    return slice(s * ROWS, (s + 1) * ROWS)


def early_kernel(a0, b0, a1, b1, a2, b2, gain, factor, *refs):
    *weights, acc, xs = refs
    for s, (own, first, second) in enumerate(((a0, a1, a2), (b0, b1, b2))):
        rows = stream_rows(s)
        scale = factor[rows, :]
        place_unit(xs, rows, 0, own[...], scale, gain, 0)
        place_unit(xs, rows, 1, first[...], scale, gain, 1)
        place_unit(xs, rows, 2, second[:ROWS, :], scale, gain, 2)
        place_unit(xs, rows, 3, second[ROWS:, :], scale, gain, 3)
    acc[...] = jnp.zeros_like(acc)
    add_units(xs, acc, weights[0], weights[1:], 0, 4)


def middle_kernel(a3, b3, gain, factor, acc_in, *refs):
    *weights, acc, xs = refs
    for s, ref in enumerate((a3, b3)):
        for n in range(2):
            part = ref[n * ROWS : (n + 1) * ROWS, :]
            place_unit(xs, stream_rows(s), n, part, factor[stream_rows(s), :], gain, 4 + n)
    acc[...] = acc_in[...]
    add_units(xs, acc, weights[0], weights[1:], 4, 2)


def turned_heads(part, cosine, sine):
    lane = lax.broadcasted_iota(jnp.int32, part.shape, 1)
    other = jnp.where(lane % 2 == 0, pltpu.roll(part, HD - 1, 1), pltpu.roll(part, 1, 1))
    return (part * cosine + other * sine).astype(jnp.bfloat16)


def last_kernel(half, lens, new, gain, factor, acc_in, cosine, sine, *refs):
    if half:
        key_early, value_early = refs[:2]
        refs = refs[2:]
    *weights, attended, key_out, value_out, xs, acc = refs
    rows = stream_rows(half)
    for n in range(2):
        part = new[n * ROWS : (n + 1) * ROWS, :]
        place_unit(xs, slice(0, ROWS), n, part, factor[rows, :], gain, 6 + n)
    acc[...] = acc_in[rows, :]
    add_units(xs, acc, weights[0], weights[1:], 6, 2)
    heads = UNIT // HD
    cos, sin = cosine[rows, :], sine[rows, :]
    key = turned_heads(acc[:, UNIT : UNIT + HD], cos, sin)
    value = acc[:, UNIT + HD :].astype(jnp.bfloat16)
    key_out[...] = key
    value_out[...] = value
    if half:
        key = jnp.concatenate([key_early[...], key], axis=0)
        value = jnp.concatenate([value_early[...], value], axis=0)
    shape = (ROWS, (half + 1) * ROWS)
    row = lax.broadcasted_iota(jnp.int32, shape, 0) + half * ROWS
    col = lax.broadcasted_iota(jnp.int32, shape, 1)
    row_request = jnp.zeros(shape, jnp.int32)
    col_request = jnp.zeros(shape, jnp.int32)
    end = jnp.int32(0)
    for k in range(lens.shape[1]):
        end = end + lens[0, k]
        row_request += (row >= end).astype(jnp.int32)
        col_request += (col >= end).astype(jnp.int32)
    keep = (row_request == col_request) & (row >= col)
    queries = [turned_heads(acc[:, h * HD : (h + 1) * HD], cos, sin) for h in range(heads)]
    scores = contract(jnp.concatenate(queries, axis=0), key) * (1.0 / math.sqrt(HD))
    scores = jnp.where(keep[None], scores.reshape(heads, *shape), -1e30)
    weights = jnp.exp(scores - jnp.max(scores, axis=2, keepdims=True))
    probs = (weights / jnp.sum(weights, axis=2, keepdims=True)).astype(jnp.bfloat16)
    probs = probs.reshape(heads * ROWS, shape[1])
    out = jnp.dot(probs, value, preferred_element_type=jnp.float32).astype(jnp.bfloat16)
    for h in range(heads):
        attended[:, h * HD : (h + 1) * HD] = out[h * ROWS : (h + 1) * ROWS, :]


def out_early_kernel(a0, b0, a1, b1, a2, b2, w0, w1, acc, xs):
    for s, (own, first, second) in enumerate(((a0, a1, a2), (b0, b1, b2))):
        rows = stream_rows(s)
        xs[0, rows, :] = own[...]
        xs[1, rows, :] = first[...]
        xs[2, rows, :] = second[:ROWS, :]
        xs[3, rows, :] = second[ROWS:, :]
    acc[...] = jnp.zeros_like(acc)
    add_units(xs, acc, w0, (w1,), 0, 4)


def out_middle_kernel(a3, b3, acc_in, w0, w1, acc, xs):
    for s, ref in enumerate((a3, b3)):
        xs[0, stream_rows(s), :] = ref[:ROWS, :]
        xs[1, stream_rows(s), :] = ref[ROWS:, :]
    acc[...] = acc_in[...]
    add_units(xs, acc, w0, (w1,), 4, 2)


def out_last_kernel(half, new, hidden, acc_in, w0, w1, *refs):
    out, xs, acc = refs[-3:]
    xs[0] = new[:ROWS, :]
    xs[1] = new[ROWS:, :]
    acc[...] = acc_in[stream_rows(half), :] + hidden[...].astype(jnp.float32)
    add_units(xs, acc, w0, (w1,), 6, 2)
    out[...] = acc[...].astype(jnp.bfloat16)


def summed_over_tp(value):
    for bits in ((1, 2), (2, 1), (4, 4)):
        pairs = [(t * 2 + p, (t ^ bits[p]) * 2 + p) for t in range(RING) for p in range(2)]
        value = value + lax.ppermute(value, ("tp", "pair"), pairs)
    return value


def kernel_call(kernel, **options):
    return pl.pallas_call(kernel, **options)


def in_vmem(value):
    return pltpu.with_memory_space_constraint(value, pltpu.VMEM)


def load(arrays):
    rows = sum(w.shape[0] for w in arrays)
    return kernel_call(
        load_kernel,
        out_shape=jax.ShapeDtypeStruct((rows, arrays[0].shape[1]), arrays[0].dtype),
        in_specs=[HBM] * len(arrays),
        out_specs=VM,
        scratch_shapes=[pltpu.SemaphoreType.DMA((len(arrays),))],
        compiler_params=params(2),
        cost_estimate=cost(0, rows * arrays[0].shape[1] // UNIT, 1),
    )(*(pltpu.with_memory_space_constraint(w, pltpu.HBM) for w in arrays))


def token_position(lengths):
    count = lengths.shape[0]
    upto = jnp.arange(count)[:, None] >= jnp.arange(count)[None, :]
    ends = jnp.sum(jnp.where(upto, lengths[None, :], 0), axis=1)
    offsets = jnp.arange(STRETCH, dtype=jnp.int32)
    finished = ends[None, :] <= offsets[:, None]
    return offsets - jnp.sum(jnp.where(finished, lengths[None, :], 0), axis=1)


def after(value, *others):
    return lax.optimization_barrier((value, *others))


def ring_body(*args):
    return ring_layer(*args)


def ring_layer(hidden_in, norm_gain, query_weight, key_weight, value_weight, output_weight, lengths):
    f32, bf16 = jnp.float32, jnp.bfloat16
    a0, b0 = hidden_in[:ROWS], hidden_in[ROWS:]
    a1, b1 = swapped(a0, 0), swapped(b0, 0)
    projections = (query_weight, key_weight, value_weight)
    others = [in_vmem(partner(w, "pair", 0)) for w in projections]
    qkv = sum(w.shape[0] for w in projections)
    stream = hidden_in.astype(f32)
    squares = jnp.sum(stream * stream, axis=1).reshape(2, 128)
    squares = summed_over_tp(squares)
    factor = lax.rsqrt(squares / (RING * UNIT) + 1e-05)
    factor = jnp.broadcast_to(factor.reshape(STRETCH, 1), (STRETCH, 128))
    a2 = swapped(jnp.concatenate([a0, a1], axis=0), 1)
    b2 = swapped(jnp.concatenate([b0, b1], axis=0), 1)
    gain = norm_gain.reshape(RING * UNIT // 128, 128)
    position = token_position(lengths[0])
    lane = jnp.arange(HD, dtype=jnp.int32)
    angle = position.astype(f32)[:, None] * scaled_freq(lane - lane % 2)[None, :]
    cosine = jnp.cos(angle)
    sine = jnp.sin(angle) * jnp.where(lane % 2 == 0, -1.0, 1.0)[None, :]
    own = load(projections)
    a2, own = after(a2, own)
    weights = (own, *others)
    a3, b3 = swapped(a2, 0), swapped(b2, 0)

    factor, cosine, sine, lengths = after(factor, cosine, sine, lengths)
    acc_shape = jax.ShapeDtypeStruct((STRETCH, qkv), f32)
    acc = kernel_call(
        early_kernel,
        out_shape=acc_shape,
        in_specs=[VM] * 12,
        out_specs=VM,
        scratch_shapes=[pltpu.VMEM((4, STRETCH, UNIT), bf16)],
        compiler_params=params(12),
        cost_estimate=cost(STRETCH, 4, qkv),
    )(a0, b0, a1, b1, a2, b2, gain, factor, *weights)
    a3, acc = after(a3, acc)
    a4, b4 = swapped(a3, 1), swapped(b3, 1)
    acc = kernel_call(
        middle_kernel,
        out_shape=acc_shape,
        in_specs=[VM] * 9,
        out_specs=VM,
        scratch_shapes=[pltpu.VMEM((2, STRETCH, UNIT), bf16)],
        compiler_params=params(12),
        cost_estimate=cost(STRETCH, 2, qkv),
    )(a3, b3, gain, factor, acc, *weights)

    def last(half, new, early):
        kv = jax.ShapeDtypeStruct((ROWS, HD), bf16)
        return kernel_call(
            lambda *refs: last_kernel(half, *refs),
            out_shape=(jax.ShapeDtypeStruct((ROWS, UNIT), bf16), kv, kv),
            in_specs=[SM] + [VM] * (10 + len(early)),
            out_specs=(VM, VM, VM),
            scratch_shapes=[pltpu.VMEM((2, ROWS, UNIT), bf16), pltpu.VMEM((ROWS, qkv), f32)],
            compiler_params=params(14),
            cost_estimate=cost(ROWS, 4, qkv),
        )(lengths, new, gain, factor, acc, cosine, sine, *early, *weights)

    a0, key_a, value_a = last(0, a4, ())
    b0, _, _ = last(1, b4, (key_a, value_a))

    other_output = in_vmem(partner(output_weight, "pair", 0))
    a1, b1 = swapped(a0, 0), swapped(b0, 0)
    a2 = swapped(jnp.concatenate([a0, a1], axis=0), 1)
    b2 = swapped(jnp.concatenate([b0, b1], axis=0), 1)
    own = load((output_weight,))
    a2, own = after(a2, own)
    a3, b3 = swapped(a2, 0), swapped(b2, 0)
    width = output_weight.shape[0]
    acc_shape = jax.ShapeDtypeStruct((STRETCH, width), f32)
    acc = kernel_call(
        out_early_kernel,
        out_shape=acc_shape,
        in_specs=[VM] * 8,
        out_specs=VM,
        scratch_shapes=[pltpu.VMEM((4, STRETCH, UNIT), bf16)],
        compiler_params=params(12),
        cost_estimate=cost(STRETCH, 4, width),
    )(a0, b0, a1, b1, a2, b2, own, other_output)
    a3, acc = after(a3, acc)
    a4, b4 = swapped(a3, 1), swapped(b3, 1)
    acc = kernel_call(
        out_middle_kernel,
        out_shape=acc_shape,
        in_specs=[VM] * 5,
        out_specs=VM,
        scratch_shapes=[pltpu.VMEM((2, STRETCH, UNIT), bf16)],
        compiler_params=params(12),
        cost_estimate=cost(STRETCH, 2, width),
    )(a3, b3, acc, own, other_output)

    def out_last(half, new, *partial):
        part = pl.BlockSpec((ROWS, UNIT), lambda i: (half, 0))
        return kernel_call(
            lambda *refs: out_last_kernel(half, *refs),
            grid=(1,),
            out_shape=jax.ShapeDtypeStruct((STRETCH, UNIT), bf16),
            in_specs=[VM, part, VM, VM, VM] + [HBM] * half,
            out_specs=part,
            scratch_shapes=[pltpu.VMEM((2, ROWS, UNIT), bf16), pltpu.VMEM((ROWS, width), f32)],
            input_output_aliases={5: 0} if half else {},
            compiler_params=params(12),
            cost_estimate=cost(ROWS, 4, width),
        )(new, hidden_in, acc, own, other_output, *partial)

    return out_last(1, b4, out_last(0, a4))


def fits_ring(mesh):
    return dict(mesh.shape)["tp"] == RING and dict(mesh.shape)["pair"] == 2


def solution(mesh):
    placed = (
        P(("group", "pair"), "tp"),
        P(),
        P("tp", "pair"),
        P("tp", "pair"),
        P("tp", "pair"),
        P("tp", "pair"),
        P(("group", "pair"), None),
    )
    body = ring_body if fits_ring(mesh) else general_body
    step = jax.shard_map(
        body, mesh=mesh, in_specs=placed, out_specs=P(("group", "pair"), "tp"), check_vma=False
    )
    if not fits_ring(mesh):
        return step
    return step
```

```python
import math

import jax
import jax.numpy as jnp
from jax import lax
from jax.experimental import pallas as pl
from jax.experimental.pallas import tpu as pltpu

from jax.sharding import PartitionSpec as P

HQ = 64
KVH = 8
HD = 128
STRETCH = 256


THETA = 500000.0


def shortened(shard):

    def short(part):
        return part.astype(jnp.bfloat16) if part.dtype == jnp.float32 else part

    return jax.tree.map(short, shard)


def partner(shard, axis, apart):
    return lax.ppermute(shard, axis, [(i, i ^ 1 << apart) for i in range(lax.axis_size(axis))])


def token_layout(lengths):
    ends = jnp.cumsum(lengths, axis=1)
    offsets = jnp.arange(STRETCH, dtype=jnp.int32)
    finished = ends[:, None, :] <= offsets[None, :, None]
    request = jnp.sum(finished.astype(jnp.int32), axis=2)
    position = offsets[None, :] - jnp.sum(jnp.where(finished, lengths[:, None, :], 0), axis=2)
    return (request, position)


def scaled_freq(dims):
    freq = jnp.exp(dims.astype(jnp.float32) * (-math.log(THETA) / HD))
    wavelen = 2.0 * math.pi / freq
    smooth = (8192.0 / wavelen - 1.0) / 3.0
    middle = (1.0 - smooth) * freq / 8.0 + smooth * freq
    return jnp.where(wavelen < 2048.0, freq, jnp.where(wavelen > 8192.0, freq / 8.0, middle))


def rotary(projected, position, dims):
    freq = scaled_freq(dims[0::2])
    angle = position.astype(jnp.float32)[:, None] * freq[None, :]
    cosine = jnp.cos(angle)
    sine = jnp.sin(angle)
    first = projected[:, 0::2]
    second = projected[:, 1::2]
    turned = jnp.stack([first * cosine - second * sine, first * sine + second * cosine], axis=-1)
    return turned.reshape(projected.shape)


def attend(query, key, value, request, stretches, heads, groups):
    repeat = heads // groups
    query_blocks = query.reshape(stretches, STRETCH, groups, repeat, HD)
    key_blocks = key.reshape(stretches, STRETCH, groups, HD)
    value_blocks = value.reshape(stretches, STRETCH, groups, HD)
    scores = jnp.einsum(
        "cqgrd,ckgd->cgrqk", query_blocks, key_blocks, preferred_element_type=jnp.float32
    ) * (1.0 / math.sqrt(HD))
    offsets = jnp.arange(STRETCH, dtype=jnp.int32)
    keep = (request[:, :, None] == request[:, None, :]) & (offsets[:, None] >= offsets[None, :])[
        None
    ]
    scores = jnp.where(keep[:, None, None], scores, -1e30)
    top = jnp.max(scores, axis=-1, keepdims=True)
    weights = jnp.exp(scores - top)
    probs = (weights / jnp.sum(weights, axis=-1, keepdims=True)).astype(jnp.bfloat16)
    attended = jnp.einsum(
        "cgrqk,ckgd->cqgrd", probs, value_blocks, preferred_element_type=jnp.float32
    )
    return attended.reshape(stretches * STRETCH, heads * HD).astype(jnp.bfloat16)


def contract(left, right):
    return lax.dot_general(
        left, right, (((1,), (1,)), ((), ())), preferred_element_type=jnp.float32
    )


def bit_count(number):
    return number.bit_length() - 1


def assemble(parts, needed_bits, device, axis):
    for bit_index in range(max(needed_bits)):
        moving = [piece for piece, needed in zip(parts, needed_bits) if bit_index < needed]
        widths = [piece.shape[axis] for piece in moving]
        sent = jnp.concatenate(moving, axis=axis)
        arrived = partner(shortened(sent), "tp", bit_index).astype(sent.dtype)
        upper = device // 2**bit_index % 2 == 1
        cuts = []
        running = 0
        for width in widths[:-1]:
            running = running + width
            cuts.append(running)
        received = jnp.split(arrived, cuts, axis=axis)
        joined = []
        counter = 0
        for piece, needed in zip(parts, needed_bits):
            if bit_index < needed:
                other = received[counter]
                counter = counter + 1
                piece = jnp.where(
                    upper,
                    jnp.concatenate([other, piece], axis=axis),
                    jnp.concatenate([piece, other], axis=axis),
                )
            joined.append(piece)
        parts = joined
    return parts


def project(normed, query_rows, key_rows, value_rows, output_rows):
    query_full, key_full, value_full, output_full = (
        lax.all_gather(query_rows, "pair", axis=1, tiled=True),
        lax.all_gather(key_rows, "pair", axis=1, tiled=True),
        lax.all_gather(value_rows, "pair", axis=1, tiled=True),
        lax.all_gather(output_rows, "pair", axis=1, tiled=True),
    )
    query_pre = contract(normed, query_full)
    key_pre = contract(normed, key_full)
    value_pre = contract(normed, value_full)
    return (query_pre, key_pre, value_pre, output_full)


def general_body(hidden_in, norm_gain, query_weight, key_weight, value_weight, output_weight, lengths):
    tp_count = lax.axis_size("tp")
    device = lax.axis_index("tp")
    query_bits = bit_count(max(1, tp_count // HQ))
    group_bits = bit_count(max(1, tp_count // KVH))
    needed_bits = [query_bits, group_bits, group_bits]
    query_cols = query_weight.shape[0]
    stretches = lengths.shape[0]
    request, position = token_layout(lengths)
    position = position.reshape(-1)
    full_rows = lax.all_gather(hidden_in, "tp", axis=1, tiled=True)
    stream = full_rows.astype(jnp.float32)
    mean_square = jnp.mean(stream * stream, axis=1, keepdims=True)
    normed = (stream * lax.rsqrt(mean_square + 1e-05) * norm_gain[None, :]).astype(jnp.bfloat16)
    query_block, key_block, value_block = assemble(
        [query_weight, key_weight, value_weight], needed_bits, device, 0
    )
    query_pre, key_pre, value_pre, output_full = project(
        normed, query_block, key_block, value_block, output_weight
    )
    query_dims = jnp.arange(query_pre.shape[1], dtype=jnp.int32) % HD
    key_dims = jnp.arange(key_pre.shape[1], dtype=jnp.int32) % HD
    query = rotary(query_pre, position, query_dims).astype(jnp.bfloat16)
    key = rotary(key_pre, position, key_dims).astype(jnp.bfloat16)
    value = value_pre.astype(jnp.bfloat16)
    heads = query.shape[1] // HD
    groups = key.shape[1] // HD
    attended = attend(query, key, value, request, stretches, heads, groups)
    own_start = device * query_cols % (heads * HD)
    own_columns = lax.dynamic_slice_in_dim(attended, own_start, query_cols, 1)
    projected = contract(lax.all_gather(own_columns, "tp", axis=1, tiled=True), output_full)
    return (hidden_in.astype(jnp.float32) + projected).astype(jnp.bfloat16)


RING = 8
ROWS = STRETCH // 2
UNIT = 1024
ORDER = (0, 1, -1, -2, 2, 3, -3, -4)


def ring_place(t):
    return t // 2 if t % 2 == 0 else RING - 1 - t // 2


def ring_member(place):
    return 2 * place if place < RING // 2 else 2 * RING - 1 - 2 * place


def ring_swap(later):
    pairs = []
    for t in range(RING):
        for p in range(2):
            place = ring_place(t)
            step = 1 if (place + p + later) % 2 == 0 else -1
            pairs.append((t * 2 + p, ring_member((place + step) % RING) * 2 + p))
    return pairs


def swapped(shard, later):
    return lax.ppermute(shard, ("tp", "pair"), ring_swap(later))


def unit_of(index):
    t = lax.axis_index("tp")
    place = jnp.where(t % 2 == 0, t // 2, RING - 1 - t // 2)
    step = 1 - 2 * ((place + lax.axis_index("pair")) % 2)
    offset = jnp.int32(ORDER[0])
    for k in range(1, len(ORDER)):
        offset = jnp.where(index == k, ORDER[k], offset)
    where = (place + offset * step + RING) % RING
    return jnp.where(where < RING // 2, 2 * where, 2 * RING - 1 - 2 * where)


def columns_of(index):
    t = unit_of(index)
    mine = t // (RING // 2) == lax.axis_index("pair")
    return mine, pl.ds(pl.multiple_of(t % (RING // 2) * UNIT, UNIT), UNIT)


def add_units(xs, acc, own, others, first, count):
    def unit_step(u, carry):
        mine, cols = columns_of(first + u)
        for here, parts in ((mine, (own,)), (jnp.logical_not(mine), others)):

            @pl.when(here)
            def _(parts=parts):
                at = 0
                for part in parts:
                    rows = part.shape[0]
                    acc[:, at : at + rows] += contract(xs[u], part[:, cols])
                    at += rows

        return carry

    lax.fori_loop(0, count, unit_step, 0)


def load_kernel(*refs):
    *sources, target, sems = refs
    copies = []
    at = 0
    for n, source in enumerate(sources):
        rows = source.shape[0]
        copies.append(pltpu.make_async_copy(source, target.at[pl.ds(at, rows), :], sems.at[n]))
        at += rows
    for copy in copies:
        copy.start()
    for copy in copies:
        copy.wait()


def normed_unit(part, factor, gain_ref, index):
    base = unit_of(index) * (UNIT // 128)
    stream = part.astype(jnp.float32)
    lanes = []
    for k in range(UNIT // 128):
        gain = gain_ref[pl.ds(base + k, 1), :]
        lanes.append((stream[:, k * 128 : (k + 1) * 128] * factor * gain).astype(jnp.bfloat16))
    return lanes


def place_unit(xs, rows, n, part, factor, gain, index):
    for k, lane in enumerate(normed_unit(part, factor, gain, index)):
        xs[n, rows, k * 128 : (k + 1) * 128] = lane


VM = pl.BlockSpec(memory_space=pltpu.VMEM)
HBM = pl.BlockSpec(memory_space=pl.ANY)
SM = pl.BlockSpec(memory_space=pltpu.SMEM)


def params(mib):
    return pltpu.CompilerParams(vmem_limit_bytes=mib * 2**20)


def cost(rows, units, width):
    return pl.CostEstimate(
        flops=2 * rows * units * UNIT * width,
        bytes_accessed=2 * units * UNIT * width + 4 * rows * width,
        transcendentals=0,
    )


def stream_rows(s):
    return slice(s * ROWS, (s + 1) * ROWS)


def early_kernel(a0, b0, a1, b1, a2, b2, gain, factor, *refs):
    *weights, acc, xs = refs
    for s, (own, first, second) in enumerate(((a0, a1, a2), (b0, b1, b2))):
        rows = stream_rows(s)
        scale = factor[rows, :]
        place_unit(xs, rows, 0, own[...], scale, gain, 0)
        place_unit(xs, rows, 1, first[...], scale, gain, 1)
        place_unit(xs, rows, 2, second[:ROWS, :], scale, gain, 2)
        place_unit(xs, rows, 3, second[ROWS:, :], scale, gain, 3)
    acc[...] = jnp.zeros_like(acc)
    add_units(xs, acc, weights[0], weights[1:], 0, 4)


def middle_kernel(a3, b3, gain, factor, acc_in, *refs):
    *weights, acc, xs = refs
    for s, ref in enumerate((a3, b3)):
        for n in range(2):
            part = ref[n * ROWS : (n + 1) * ROWS, :]
            place_unit(xs, stream_rows(s), n, part, factor[stream_rows(s), :], gain, 4 + n)
    acc[...] = acc_in[...]
    add_units(xs, acc, weights[0], weights[1:], 4, 2)


def turned_heads(part, cosine, sine):
    lane = lax.broadcasted_iota(jnp.int32, part.shape, 1)
    other = jnp.where(lane % 2 == 0, pltpu.roll(part, HD - 1, 1), pltpu.roll(part, 1, 1))
    return (part * cosine + other * sine).astype(jnp.bfloat16)


def project_kernel(half, new, gain, factor, acc_in, *refs):
    *weights, acc, xs = refs
    rows = stream_rows(half)
    for n in range(2):
        part = new[n * ROWS : (n + 1) * ROWS, :]
        place_unit(xs, slice(0, ROWS), n, part, factor[rows, :], gain, 6 + n)
    acc[...] = acc_in[rows, :]
    add_units(xs, acc, weights[0], weights[1:], 6, 2)


def attend_kernel(half, lens, acc, cosine, sine, *refs):
    if half:
        key_early, value_early = refs[:2]
    attended, key_out, value_out = refs[-3:]
    rows = stream_rows(half)
    heads = UNIT // HD
    cos, sin = cosine[rows, :], sine[rows, :]
    key = turned_heads(acc[:, UNIT : UNIT + HD], cos, sin)
    value = acc[:, UNIT + HD :].astype(jnp.bfloat16)
    key_out[...] = key
    value_out[...] = value
    if half:
        key = jnp.concatenate([key_early[...], key], axis=0)
        value = jnp.concatenate([value_early[...], value], axis=0)
    shape = (ROWS, (half + 1) * ROWS)
    row = lax.broadcasted_iota(jnp.int32, shape, 0) + half * ROWS
    col = lax.broadcasted_iota(jnp.int32, shape, 1)
    row_request = jnp.zeros(shape, jnp.int32)
    col_request = jnp.zeros(shape, jnp.int32)
    end = jnp.int32(0)
    for k in range(lens.shape[1]):
        end = end + lens[0, k]
        row_request += (row >= end).astype(jnp.int32)
        col_request += (col >= end).astype(jnp.int32)
    keep = (row_request == col_request) & (row >= col)
    queries = [turned_heads(acc[:, h * HD : (h + 1) * HD], cos, sin) for h in range(heads)]
    scores = contract(jnp.concatenate(queries, axis=0), key) * (1.0 / math.sqrt(HD))
    scores = jnp.where(keep[None], scores.reshape(heads, *shape), -1e30)
    weights = jnp.exp(scores - jnp.max(scores, axis=2, keepdims=True))
    probs = (weights / jnp.sum(weights, axis=2, keepdims=True)).astype(jnp.bfloat16)
    probs = probs.reshape(heads * ROWS, shape[1])
    out = jnp.dot(probs, value, preferred_element_type=jnp.float32).astype(jnp.bfloat16)
    for h in range(heads):
        attended[:, h * HD : (h + 1) * HD] = out[h * ROWS : (h + 1) * ROWS, :]


def out_early_kernel(a0, b0, a1, b1, a2, b2, w0, w1, acc, xs):
    for s, (own, first, second) in enumerate(((a0, a1, a2), (b0, b1, b2))):
        rows = stream_rows(s)
        xs[0, rows, :] = own[...]
        xs[1, rows, :] = first[...]
        xs[2, rows, :] = second[:ROWS, :]
        xs[3, rows, :] = second[ROWS:, :]
    acc[...] = jnp.zeros_like(acc)
    add_units(xs, acc, w0, (w1,), 0, 4)


def out_middle_kernel(a3, b3, acc_in, hidden, w0, w1, acc, xs):
    for s, ref in enumerate((a3, b3)):
        xs[0, stream_rows(s), :] = ref[:ROWS, :]
        xs[1, stream_rows(s), :] = ref[ROWS:, :]
    acc[...] = acc_in[...] + hidden[...].astype(jnp.float32)
    add_units(xs, acc, w0, (w1,), 4, 2)


def out_last_kernel(half, new, acc_in, w0, w1, *refs):
    out, xs, acc = refs[-3:]
    xs[0] = new[:ROWS, :]
    xs[1] = new[ROWS:, :]
    acc[...] = acc_in[stream_rows(half), :]
    add_units(xs, acc, w0, (w1,), 6, 2)
    out[...] = acc[...].astype(jnp.bfloat16)


def summed_over_tp(value):
    for bits in ((1, 2), (2, 1), (4, 4)):
        pairs = [(t * 2 + p, (t ^ bits[p]) * 2 + p) for t in range(RING) for p in range(2)]
        value = value + lax.ppermute(value, ("tp", "pair"), pairs)
    return value


def kernel_call(kernel, **options):
    return pl.pallas_call(kernel, **options)


def in_vmem(value):
    return pltpu.with_memory_space_constraint(value, pltpu.VMEM)


def load(arrays):
    rows = sum(w.shape[0] for w in arrays)
    return kernel_call(
        load_kernel,
        out_shape=jax.ShapeDtypeStruct((rows, arrays[0].shape[1]), arrays[0].dtype),
        in_specs=[HBM] * len(arrays),
        out_specs=VM,
        scratch_shapes=[pltpu.SemaphoreType.DMA((len(arrays),))],
        compiler_params=params(2),
        cost_estimate=cost(0, rows * arrays[0].shape[1] // UNIT, 1),
    )(*(pltpu.with_memory_space_constraint(w, pltpu.HBM) for w in arrays))


def token_position(lengths):
    count = lengths.shape[0]
    upto = jnp.arange(count)[:, None] >= jnp.arange(count)[None, :]
    ends = jnp.sum(jnp.where(upto, lengths[None, :], 0), axis=1)
    offsets = jnp.arange(STRETCH, dtype=jnp.int32)
    finished = ends[None, :] <= offsets[:, None]
    return offsets - jnp.sum(jnp.where(finished, lengths[None, :], 0), axis=1)


def after(value, *others):
    return lax.optimization_barrier((value, *others))


def ring_body(*args):
    return ring_layer(*args)


def ring_layer(hidden_in, norm_gain, query_weight, key_weight, value_weight, output_weight, lengths):
    f32, bf16 = jnp.float32, jnp.bfloat16
    a0, b0 = hidden_in[:ROWS], hidden_in[ROWS:]
    a1, b1 = swapped(a0, 0), swapped(b0, 0)
    projections = (query_weight, key_weight, value_weight)
    others = []
    for w in projections:
        others.append(in_vmem(partner(w, "pair", 0)))
    qkv = sum(w.shape[0] for w in projections)
    stream = hidden_in.astype(f32)
    squares = jnp.sum(stream * stream, axis=1).reshape(2, 128)
    squares = summed_over_tp(squares)
    factor = lax.rsqrt(squares / (RING * UNIT) + 1e-05)
    factor = jnp.broadcast_to(factor.reshape(STRETCH, 1), (STRETCH, 128))
    a2 = swapped(jnp.concatenate([a0, a1], axis=0), 1)
    b2 = swapped(jnp.concatenate([b0, b1], axis=0), 1)
    gain = norm_gain.reshape(RING * UNIT // 128, 128)
    position = token_position(lengths[0])
    lane = jnp.arange(HD, dtype=jnp.int32)
    angle = position.astype(f32)[:, None] * scaled_freq(lane - lane % 2)[None, :]
    cosine = jnp.cos(angle)
    sine = jnp.sin(angle) * jnp.where(lane % 2 == 0, -1.0, 1.0)[None, :]
    other_output = in_vmem(partner(output_weight, "pair", 0))
    own = load(projections)
    a2, own = after(a2, own)
    weights = (own, *others)
    a3, b3 = swapped(a2, 0), swapped(b2, 0)

    factor, cosine, sine, lengths = after(factor, cosine, sine, lengths)
    acc_shape = jax.ShapeDtypeStruct((STRETCH, qkv), f32)
    acc = kernel_call(
        early_kernel,
        out_shape=acc_shape,
        in_specs=[VM] * 12,
        out_specs=VM,
        scratch_shapes=[pltpu.VMEM((4, STRETCH, UNIT), bf16)],
        compiler_params=params(12),
        cost_estimate=cost(STRETCH, 4, qkv),
    )(a0, b0, a1, b1, a2, b2, gain, factor, *weights)
    a3, acc = after(a3, acc)
    a4, b4 = swapped(a3, 1), swapped(b3, 1)
    acc = kernel_call(
        middle_kernel,
        out_shape=acc_shape,
        in_specs=[VM] * 9,
        out_specs=VM,
        scratch_shapes=[pltpu.VMEM((2, STRETCH, UNIT), bf16)],
        compiler_params=params(12),
        cost_estimate=cost(STRETCH, 2, qkv),
    )(a3, b3, gain, factor, acc, *weights)

    def project(half, new):
        return kernel_call(
            lambda *refs: project_kernel(half, *refs),
            out_shape=jax.ShapeDtypeStruct((ROWS, qkv), f32),
            in_specs=[VM] * 8,
            out_specs=VM,
            scratch_shapes=[pltpu.VMEM((2, ROWS, UNIT), bf16)],
            compiler_params=params(12),
            cost_estimate=cost(ROWS, 2, qkv),
        )(new, gain, factor, acc, *weights)

    def attend_stream(half, projected, early):
        kv = jax.ShapeDtypeStruct((ROWS, HD), bf16)
        return kernel_call(
            lambda *refs: attend_kernel(half, *refs),
            out_shape=(jax.ShapeDtypeStruct((ROWS, UNIT), bf16), kv, kv),
            in_specs=[SM] + [VM] * (3 + len(early)),
            out_specs=(VM, VM, VM),
            compiler_params=params(12),
            cost_estimate=cost(ROWS, 2, qkv),
        )(lengths, projected, cosine, sine, *early)

    a0, key_a, value_a = attend_stream(0, project(0, a4), ())
    a1 = swapped(a0, 0)
    projected = project(1, b4)
    a1, projected = after(a1, projected)
    a2 = swapped(jnp.concatenate([a0, a1], axis=0), 1)
    b0, _, _ = attend_stream(1, projected, (key_a, value_a))
    b1 = swapped(b0, 0)
    b2 = swapped(jnp.concatenate([b0, b1], axis=0), 1)
    a3, b3 = swapped(a2, 0), swapped(b2, 0)
    width = output_weight.shape[0]
    acc_shape = jax.ShapeDtypeStruct((STRETCH, width), f32)
    acc = kernel_call(
        out_early_kernel,
        out_shape=acc_shape,
        in_specs=[VM] * 8,
        out_specs=VM,
        scratch_shapes=[pltpu.VMEM((4, STRETCH, UNIT), bf16)],
        compiler_params=params(12),
        cost_estimate=cost(STRETCH, 4, width),
    )(a0, b0, a1, b1, a2, b2, output_weight, other_output)
    a3, acc = after(a3, acc)
    a4, b4 = swapped(a3, 1), swapped(b3, 1)
    acc = kernel_call(
        out_middle_kernel,
        out_shape=acc_shape,
        in_specs=[VM] * 6,
        out_specs=VM,
        scratch_shapes=[pltpu.VMEM((2, STRETCH, UNIT), bf16)],
        compiler_params=params(12),
        cost_estimate=cost(STRETCH, 2, width),
    )(a3, b3, acc, hidden_in, output_weight, other_output)

    def out_last(half, new, *partial):
        part = pl.BlockSpec((ROWS, UNIT), lambda i: (half, 0))
        return kernel_call(
            lambda *refs: out_last_kernel(half, *refs),
            grid=(1,),
            out_shape=jax.ShapeDtypeStruct((STRETCH, UNIT), bf16),
            in_specs=[VM, VM, VM, VM] + [HBM] * half,
            out_specs=part,
            scratch_shapes=[pltpu.VMEM((2, ROWS, UNIT), bf16), pltpu.VMEM((ROWS, width), f32)],
            input_output_aliases={4: 0} if half else {},
            compiler_params=params(12),
            cost_estimate=cost(ROWS, 4, width),
        )(new, acc, output_weight, other_output, *partial)

    return out_last(1, b4, out_last(0, a4))


def fits_ring(mesh):
    return dict(mesh.shape)["tp"] == RING and dict(mesh.shape)["pair"] == 2


def solution(mesh):
    placed = (
        P(("group", "pair"), "tp"),
        P(),
        P("tp", "pair"),
        P("tp", "pair"),
        P("tp", "pair"),
        P("tp", "pair"),
        P(("group", "pair"), None),
    )
    body = ring_body if fits_ring(mesh) else general_body
    step = jax.shard_map(
        body, mesh=mesh, in_specs=placed, out_specs=P(("group", "pair"), "tp"), check_vma=False
    )
    if not fits_ring(mesh):
        return step
    return step
```

```python
import math

import jax
import jax.numpy as jnp
from jax import lax
from jax.experimental import pallas as pl
from jax.experimental.pallas import tpu as pltpu

from jax.sharding import PartitionSpec as P

HQ = 64
KVH = 8
HD = 128
STRETCH = 256


THETA = 500000.0


def shortened(shard):

    def short(part):
        return part.astype(jnp.bfloat16) if part.dtype == jnp.float32 else part

    return jax.tree.map(short, shard)


def partner(shard, axis, apart):
    return lax.ppermute(shard, axis, [(i, i ^ 1 << apart) for i in range(lax.axis_size(axis))])


def token_layout(lengths):
    ends = jnp.cumsum(lengths, axis=1)
    offsets = jnp.arange(STRETCH, dtype=jnp.int32)
    finished = ends[:, None, :] <= offsets[None, :, None]
    request = jnp.sum(finished.astype(jnp.int32), axis=2)
    position = offsets[None, :] - jnp.sum(jnp.where(finished, lengths[:, None, :], 0), axis=2)
    return (request, position)


def scaled_freq(dims):
    freq = jnp.exp(dims.astype(jnp.float32) * (-math.log(THETA) / HD))
    wavelen = 2.0 * math.pi / freq
    smooth = (8192.0 / wavelen - 1.0) / 3.0
    middle = (1.0 - smooth) * freq / 8.0 + smooth * freq
    return jnp.where(wavelen < 2048.0, freq, jnp.where(wavelen > 8192.0, freq / 8.0, middle))


def rotary(projected, position, dims):
    freq = scaled_freq(dims[0::2])
    angle = position.astype(jnp.float32)[:, None] * freq[None, :]
    cosine = jnp.cos(angle)
    sine = jnp.sin(angle)
    first = projected[:, 0::2]
    second = projected[:, 1::2]
    turned = jnp.stack([first * cosine - second * sine, first * sine + second * cosine], axis=-1)
    return turned.reshape(projected.shape)


def attend(query, key, value, request, stretches, heads, groups):
    repeat = heads // groups
    query_blocks = query.reshape(stretches, STRETCH, groups, repeat, HD)
    key_blocks = key.reshape(stretches, STRETCH, groups, HD)
    value_blocks = value.reshape(stretches, STRETCH, groups, HD)
    scores = jnp.einsum(
        "cqgrd,ckgd->cgrqk", query_blocks, key_blocks, preferred_element_type=jnp.float32
    ) * (1.0 / math.sqrt(HD))
    offsets = jnp.arange(STRETCH, dtype=jnp.int32)
    keep = (request[:, :, None] == request[:, None, :]) & (offsets[:, None] >= offsets[None, :])[
        None
    ]
    scores = jnp.where(keep[:, None, None], scores, -1e30)
    top = jnp.max(scores, axis=-1, keepdims=True)
    weights = jnp.exp(scores - top)
    probs = (weights / jnp.sum(weights, axis=-1, keepdims=True)).astype(jnp.bfloat16)
    attended = jnp.einsum(
        "cgrqk,ckgd->cqgrd", probs, value_blocks, preferred_element_type=jnp.float32
    )
    return attended.reshape(stretches * STRETCH, heads * HD).astype(jnp.bfloat16)


def contract(left, right):
    return lax.dot_general(
        left, right, (((1,), (1,)), ((), ())), preferred_element_type=jnp.float32
    )


def bit_count(number):
    return number.bit_length() - 1


def assemble(parts, needed_bits, device, axis):
    for bit_index in range(max(needed_bits)):
        moving = [piece for piece, needed in zip(parts, needed_bits) if bit_index < needed]
        widths = [piece.shape[axis] for piece in moving]
        sent = jnp.concatenate(moving, axis=axis)
        arrived = partner(shortened(sent), "tp", bit_index).astype(sent.dtype)
        upper = device // 2**bit_index % 2 == 1
        cuts = []
        running = 0
        for width in widths[:-1]:
            running = running + width
            cuts.append(running)
        received = jnp.split(arrived, cuts, axis=axis)
        joined = []
        counter = 0
        for piece, needed in zip(parts, needed_bits):
            if bit_index < needed:
                other = received[counter]
                counter = counter + 1
                piece = jnp.where(
                    upper,
                    jnp.concatenate([other, piece], axis=axis),
                    jnp.concatenate([piece, other], axis=axis),
                )
            joined.append(piece)
        parts = joined
    return parts


def project(normed, query_rows, key_rows, value_rows, output_rows):
    query_full, key_full, value_full, output_full = (
        lax.all_gather(query_rows, "pair", axis=1, tiled=True),
        lax.all_gather(key_rows, "pair", axis=1, tiled=True),
        lax.all_gather(value_rows, "pair", axis=1, tiled=True),
        lax.all_gather(output_rows, "pair", axis=1, tiled=True),
    )
    query_pre = contract(normed, query_full)
    key_pre = contract(normed, key_full)
    value_pre = contract(normed, value_full)
    return (query_pre, key_pre, value_pre, output_full)


def general_body(hidden_in, norm_gain, query_weight, key_weight, value_weight, output_weight, lengths):
    tp_count = lax.axis_size("tp")
    device = lax.axis_index("tp")
    query_bits = bit_count(max(1, tp_count // HQ))
    group_bits = bit_count(max(1, tp_count // KVH))
    needed_bits = [query_bits, group_bits, group_bits]
    query_cols = query_weight.shape[0]
    stretches = lengths.shape[0]
    request, position = token_layout(lengths)
    position = position.reshape(-1)
    full_rows = lax.all_gather(hidden_in, "tp", axis=1, tiled=True)
    stream = full_rows.astype(jnp.float32)
    mean_square = jnp.mean(stream * stream, axis=1, keepdims=True)
    normed = (stream * lax.rsqrt(mean_square + 1e-05) * norm_gain[None, :]).astype(jnp.bfloat16)
    query_block, key_block, value_block = assemble(
        [query_weight, key_weight, value_weight], needed_bits, device, 0
    )
    query_pre, key_pre, value_pre, output_full = project(
        normed, query_block, key_block, value_block, output_weight
    )
    query_dims = jnp.arange(query_pre.shape[1], dtype=jnp.int32) % HD
    key_dims = jnp.arange(key_pre.shape[1], dtype=jnp.int32) % HD
    query = rotary(query_pre, position, query_dims).astype(jnp.bfloat16)
    key = rotary(key_pre, position, key_dims).astype(jnp.bfloat16)
    value = value_pre.astype(jnp.bfloat16)
    heads = query.shape[1] // HD
    groups = key.shape[1] // HD
    attended = attend(query, key, value, request, stretches, heads, groups)
    own_start = device * query_cols % (heads * HD)
    own_columns = lax.dynamic_slice_in_dim(attended, own_start, query_cols, 1)
    projected = contract(lax.all_gather(own_columns, "tp", axis=1, tiled=True), output_full)
    return (hidden_in.astype(jnp.float32) + projected).astype(jnp.bfloat16)


RING = 8
ROWS = STRETCH // 2
UNIT = 1024
ORDER = (0, 1, -1, -2, 2, 3, -3, -4)


def ring_place(t):
    return t // 2 if t % 2 == 0 else RING - 1 - t // 2


def ring_member(place):
    return 2 * place if place < RING // 2 else 2 * RING - 1 - 2 * place


def ring_swap(later):
    pairs = []
    for t in range(RING):
        for p in range(2):
            place = ring_place(t)
            step = 1 if (place + p + later) % 2 == 0 else -1
            pairs.append((t * 2 + p, ring_member((place + step) % RING) * 2 + p))
    return pairs


def swapped(shard, later):
    return lax.ppermute(shard, ("tp", "pair"), ring_swap(later))


def unit_of(index):
    t = lax.axis_index("tp")
    place = jnp.where(t % 2 == 0, t // 2, RING - 1 - t // 2)
    step = 1 - 2 * ((place + lax.axis_index("pair")) % 2)
    offset = jnp.int32(ORDER[0])
    for k in range(1, len(ORDER)):
        offset = jnp.where(index == k, ORDER[k], offset)
    where = (place + offset * step + RING) % RING
    return jnp.where(where < RING // 2, 2 * where, 2 * RING - 1 - 2 * where)


def columns_of(index):
    t = unit_of(index)
    mine = t // (RING // 2) == lax.axis_index("pair")
    return mine, pl.ds(pl.multiple_of(t % (RING // 2) * UNIT, UNIT), UNIT)


def add_units(xs, acc, own, others, first, count):
    def unit_step(u, carry):
        mine, cols = columns_of(first + u)
        for here, parts in ((mine, (own,)), (jnp.logical_not(mine), others)):

            @pl.when(here)
            def _(parts=parts):
                at = 0
                for part in parts:
                    rows = part.shape[0]
                    acc[:, at : at + rows] += contract(xs[u], part[:, cols])
                    at += rows

        return carry

    lax.fori_loop(0, count, unit_step, 0)


def load_kernel(*refs):
    *sources, target, sems = refs
    copies = []
    at = 0
    for n, source in enumerate(sources):
        rows = source.shape[0]
        copies.append(pltpu.make_async_copy(source, target.at[pl.ds(at, rows), :], sems.at[n]))
        at += rows
    for copy in copies:
        copy.start()
    for copy in copies:
        copy.wait()


def normed_unit(part, factor, gain_ref, index):
    base = unit_of(index) * (UNIT // 128)
    stream = part.astype(jnp.float32)
    lanes = []
    for k in range(UNIT // 128):
        gain = gain_ref[pl.ds(base + k, 1), :]
        lanes.append((stream[:, k * 128 : (k + 1) * 128] * factor * gain).astype(jnp.bfloat16))
    return lanes


def place_unit(xs, rows, n, part, factor, gain, index):
    for k, lane in enumerate(normed_unit(part, factor, gain, index)):
        xs[n, rows, k * 128 : (k + 1) * 128] = lane


VM = pl.BlockSpec(memory_space=pltpu.VMEM)
HBM = pl.BlockSpec(memory_space=pl.ANY)
SM = pl.BlockSpec(memory_space=pltpu.SMEM)


def params(mib):
    return pltpu.CompilerParams(vmem_limit_bytes=mib * 2**20)


def cost(rows, units, width):
    return pl.CostEstimate(
        flops=2 * rows * units * UNIT * width,
        bytes_accessed=2 * units * UNIT * width + 4 * rows * width,
        transcendentals=0,
    )


def stream_rows(s):
    return slice(s * ROWS, (s + 1) * ROWS)


def early_kernel(a0, b0, a1, b1, a2, b2, gain, factor, *refs):
    *weights, acc, xs = refs
    for s, (own, first, second) in enumerate(((a0, a1, a2), (b0, b1, b2))):
        rows = stream_rows(s)
        scale = factor[rows, :]
        place_unit(xs, rows, 0, own[...], scale, gain, 0)
        place_unit(xs, rows, 1, first[...], scale, gain, 1)
        place_unit(xs, rows, 2, second[:ROWS, :], scale, gain, 2)
        place_unit(xs, rows, 3, second[ROWS:, :], scale, gain, 3)
    acc[...] = jnp.zeros_like(acc)
    add_units(xs, acc, weights[0], weights[1:], 0, 4)


def middle_kernel(a3, b3, gain, factor, acc_in, *refs):
    *weights, acc, xs = refs
    for s, ref in enumerate((a3, b3)):
        for n in range(2):
            part = ref[n * ROWS : (n + 1) * ROWS, :]
            place_unit(xs, stream_rows(s), n, part, factor[stream_rows(s), :], gain, 4 + n)
    acc[...] = acc_in[...]
    add_units(xs, acc, weights[0], weights[1:], 4, 2)


def turned_heads(part, cosine, sine):
    lane = lax.broadcasted_iota(jnp.int32, part.shape, 1)
    other = jnp.where(lane % 2 == 0, pltpu.roll(part, HD - 1, 1), pltpu.roll(part, 1, 1))
    return (part * cosine + other * sine).astype(jnp.bfloat16)


def project_kernel(half, new, gain, factor, acc_in, *refs):
    *weights, acc, xs = refs
    rows = stream_rows(half)
    for n in range(2):
        part = new[n * ROWS : (n + 1) * ROWS, :]
        place_unit(xs, slice(0, ROWS), n, part, factor[rows, :], gain, 6 + n)
    acc[...] = acc_in[rows, :]
    add_units(xs, acc, weights[0], weights[1:], 6, 2)


def attend_kernel(half, lens, acc, cosine, sine, *refs):
    if half:
        key_early, value_early = refs[:2]
    attended, key_out, value_out = refs[-3:]
    rows = stream_rows(half)
    heads = UNIT // HD
    cos, sin = cosine[rows, :], sine[rows, :]
    key = turned_heads(acc[:, UNIT : UNIT + HD], cos, sin)
    value = acc[:, UNIT + HD :].astype(jnp.bfloat16)
    key_out[...] = key
    value_out[...] = value
    if half:
        key = jnp.concatenate([key_early[...], key], axis=0)
        value = jnp.concatenate([value_early[...], value], axis=0)
    shape = (ROWS, (half + 1) * ROWS)
    row = lax.broadcasted_iota(jnp.int32, shape, 0) + half * ROWS
    col = lax.broadcasted_iota(jnp.int32, shape, 1)
    row_request = jnp.zeros(shape, jnp.int32)
    col_request = jnp.zeros(shape, jnp.int32)
    end = jnp.int32(0)
    for k in range(lens.shape[1]):
        end = end + lens[0, k]
        row_request += (row >= end).astype(jnp.int32)
        col_request += (col >= end).astype(jnp.int32)
    keep = (row_request == col_request) & (row >= col)
    queries = [turned_heads(acc[:, h * HD : (h + 1) * HD], cos, sin) for h in range(heads)]
    scores = contract(jnp.concatenate(queries, axis=0), key) * (1.0 / math.sqrt(HD))
    scores = jnp.where(keep[None], scores.reshape(heads, *shape), -1e30)
    weights = jnp.exp(scores - jnp.max(scores, axis=2, keepdims=True))
    probs = (weights / jnp.sum(weights, axis=2, keepdims=True)).astype(jnp.bfloat16)
    probs = probs.reshape(heads * ROWS, shape[1])
    out = jnp.dot(probs, value, preferred_element_type=jnp.float32).astype(jnp.bfloat16)
    for h in range(heads):
        attended[:, h * HD : (h + 1) * HD] = out[h * ROWS : (h + 1) * ROWS, :]


def stream_units(xs, *streams):
    for s, units in enumerate(streams):
        for n, unit in enumerate(units):
            xs[n, stream_rows(s), :] = unit[...]


def out_early_kernel(a0, a1, a2, a3, b0, b1, b2, b3, w0, w1, acc, xs):
    stream_units(xs, (a0, a1, a2, a3), (b0, b1, b2, b3))
    acc[...] = jnp.zeros_like(acc)
    add_units(xs, acc, w0, (w1,), 0, 4)


def out_middle_kernel(a4, a5, b4, b5, acc_in, hidden, w0, w1, acc, xs):
    stream_units(xs, (a4, a5), (b4, b5))
    acc[...] = acc_in[...] + hidden[...].astype(jnp.float32)
    add_units(xs, acc, w0, (w1,), 4, 2)


def out_last_kernel(half, new, newer, acc_in, w0, w1, *refs):
    out, xs, acc = refs[-3:]
    stream_units(xs, (new, newer))
    acc[...] = acc_in[stream_rows(half), :]
    add_units(xs, acc, w0, (w1,), 6, 2)
    out[...] = acc[...].astype(jnp.bfloat16)


def summed_over_tp(value):
    for bits in ((1, 2), (2, 1), (4, 4)):
        pairs = [(t * 2 + p, (t ^ bits[p]) * 2 + p) for t in range(RING) for p in range(2)]
        value = value + lax.ppermute(value, ("tp", "pair"), pairs)
    return value


def kernel_call(kernel, **options):
    return pl.pallas_call(kernel, **options)


def in_vmem(value):
    return pltpu.with_memory_space_constraint(value, pltpu.VMEM)


def load(arrays):
    rows = sum(w.shape[0] for w in arrays)
    return kernel_call(
        load_kernel,
        out_shape=jax.ShapeDtypeStruct((rows, arrays[0].shape[1]), arrays[0].dtype),
        in_specs=[HBM] * len(arrays),
        out_specs=VM,
        scratch_shapes=[pltpu.SemaphoreType.DMA((len(arrays),))],
        compiler_params=params(2),
        cost_estimate=cost(0, rows * arrays[0].shape[1] // UNIT, 1),
    )(*(pltpu.with_memory_space_constraint(w, pltpu.HBM) for w in arrays))


def token_position(lengths):
    count = lengths.shape[0]
    upto = jnp.arange(count)[:, None] >= jnp.arange(count)[None, :]
    ends = jnp.sum(jnp.where(upto, lengths[None, :], 0), axis=1)
    offsets = jnp.arange(STRETCH, dtype=jnp.int32)
    finished = ends[None, :] <= offsets[:, None]
    return offsets - jnp.sum(jnp.where(finished, lengths[None, :], 0), axis=1)


def after(value, *others):
    return lax.optimization_barrier((value, *others))


def ring_body(*args):
    return ring_layer(*args)


def ring_layer(hidden_in, norm_gain, query_weight, key_weight, value_weight, output_weight, lengths):
    f32, bf16 = jnp.float32, jnp.bfloat16
    a0, b0 = hidden_in[:ROWS], hidden_in[ROWS:]
    a1, b1 = swapped(a0, 0), swapped(b0, 0)
    projections = (query_weight, key_weight, value_weight)
    others = []
    for w in projections:
        others.append(in_vmem(partner(w, "pair", 0)))
    qkv = sum(w.shape[0] for w in projections)
    stream = hidden_in.astype(f32)
    squares = jnp.sum(stream * stream, axis=1).reshape(2, 128)
    squares = summed_over_tp(squares)
    factor = lax.rsqrt(squares / (RING * UNIT) + 1e-05)
    factor = jnp.broadcast_to(factor.reshape(STRETCH, 1), (STRETCH, 128))
    a2 = swapped(jnp.concatenate([a0, a1], axis=0), 1)
    b2 = swapped(jnp.concatenate([b0, b1], axis=0), 1)
    gain = norm_gain.reshape(RING * UNIT // 128, 128)
    position = token_position(lengths[0])
    lane = jnp.arange(HD, dtype=jnp.int32)
    angle = position.astype(f32)[:, None] * scaled_freq(lane - lane % 2)[None, :]
    cosine = jnp.cos(angle)
    sine = jnp.sin(angle) * jnp.where(lane % 2 == 0, -1.0, 1.0)[None, :]
    other_output = in_vmem(partner(output_weight, "pair", 0))
    own = load(projections)
    a2, own = after(a2, own)
    weights = (own, *others)
    a3, b3 = swapped(a2, 0), swapped(b2, 0)

    factor, cosine, sine, lengths = after(factor, cosine, sine, lengths)
    acc_shape = jax.ShapeDtypeStruct((STRETCH, qkv), f32)
    acc = kernel_call(
        early_kernel,
        out_shape=acc_shape,
        in_specs=[VM] * 12,
        out_specs=VM,
        scratch_shapes=[pltpu.VMEM((4, STRETCH, UNIT), bf16)],
        compiler_params=params(12),
        cost_estimate=cost(STRETCH, 4, qkv),
    )(a0, b0, a1, b1, a2, b2, gain, factor, *weights)
    a3, acc = after(a3, acc)
    a4, b4 = swapped(a3, 1), swapped(b3, 1)
    acc = kernel_call(
        middle_kernel,
        out_shape=acc_shape,
        in_specs=[VM] * 9,
        out_specs=VM,
        scratch_shapes=[pltpu.VMEM((2, STRETCH, UNIT), bf16)],
        compiler_params=params(12),
        cost_estimate=cost(STRETCH, 2, qkv),
    )(a3, b3, gain, factor, acc, *weights)

    def project(half, new):
        return kernel_call(
            lambda *refs: project_kernel(half, *refs),
            out_shape=jax.ShapeDtypeStruct((ROWS, qkv), f32),
            in_specs=[VM] * 8,
            out_specs=VM,
            scratch_shapes=[pltpu.VMEM((2, ROWS, UNIT), bf16)],
            compiler_params=params(12),
            cost_estimate=cost(ROWS, 2, qkv),
        )(new, gain, factor, acc, *weights)

    def attend_stream(half, projected, early):
        kv = jax.ShapeDtypeStruct((ROWS, HD), bf16)
        return kernel_call(
            lambda *refs: attend_kernel(half, *refs),
            out_shape=(jax.ShapeDtypeStruct((ROWS, UNIT), bf16), kv, kv),
            in_specs=[SM] + [VM] * (3 + len(early)),
            out_specs=(VM, VM, VM),
            compiler_params=params(12),
            cost_estimate=cost(ROWS, 2, qkv),
        )(lengths, projected, cosine, sine, *early)

    a0, key_a, value_a = attend_stream(0, project(0, a4), ())
    a1, a2 = swapped(a0, 0), swapped(a0, 1)
    projected = project(1, b4)
    a1, projected = after(a1, projected)
    a3 = swapped(a1, 1)
    b0, _, _ = attend_stream(1, projected, (key_a, value_a))
    b1, b2 = swapped(b0, 0), swapped(b0, 1)
    a4, b3 = swapped(a2, 0), swapped(b1, 1)
    a5, b4 = swapped(a3, 0), swapped(b2, 0)
    a6, b5 = swapped(a4, 1), swapped(b3, 0)
    width = output_weight.shape[0]
    acc_shape = jax.ShapeDtypeStruct((STRETCH, width), f32)
    acc = kernel_call(
        out_early_kernel,
        out_shape=acc_shape,
        in_specs=[VM] * 10,
        out_specs=VM,
        scratch_shapes=[pltpu.VMEM((4, STRETCH, UNIT), bf16)],
        compiler_params=params(12),
        cost_estimate=cost(STRETCH, 4, width),
    )(a0, a1, a2, a3, b0, b1, b2, b3, output_weight, other_output)
    a5, acc = after(a5, acc)
    a7, b6, b7 = swapped(a5, 1), swapped(b4, 1), swapped(b5, 1)
    acc = kernel_call(
        out_middle_kernel,
        out_shape=acc_shape,
        in_specs=[VM] * 8,
        out_specs=VM,
        scratch_shapes=[pltpu.VMEM((2, STRETCH, UNIT), bf16)],
        compiler_params=params(12),
        cost_estimate=cost(STRETCH, 2, width),
    )(a4, a5, b4, b5, acc, hidden_in, output_weight, other_output)

    def out_last(half, new, newer, *partial):
        part = pl.BlockSpec((ROWS, UNIT), lambda i: (half, 0))
        return kernel_call(
            lambda *refs: out_last_kernel(half, *refs),
            grid=(1,),
            out_shape=jax.ShapeDtypeStruct((STRETCH, UNIT), bf16),
            in_specs=[VM, VM, VM, VM, VM] + [HBM] * half,
            out_specs=part,
            scratch_shapes=[pltpu.VMEM((2, ROWS, UNIT), bf16), pltpu.VMEM((ROWS, width), f32)],
            input_output_aliases={5: 0} if half else {},
            compiler_params=params(12),
            cost_estimate=cost(ROWS, 4, width),
        )(new, newer, acc, output_weight, other_output, *partial)

    return out_last(1, b6, b7, out_last(0, a6, a7))


def fits_ring(mesh):
    return dict(mesh.shape)["tp"] == RING and dict(mesh.shape)["pair"] == 2


def solution(mesh):
    placed = (
        P(("group", "pair"), "tp"),
        P(),
        P("tp", "pair"),
        P("tp", "pair"),
        P("tp", "pair"),
        P("tp", "pair"),
        P(("group", "pair"), None),
    )
    body = ring_body if fits_ring(mesh) else general_body
    step = jax.shard_map(
        body, mesh=mesh, in_specs=placed, out_specs=P(("group", "pair"), "tp"), check_vma=False
    )
    if not fits_ring(mesh):
        return step
    return step
```

```python
import math

import jax
import jax.numpy as jnp
from jax import lax
from jax.experimental import pallas as pl
from jax.experimental.pallas import tpu as pltpu

from jax.sharding import PartitionSpec as P

HQ = 64
KVH = 8
HD = 128
STRETCH = 256


THETA = 500000.0


def shortened(shard):

    def short(part):
        return part.astype(jnp.bfloat16) if part.dtype == jnp.float32 else part

    return jax.tree.map(short, shard)


def partner(shard, axis, apart):
    return lax.ppermute(shard, axis, [(i, i ^ 1 << apart) for i in range(lax.axis_size(axis))])


def token_layout(lengths):
    ends = jnp.cumsum(lengths, axis=1)
    offsets = jnp.arange(STRETCH, dtype=jnp.int32)
    finished = ends[:, None, :] <= offsets[None, :, None]
    request = jnp.sum(finished.astype(jnp.int32), axis=2)
    position = offsets[None, :] - jnp.sum(jnp.where(finished, lengths[:, None, :], 0), axis=2)
    return (request, position)


def scaled_freq(dims):
    freq = jnp.exp(dims.astype(jnp.float32) * (-math.log(THETA) / HD))
    wavelen = 2.0 * math.pi / freq
    smooth = (8192.0 / wavelen - 1.0) / 3.0
    middle = (1.0 - smooth) * freq / 8.0 + smooth * freq
    return jnp.where(wavelen < 2048.0, freq, jnp.where(wavelen > 8192.0, freq / 8.0, middle))


def rotary(projected, position, dims):
    freq = scaled_freq(dims[0::2])
    angle = position.astype(jnp.float32)[:, None] * freq[None, :]
    cosine = jnp.cos(angle)
    sine = jnp.sin(angle)
    first = projected[:, 0::2]
    second = projected[:, 1::2]
    turned = jnp.stack([first * cosine - second * sine, first * sine + second * cosine], axis=-1)
    return turned.reshape(projected.shape)


def attend(query, key, value, request, stretches, heads, groups):
    repeat = heads // groups
    query_blocks = query.reshape(stretches, STRETCH, groups, repeat, HD)
    key_blocks = key.reshape(stretches, STRETCH, groups, HD)
    value_blocks = value.reshape(stretches, STRETCH, groups, HD)
    scores = jnp.einsum(
        "cqgrd,ckgd->cgrqk", query_blocks, key_blocks, preferred_element_type=jnp.float32
    ) * (1.0 / math.sqrt(HD))
    offsets = jnp.arange(STRETCH, dtype=jnp.int32)
    keep = (request[:, :, None] == request[:, None, :]) & (offsets[:, None] >= offsets[None, :])[
        None
    ]
    scores = jnp.where(keep[:, None, None], scores, -1e30)
    top = jnp.max(scores, axis=-1, keepdims=True)
    weights = jnp.exp(scores - top)
    probs = (weights / jnp.sum(weights, axis=-1, keepdims=True)).astype(jnp.bfloat16)
    attended = jnp.einsum(
        "cgrqk,ckgd->cqgrd", probs, value_blocks, preferred_element_type=jnp.float32
    )
    return attended.reshape(stretches * STRETCH, heads * HD).astype(jnp.bfloat16)


def contract(left, right):
    return lax.dot_general(
        left, right, (((1,), (1,)), ((), ())), preferred_element_type=jnp.float32
    )


def bit_count(number):
    return number.bit_length() - 1


def assemble(parts, needed_bits, device, axis):
    for bit_index in range(max(needed_bits)):
        moving = [piece for piece, needed in zip(parts, needed_bits) if bit_index < needed]
        widths = [piece.shape[axis] for piece in moving]
        sent = jnp.concatenate(moving, axis=axis)
        arrived = partner(shortened(sent), "tp", bit_index).astype(sent.dtype)
        upper = device // 2**bit_index % 2 == 1
        cuts = []
        running = 0
        for width in widths[:-1]:
            running = running + width
            cuts.append(running)
        received = jnp.split(arrived, cuts, axis=axis)
        joined = []
        counter = 0
        for piece, needed in zip(parts, needed_bits):
            if bit_index < needed:
                other = received[counter]
                counter = counter + 1
                piece = jnp.where(
                    upper,
                    jnp.concatenate([other, piece], axis=axis),
                    jnp.concatenate([piece, other], axis=axis),
                )
            joined.append(piece)
        parts = joined
    return parts


def project(normed, query_rows, key_rows, value_rows, output_rows):
    query_full, key_full, value_full, output_full = (
        lax.all_gather(query_rows, "pair", axis=1, tiled=True),
        lax.all_gather(key_rows, "pair", axis=1, tiled=True),
        lax.all_gather(value_rows, "pair", axis=1, tiled=True),
        lax.all_gather(output_rows, "pair", axis=1, tiled=True),
    )
    query_pre = contract(normed, query_full)
    key_pre = contract(normed, key_full)
    value_pre = contract(normed, value_full)
    return (query_pre, key_pre, value_pre, output_full)


def general_body(hidden_in, norm_gain, query_weight, key_weight, value_weight, output_weight, lengths):
    tp_count = lax.axis_size("tp")
    device = lax.axis_index("tp")
    query_bits = bit_count(max(1, tp_count // HQ))
    group_bits = bit_count(max(1, tp_count // KVH))
    needed_bits = [query_bits, group_bits, group_bits]
    query_cols = query_weight.shape[0]
    stretches = lengths.shape[0]
    request, position = token_layout(lengths)
    position = position.reshape(-1)
    full_rows = lax.all_gather(hidden_in, "tp", axis=1, tiled=True)
    stream = full_rows.astype(jnp.float32)
    mean_square = jnp.mean(stream * stream, axis=1, keepdims=True)
    normed = (stream * lax.rsqrt(mean_square + 1e-05) * norm_gain[None, :]).astype(jnp.bfloat16)
    query_block, key_block, value_block = assemble(
        [query_weight, key_weight, value_weight], needed_bits, device, 0
    )
    query_pre, key_pre, value_pre, output_full = project(
        normed, query_block, key_block, value_block, output_weight
    )
    query_dims = jnp.arange(query_pre.shape[1], dtype=jnp.int32) % HD
    key_dims = jnp.arange(key_pre.shape[1], dtype=jnp.int32) % HD
    query = rotary(query_pre, position, query_dims).astype(jnp.bfloat16)
    key = rotary(key_pre, position, key_dims).astype(jnp.bfloat16)
    value = value_pre.astype(jnp.bfloat16)
    heads = query.shape[1] // HD
    groups = key.shape[1] // HD
    attended = attend(query, key, value, request, stretches, heads, groups)
    own_start = device * query_cols % (heads * HD)
    own_columns = lax.dynamic_slice_in_dim(attended, own_start, query_cols, 1)
    projected = contract(lax.all_gather(own_columns, "tp", axis=1, tiled=True), output_full)
    return (hidden_in.astype(jnp.float32) + projected).astype(jnp.bfloat16)


RING = 8
ROWS = STRETCH // 2
UNIT = 1024
ORDER = (0, 1, -1, -2, 2, 3, -3, -4)


def ring_place(t):
    return t // 2 if t % 2 == 0 else RING - 1 - t // 2


def ring_member(place):
    return 2 * place if place < RING // 2 else 2 * RING - 1 - 2 * place


def ring_swap(later):
    pairs = []
    for t in range(RING):
        for p in range(2):
            place = ring_place(t)
            step = 1 if (place + p + later) % 2 == 0 else -1
            pairs.append((t * 2 + p, ring_member((place + step) % RING) * 2 + p))
    return pairs


def swapped(shard, later):
    return lax.ppermute(shard, ("tp", "pair"), ring_swap(later))


def unit_of(index):
    t = lax.axis_index("tp")
    place = jnp.where(t % 2 == 0, t // 2, RING - 1 - t // 2)
    step = 1 - 2 * ((place + lax.axis_index("pair")) % 2)
    offset = jnp.int32(ORDER[0])
    for k in range(1, len(ORDER)):
        offset = jnp.where(index == k, ORDER[k], offset)
    where = (place + offset * step + RING) % RING
    return jnp.where(where < RING // 2, 2 * where, 2 * RING - 1 - 2 * where)


def columns_of(index):
    t = unit_of(index)
    mine = t // (RING // 2) == lax.axis_index("pair")
    return mine, pl.ds(pl.multiple_of(t % (RING // 2) * UNIT, UNIT), UNIT)


def add_units(xs, acc, own, others, first, count):
    def unit_step(u, carry):
        mine, cols = columns_of(first + u)
        for here, parts in ((mine, own), (jnp.logical_not(mine), others)):

            @pl.when(here)
            def _(parts=parts):
                at = 0
                for part in parts:
                    rows = part.shape[0]
                    acc[:, at : at + rows] += contract(xs[u], part[:, cols])
                    at += rows

        return carry

    lax.fori_loop(0, count, unit_step, 0)


def load_kernel(spans, *refs):
    *sources, target, sems = refs
    copies = []
    at = 0
    for n, (source, (start, rows)) in enumerate(zip(sources, spans)):
        where = target.at[pl.ds(at, rows), :]
        copies.append(pltpu.make_async_copy(source.at[pl.ds(start, rows), :], where, sems.at[n]))
        at += rows
    for copy in copies:
        copy.start()
    for copy in copies:
        copy.wait()


def normed_unit(part, factor, gain_ref, index):
    base = unit_of(index) * (UNIT // 128)
    stream = part.astype(jnp.float32)
    lanes = []
    for k in range(UNIT // 128):
        gain = gain_ref[pl.ds(base + k, 1), :]
        lanes.append((stream[:, k * 128 : (k + 1) * 128] * factor * gain).astype(jnp.bfloat16))
    return lanes


def place_unit(xs, rows, n, part, factor, gain, index):
    for k, lane in enumerate(normed_unit(part, factor, gain, index)):
        xs[n, rows, k * 128 : (k + 1) * 128] = lane


VM = pl.BlockSpec(memory_space=pltpu.VMEM)
HBM = pl.BlockSpec(memory_space=pl.ANY)
SM = pl.BlockSpec(memory_space=pltpu.SMEM)


def params(mib):
    return pltpu.CompilerParams(vmem_limit_bytes=mib * 2**20)


def cost(rows, units, width):
    return pl.CostEstimate(
        flops=2 * rows * units * UNIT * width,
        bytes_accessed=2 * units * UNIT * width + 4 * rows * width,
        transcendentals=0,
    )


def stream_rows(s):
    return slice(s * ROWS, (s + 1) * ROWS)


def normed_units(xs, gain, factor, first, *streams):
    for s, units in enumerate(streams):
        for n, unit in enumerate(units):
            place_unit(xs, stream_rows(s), n, unit[...], factor[stream_rows(s), :], gain, first + n)


def early_kernel(a0, a1, a2, a3, b0, b1, b2, b3, gain, factor, *refs):
    *weights, acc, xs = refs
    normed_units(xs, gain, factor, 0, (a0, a1, a2, a3), (b0, b1, b2, b3))
    acc[...] = jnp.zeros_like(acc)
    add_units(xs, acc, weights[:2], weights[2:], 0, 4)


def middle_kernel(a4, a5, b4, b5, gain, factor, acc_in, *refs):
    *weights, acc, xs = refs
    normed_units(xs, gain, factor, 4, (a4, a5), (b4, b5))
    acc[...] = acc_in[...]
    add_units(xs, acc, weights[:2], weights[2:], 4, 2)


def project_first_kernel(a6, a7, b6, gain, factor, acc_in, *refs):
    *weights, first, second, acc, xs, late = refs
    normed_units(xs, gain, factor, 6, (a6,), (b6,))
    normed_units(late, gain, factor, 7, (a7,))
    acc[...] = acc_in[...]
    add_units(xs, acc, weights[:2], weights[2:], 6, 1)
    first[...] = acc[:ROWS, :]
    second[...] = acc[ROWS:, :]
    add_units(late, first, weights[:2], weights[2:], 7, 1)


def project_second_kernel(b7, gain, factor, acc_in, *refs):
    *weights, acc, late = refs
    place_unit(late, slice(0, ROWS), 0, b7[...], factor[ROWS:, :], gain, 7)
    acc[...] = acc_in[...]
    add_units(late, acc, weights[:2], weights[2:], 7, 1)


def turned_heads(part, cosine, sine):
    lane = lax.broadcasted_iota(jnp.int32, part.shape, 1)
    other = jnp.where(lane % 2 == 0, pltpu.roll(part, HD - 1, 1), pltpu.roll(part, 1, 1))
    return (part * cosine + other * sine).astype(jnp.bfloat16)


def attend_kernel(half, lens, acc, cosine, sine, *refs):
    if half:
        key_early, value_early = refs[:2]
    attended, key_out, value_out = refs[-3:]
    rows = stream_rows(half)
    heads = UNIT // HD
    cos, sin = cosine[rows, :], sine[rows, :]
    key = turned_heads(acc[:, UNIT : UNIT + HD], cos, sin)
    value = acc[:, UNIT + HD :].astype(jnp.bfloat16)
    key_out[...] = key
    value_out[...] = value
    if half:
        key = jnp.concatenate([key_early[...], key], axis=0)
        value = jnp.concatenate([value_early[...], value], axis=0)
    shape = (ROWS, (half + 1) * ROWS)
    row = lax.broadcasted_iota(jnp.int32, shape, 0) + half * ROWS
    col = lax.broadcasted_iota(jnp.int32, shape, 1)
    row_request = jnp.zeros(shape, jnp.int32)
    col_request = jnp.zeros(shape, jnp.int32)
    end = jnp.int32(0)
    for k in range(lens.shape[1]):
        end = end + lens[0, k]
        row_request += (row >= end).astype(jnp.int32)
        col_request += (col >= end).astype(jnp.int32)
    keep = (row_request == col_request) & (row >= col)
    queries = [turned_heads(acc[:, h * HD : (h + 1) * HD], cos, sin) for h in range(heads)]
    scores = contract(jnp.concatenate(queries, axis=0), key) * (1.0 / math.sqrt(HD))
    scores = jnp.where(keep[None], scores.reshape(heads, *shape), -1e30)
    weights = jnp.exp(scores - jnp.max(scores, axis=2, keepdims=True))
    probs = (weights / jnp.sum(weights, axis=2, keepdims=True)).astype(jnp.bfloat16)
    probs = probs.reshape(heads * ROWS, shape[1])
    out = jnp.dot(probs, value, preferred_element_type=jnp.float32).astype(jnp.bfloat16)
    for h in range(heads):
        attended[:, h * HD : (h + 1) * HD] = out[h * ROWS : (h + 1) * ROWS, :]


def stream_units(xs, *streams):
    for s, units in enumerate(streams):
        for n, unit in enumerate(units):
            xs[n, stream_rows(s), :] = unit[...]


def out_early_kernel(a0, a1, a2, a3, b0, b1, b2, b3, w0, w1, acc, xs):
    stream_units(xs, (a0, a1, a2, a3), (b0, b1, b2, b3))
    acc[...] = jnp.zeros_like(acc)
    add_units(xs, acc, (w0,), (w1,), 0, 4)


def out_middle_kernel(a4, a5, b4, b5, acc_in, hidden, w0, w1, acc, xs):
    stream_units(xs, (a4, a5), (b4, b5))
    acc[...] = acc_in[...] + hidden[...].astype(jnp.float32)
    add_units(xs, acc, (w0,), (w1,), 4, 2)


def out_first_kernel(a6, a7, b6, acc_in, w0, w1, out, second, acc, first, xs, late):
    stream_units(xs, (a6,), (b6,))
    stream_units(late, (a7,))
    acc[...] = acc_in[...]
    add_units(xs, acc, (w0,), (w1,), 6, 1)
    first[...] = acc[:ROWS, :]
    second[...] = acc[ROWS:, :]
    add_units(late, first, (w0,), (w1,), 7, 1)
    out[...] = first[...].astype(jnp.bfloat16)


def out_second_kernel(b7, acc_in, w0, w1, partial, out, acc, late):
    stream_units(late, (b7,))
    acc[...] = acc_in[...]
    add_units(late, acc, (w0,), (w1,), 7, 1)
    out[...] = acc[...].astype(jnp.bfloat16)


def summed_over_tp(value):
    for bits in ((1, 2), (2, 1), (4, 4)):
        pairs = [(t * 2 + p, (t ^ bits[p]) * 2 + p) for t in range(RING) for p in range(2)]
        value = value + lax.ppermute(value, ("tp", "pair"), pairs)
    return value


def kernel_call(kernel, **options):
    return pl.pallas_call(kernel, **options)


def in_vmem(value):
    return pltpu.with_memory_space_constraint(value, pltpu.VMEM)


def load(arrays, spans):
    rows = sum(span for _, span in spans)
    return kernel_call(
        lambda *refs: load_kernel(spans, *refs),
        out_shape=jax.ShapeDtypeStruct((rows, arrays[0].shape[1]), arrays[0].dtype),
        in_specs=[HBM] * len(arrays),
        out_specs=VM,
        scratch_shapes=[pltpu.SemaphoreType.DMA((len(arrays),))],
        compiler_params=params(2),
        cost_estimate=cost(0, rows * arrays[0].shape[1] // UNIT, 1),
    )(*(pltpu.with_memory_space_constraint(w, pltpu.HBM) for w in arrays))


def token_position(lengths):
    count = lengths.shape[0]
    upto = jnp.arange(count)[:, None] >= jnp.arange(count)[None, :]
    ends = jnp.sum(jnp.where(upto, lengths[None, :], 0), axis=1)
    offsets = jnp.arange(STRETCH, dtype=jnp.int32)
    finished = ends[None, :] <= offsets[:, None]
    return offsets - jnp.sum(jnp.where(finished, lengths[None, :], 0), axis=1)


def after(value, *others):
    return lax.optimization_barrier((value, *others))


def ring_body(*args):
    return ring_layer(*args)


def ring_layer(hidden_in, norm_gain, query_weight, key_weight, value_weight, output_weight, lengths):
    f32, bf16 = jnp.float32, jnp.bfloat16
    a0, b0 = hidden_in[:ROWS], hidden_in[ROWS:]
    a1, b1 = swapped(a0, 0), swapped(b0, 0)
    a2, b2 = swapped(a0, 1), swapped(b0, 1)
    projections = (query_weight, key_weight, value_weight)
    others = []
    for w in projections:
        others.append(in_vmem(partner(w, "pair", 0)))
    qkv = sum(w.shape[0] for w in projections)
    stream = hidden_in.astype(f32)
    squares = jnp.sum(stream * stream, axis=1).reshape(2, 128)
    squares = summed_over_tp(squares)
    factor = lax.rsqrt(squares / (RING * UNIT) + 1e-05)
    factor = jnp.broadcast_to(factor.reshape(STRETCH, 1), (STRETCH, 128))
    gain = norm_gain.reshape(RING * UNIT // 128, 128)
    position = token_position(lengths[0])
    lane = jnp.arange(HD, dtype=jnp.int32)
    angle = position.astype(f32)[:, None] * scaled_freq(lane - lane % 2)[None, :]
    cosine = jnp.cos(angle)
    sine = jnp.sin(angle) * jnp.where(lane % 2 == 0, -1.0, 1.0)[None, :]
    a3, b3 = swapped(a1, 1), swapped(b1, 1)
    a4, b4 = swapped(a2, 0), swapped(b2, 0)
    other_output = in_vmem(partner(output_weight, "pair", 0))
    cut = query_weight.shape[0] // 2
    own_first = load((query_weight,), ((0, cut),))
    own_second = load(
        projections,
        ((cut, query_weight.shape[0] - cut), (0, key_weight.shape[0]), (0, value_weight.shape[0])),
    )
    a3, own_first = after(a3, own_first)
    a4, own_second = after(a4, own_second)
    weights = (own_first, own_second, *others)
    a5, b5 = swapped(a3, 0), swapped(b3, 0)
    a6, b6 = swapped(a4, 1), swapped(b4, 1)
    factor, cosine, sine, lengths = after(factor, cosine, sine, lengths)
    acc_shape = jax.ShapeDtypeStruct((STRETCH, qkv), f32)
    acc = kernel_call(
        early_kernel,
        out_shape=acc_shape,
        in_specs=[VM] * 15,
        out_specs=VM,
        scratch_shapes=[pltpu.VMEM((4, STRETCH, UNIT), bf16)],
        compiler_params=params(10),
        cost_estimate=cost(STRETCH, 4, qkv),
    )(a0, a1, a2, a3, b0, b1, b2, b3, gain, factor, *weights)
    a5, acc = after(a5, acc)
    a7, b7 = swapped(a5, 1), swapped(b5, 1)
    acc = kernel_call(
        middle_kernel,
        out_shape=acc_shape,
        in_specs=[VM] * 12,
        out_specs=VM,
        scratch_shapes=[pltpu.VMEM((2, STRETCH, UNIT), bf16)],
        compiler_params=params(8),
        cost_estimate=cost(STRETCH, 2, qkv),
    )(a4, a5, b4, b5, gain, factor, acc, *weights)
    half_shape = jax.ShapeDtypeStruct((ROWS, qkv), f32)
    first, second = kernel_call(
        project_first_kernel,
        out_shape=(half_shape, half_shape),
        in_specs=[VM] * 11,
        out_specs=(VM, VM),
        scratch_shapes=[
            pltpu.VMEM((STRETCH, qkv), f32),
            pltpu.VMEM((1, STRETCH, UNIT), bf16),
            pltpu.VMEM((1, ROWS, UNIT), bf16),
        ],
        compiler_params=params(8),
        cost_estimate=cost(STRETCH, 2, qkv),
    )(a6, a7, b6, gain, factor, acc, *weights)

    def attend_stream(half, projected, early):
        kv = jax.ShapeDtypeStruct((ROWS, HD), bf16)
        return kernel_call(
            lambda *refs: attend_kernel(half, *refs),
            out_shape=(jax.ShapeDtypeStruct((ROWS, UNIT), bf16), kv, kv),
            in_specs=[SM] + [VM] * (3 + len(early)),
            out_specs=(VM, VM, VM),
            compiler_params=params(8),
            cost_estimate=cost(ROWS, 2, qkv),
        )(lengths, projected, cosine, sine, *early)

    a0, key_a, value_a = attend_stream(0, first, ())
    a1, a2 = swapped(a0, 0), swapped(a0, 1)
    projected = kernel_call(
        project_second_kernel,
        out_shape=half_shape,
        in_specs=[VM] * 9,
        out_specs=VM,
        scratch_shapes=[pltpu.VMEM((1, ROWS, UNIT), bf16)],
        compiler_params=params(10),
        cost_estimate=cost(ROWS, 1, qkv),
    )(b7, gain, factor, second, *weights)
    a1, projected = after(a1, projected)
    a3 = swapped(a1, 1)
    b0, _, _ = attend_stream(1, projected, (key_a, value_a))
    b1, b2 = swapped(b0, 0), swapped(b0, 1)
    a4, b3 = swapped(a2, 0), swapped(b1, 1)
    a5, b4 = swapped(a3, 0), swapped(b2, 0)
    a6, b5 = swapped(a4, 1), swapped(b3, 0)
    width = output_weight.shape[0]
    acc_shape = jax.ShapeDtypeStruct((STRETCH, width), f32)
    acc = kernel_call(
        out_early_kernel,
        out_shape=acc_shape,
        in_specs=[VM] * 10,
        out_specs=VM,
        scratch_shapes=[pltpu.VMEM((4, STRETCH, UNIT), bf16)],
        compiler_params=params(10),
        cost_estimate=cost(STRETCH, 4, width),
    )(a0, a1, a2, a3, b0, b1, b2, b3, output_weight, other_output)
    a5, acc = after(a5, acc)
    a7, b6, b7 = swapped(a5, 1), swapped(b4, 1), swapped(b5, 1)
    acc = kernel_call(
        out_middle_kernel,
        out_shape=acc_shape,
        in_specs=[VM] * 8,
        out_specs=VM,
        scratch_shapes=[pltpu.VMEM((2, STRETCH, UNIT), bf16)],
        compiler_params=params(8),
        cost_estimate=cost(STRETCH, 2, width),
    )(a4, a5, b4, b5, acc, hidden_in, output_weight, other_output)

    out_shape = jax.ShapeDtypeStruct((STRETCH, UNIT), bf16)
    half_shape = jax.ShapeDtypeStruct((ROWS, width), f32)
    half = pltpu.VMEM((ROWS, width), f32)
    late = pltpu.VMEM((1, ROWS, UNIT), bf16)
    out, acc = kernel_call(
        out_first_kernel,
        grid=(1,),
        out_shape=(out_shape, half_shape),
        in_specs=[VM] * 6,
        out_specs=(pl.BlockSpec((ROWS, UNIT), lambda i: (0, 0)), VM),
        scratch_shapes=[
            pltpu.VMEM((STRETCH, width), f32),
            half,
            pltpu.VMEM((1, STRETCH, UNIT), bf16),
            late,
        ],
        compiler_params=params(8),
        cost_estimate=cost(STRETCH, 2, width),
    )(a6, a7, b6, acc, output_weight, other_output)
    return kernel_call(
        out_second_kernel,
        grid=(1,),
        out_shape=out_shape,
        in_specs=[VM] * 4 + [HBM],
        out_specs=pl.BlockSpec((ROWS, UNIT), lambda i: (1, 0)),
        scratch_shapes=[half, late],
        input_output_aliases={4: 0},
        compiler_params=params(8),
        cost_estimate=cost(ROWS, 1, width),
    )(b7, acc, output_weight, other_output, out)


def fits_ring(mesh):
    return dict(mesh.shape)["tp"] == RING and dict(mesh.shape)["pair"] == 2


def solution(mesh):
    placed = (
        P(("group", "pair"), "tp"),
        P(),
        P("tp", "pair"),
        P("tp", "pair"),
        P("tp", "pair"),
        P("tp", "pair"),
        P(("group", "pair"), None),
    )
    body = ring_body if fits_ring(mesh) else general_body
    step = jax.shard_map(
        body, mesh=mesh, in_specs=placed, out_specs=P(("group", "pair"), "tp"), check_vma=False
    )
    if not fits_ring(mesh):
        return step
    return step
```

```python
import math

import jax
import jax.numpy as jnp
from jax import lax
from jax.experimental import pallas as pl
from jax.experimental.pallas import tpu as pltpu

from jax.sharding import PartitionSpec as P

HQ = 64
KVH = 8
HD = 128
STRETCH = 256


THETA = 500000.0


def shortened(shard):

    def short(part):
        return part.astype(jnp.bfloat16) if part.dtype == jnp.float32 else part

    return jax.tree.map(short, shard)


def partner(shard, axis, apart):
    return lax.ppermute(shard, axis, [(i, i ^ 1 << apart) for i in range(lax.axis_size(axis))])


def token_layout(lengths):
    ends = jnp.cumsum(lengths, axis=1)
    offsets = jnp.arange(STRETCH, dtype=jnp.int32)
    finished = ends[:, None, :] <= offsets[None, :, None]
    request = jnp.sum(finished.astype(jnp.int32), axis=2)
    position = offsets[None, :] - jnp.sum(jnp.where(finished, lengths[:, None, :], 0), axis=2)
    return (request, position)


def scaled_freq(dims):
    freq = jnp.exp(dims.astype(jnp.float32) * (-math.log(THETA) / HD))
    wavelen = 2.0 * math.pi / freq
    smooth = (8192.0 / wavelen - 1.0) / 3.0
    middle = (1.0 - smooth) * freq / 8.0 + smooth * freq
    return jnp.where(wavelen < 2048.0, freq, jnp.where(wavelen > 8192.0, freq / 8.0, middle))


def rotary(projected, position, dims):
    freq = scaled_freq(dims[0::2])
    angle = position.astype(jnp.float32)[:, None] * freq[None, :]
    cosine = jnp.cos(angle)
    sine = jnp.sin(angle)
    first = projected[:, 0::2]
    second = projected[:, 1::2]
    turned = jnp.stack([first * cosine - second * sine, first * sine + second * cosine], axis=-1)
    return turned.reshape(projected.shape)


def attend(query, key, value, request, stretches, heads, groups):
    repeat = heads // groups
    query_blocks = query.reshape(stretches, STRETCH, groups, repeat, HD)
    key_blocks = key.reshape(stretches, STRETCH, groups, HD)
    value_blocks = value.reshape(stretches, STRETCH, groups, HD)
    scores = jnp.einsum(
        "cqgrd,ckgd->cgrqk", query_blocks, key_blocks, preferred_element_type=jnp.float32
    ) * (1.0 / math.sqrt(HD))
    offsets = jnp.arange(STRETCH, dtype=jnp.int32)
    keep = (request[:, :, None] == request[:, None, :]) & (offsets[:, None] >= offsets[None, :])[
        None
    ]
    scores = jnp.where(keep[:, None, None], scores, -1e30)
    top = jnp.max(scores, axis=-1, keepdims=True)
    weights = jnp.exp(scores - top)
    probs = (weights / jnp.sum(weights, axis=-1, keepdims=True)).astype(jnp.bfloat16)
    attended = jnp.einsum(
        "cgrqk,ckgd->cqgrd", probs, value_blocks, preferred_element_type=jnp.float32
    )
    return attended.reshape(stretches * STRETCH, heads * HD).astype(jnp.bfloat16)


def contract(left, right):
    return lax.dot_general(
        left, right, (((1,), (1,)), ((), ())), preferred_element_type=jnp.float32
    )


def bit_count(number):
    return number.bit_length() - 1


def assemble(parts, needed_bits, device, axis):
    for bit_index in range(max(needed_bits)):
        moving = [piece for piece, needed in zip(parts, needed_bits) if bit_index < needed]
        widths = [piece.shape[axis] for piece in moving]
        sent = jnp.concatenate(moving, axis=axis)
        arrived = partner(shortened(sent), "tp", bit_index).astype(sent.dtype)
        upper = device // 2**bit_index % 2 == 1
        cuts = []
        running = 0
        for width in widths[:-1]:
            running = running + width
            cuts.append(running)
        received = jnp.split(arrived, cuts, axis=axis)
        joined = []
        counter = 0
        for piece, needed in zip(parts, needed_bits):
            if bit_index < needed:
                other = received[counter]
                counter = counter + 1
                piece = jnp.where(
                    upper,
                    jnp.concatenate([other, piece], axis=axis),
                    jnp.concatenate([piece, other], axis=axis),
                )
            joined.append(piece)
        parts = joined
    return parts


def project(normed, query_rows, key_rows, value_rows, output_rows):
    query_full, key_full, value_full, output_full = (
        lax.all_gather(query_rows, "pair", axis=1, tiled=True),
        lax.all_gather(key_rows, "pair", axis=1, tiled=True),
        lax.all_gather(value_rows, "pair", axis=1, tiled=True),
        lax.all_gather(output_rows, "pair", axis=1, tiled=True),
    )
    query_pre = contract(normed, query_full)
    key_pre = contract(normed, key_full)
    value_pre = contract(normed, value_full)
    return (query_pre, key_pre, value_pre, output_full)


def general_body(hidden_in, norm_gain, query_weight, key_weight, value_weight, output_weight, lengths):
    tp_count = lax.axis_size("tp")
    device = lax.axis_index("tp")
    query_bits = bit_count(max(1, tp_count // HQ))
    group_bits = bit_count(max(1, tp_count // KVH))
    needed_bits = [query_bits, group_bits, group_bits]
    query_cols = query_weight.shape[0]
    stretches = lengths.shape[0]
    request, position = token_layout(lengths)
    position = position.reshape(-1)
    full_rows = lax.all_gather(hidden_in, "tp", axis=1, tiled=True)
    stream = full_rows.astype(jnp.float32)
    mean_square = jnp.mean(stream * stream, axis=1, keepdims=True)
    normed = (stream * lax.rsqrt(mean_square + 1e-05) * norm_gain[None, :]).astype(jnp.bfloat16)
    query_block, key_block, value_block = assemble(
        [query_weight, key_weight, value_weight], needed_bits, device, 0
    )
    query_pre, key_pre, value_pre, output_full = project(
        normed, query_block, key_block, value_block, output_weight
    )
    query_dims = jnp.arange(query_pre.shape[1], dtype=jnp.int32) % HD
    key_dims = jnp.arange(key_pre.shape[1], dtype=jnp.int32) % HD
    query = rotary(query_pre, position, query_dims).astype(jnp.bfloat16)
    key = rotary(key_pre, position, key_dims).astype(jnp.bfloat16)
    value = value_pre.astype(jnp.bfloat16)
    heads = query.shape[1] // HD
    groups = key.shape[1] // HD
    attended = attend(query, key, value, request, stretches, heads, groups)
    own_start = device * query_cols % (heads * HD)
    own_columns = lax.dynamic_slice_in_dim(attended, own_start, query_cols, 1)
    projected = contract(lax.all_gather(own_columns, "tp", axis=1, tiled=True), output_full)
    return (hidden_in.astype(jnp.float32) + projected).astype(jnp.bfloat16)


RING = 8
ROWS = STRETCH // 2
UNIT = 1024
ORDER = (0, 1, -1, -2, 2, 3, -3, -4)


def ring_place(t):
    return t // 2 if t % 2 == 0 else RING - 1 - t // 2


def ring_member(place):
    return 2 * place if place < RING // 2 else 2 * RING - 1 - 2 * place


def ring_swap(later):
    pairs = []
    for t in range(RING):
        for p in range(2):
            place = ring_place(t)
            step = 1 if (place + p + later) % 2 == 0 else -1
            pairs.append((t * 2 + p, ring_member((place + step) % RING) * 2 + p))
    return pairs


def swapped(shard, later):
    return lax.ppermute(shard, ("tp", "pair"), ring_swap(later))


def unit_of(index):
    t = lax.axis_index("tp")
    place = jnp.where(t % 2 == 0, t // 2, RING - 1 - t // 2)
    step = 1 - 2 * ((place + lax.axis_index("pair")) % 2)
    offset = jnp.int32(ORDER[0])
    for k in range(1, len(ORDER)):
        offset = jnp.where(index == k, ORDER[k], offset)
    where = (place + offset * step + RING) % RING
    return jnp.where(where < RING // 2, 2 * where, 2 * RING - 1 - 2 * where)


def columns_of(index):
    t = unit_of(index)
    mine = t // (RING // 2) == lax.axis_index("pair")
    return mine, pl.ds(pl.multiple_of(t % (RING // 2) * UNIT, UNIT), UNIT)


def add_units(xs, acc, own, others, first, count, ready=None):
    def unit_step(u, carry):
        mine, cols = columns_of(first + u)
        for here, parts in ((mine, own), (jnp.logical_not(mine), others)):

            @pl.when(here)
            def _(parts=parts):
                if ready is not None and parts is own:
                    ready(first + u)
                at = 0
                for part in parts:
                    rows = part.shape[0]
                    acc[:, at : at + rows] += contract(xs[u], part[:, cols])
                    at += rows

        return carry

    lax.fori_loop(0, count, unit_step, 0)


def fetch_unit(moves, sems, index, go):
    _, cols = columns_of(index)
    for n, (source, target) in enumerate(moves):
        copy = pltpu.make_async_copy(source.at[:, cols], target.at[:, cols], sems.at[n, index])
        copy.start() if go else copy.wait()


def each_own_unit(first, count, action):
    def unit_step(u, carry):
        mine, _ = columns_of(u)

        @pl.when(mine)
        def _():
            action(u)

        return carry

    lax.fori_loop(first, first + count, unit_step, 0)


def normed_unit(part, factor, gain_ref, index):
    base = unit_of(index) * (UNIT // 128)
    stream = part.astype(jnp.float32)
    lanes = []
    for k in range(UNIT // 128):
        gain = gain_ref[pl.ds(base + k, 1), :]
        lanes.append((stream[:, k * 128 : (k + 1) * 128] * factor * gain).astype(jnp.bfloat16))
    return lanes


def place_unit(xs, rows, n, part, factor, gain, index):
    for k, lane in enumerate(normed_unit(part, factor, gain, index)):
        xs[n, rows, k * 128 : (k + 1) * 128] = lane


VM = pl.BlockSpec(memory_space=pltpu.VMEM)
HBM = pl.BlockSpec(memory_space=pl.ANY)
SM = pl.BlockSpec(memory_space=pltpu.SMEM)


def params(mib):
    return pltpu.CompilerParams(vmem_limit_bytes=mib * 2**20)


def cost(rows, units, width):
    return pl.CostEstimate(
        flops=2 * rows * units * UNIT * width,
        bytes_accessed=2 * units * UNIT * width + 4 * rows * width,
        transcendentals=0,
    )


def stream_rows(s):
    return slice(s * ROWS, (s + 1) * ROWS)


def normed_units(xs, gain, factor, first, *streams):
    for s, units in enumerate(streams):
        for n, unit in enumerate(units):
            place_unit(xs, stream_rows(s), n, unit[...], factor[stream_rows(s), :], gain, first + n)


def early_kernel(a0, a1, a2, a3, b0, b1, b2, b3, gain, factor, *refs):
    query, key, value = refs[:3]
    others = refs[3:6]
    acc, top, bottom, both, xs, sems = refs[6:]
    rows, kv = top.shape[0], key.shape[0]
    moves = (
        (query.at[pl.ds(0, rows), :], top),
        (query.at[pl.ds(rows, rows), :], bottom),
        (key, both.at[pl.ds(0, kv), :]),
        (value, both.at[pl.ds(kv, kv), :]),
    )
    each_own_unit(0, RING, lambda u: fetch_unit(moves, sems, u, True))
    normed_units(xs, gain, factor, 0, (a0, a1, a2, a3), (b0, b1, b2, b3))
    acc[...] = jnp.zeros_like(acc)
    wait = lambda u: fetch_unit(moves, sems, u, False)
    add_units(xs, acc, (top, bottom, both), others, 0, 4, wait)
    each_own_unit(4, 4, wait)


def middle_kernel(a4, a5, b4, b5, gain, factor, acc_in, *refs):
    *weights, acc, xs = refs
    normed_units(xs, gain, factor, 4, (a4, a5), (b4, b5))
    acc[...] = acc_in[...]
    add_units(xs, acc, weights[:3], weights[3:], 4, 2)


def project_first_kernel(a6, a7, b6, gain, factor, acc_in, *refs):
    *weights, first, second, acc, xs, late = refs
    normed_units(xs, gain, factor, 6, (a6,), (b6,))
    normed_units(late, gain, factor, 7, (a7,))
    acc[...] = acc_in[...]
    add_units(xs, acc, weights[:3], weights[3:], 6, 1)
    first[...] = acc[:ROWS, :]
    second[...] = acc[ROWS:, :]
    add_units(late, first, weights[:3], weights[3:], 7, 1)


def project_second_kernel(b7, gain, factor, acc_in, *refs):
    *weights, acc, late = refs
    place_unit(late, slice(0, ROWS), 0, b7[...], factor[ROWS:, :], gain, 7)
    acc[...] = acc_in[...]
    add_units(late, acc, weights[:3], weights[3:], 7, 1)


def turned_heads(part, cosine, sine):
    lane = lax.broadcasted_iota(jnp.int32, part.shape, 1)
    other = jnp.where(lane % 2 == 0, pltpu.roll(part, HD - 1, 1), pltpu.roll(part, 1, 1))
    return (part * cosine + other * sine).astype(jnp.bfloat16)


def attend_kernel(half, lens, acc, cosine, sine, *refs):
    if half:
        key_early, value_early = refs[:2]
    attended, key_out, value_out = refs[-3:]
    rows = stream_rows(half)
    heads = UNIT // HD
    cos, sin = cosine[rows, :], sine[rows, :]
    key = turned_heads(acc[:, UNIT : UNIT + HD], cos, sin)
    value = acc[:, UNIT + HD :].astype(jnp.bfloat16)
    key_out[...] = key
    value_out[...] = value
    if half:
        key = jnp.concatenate([key_early[...], key], axis=0)
        value = jnp.concatenate([value_early[...], value], axis=0)
    shape = (ROWS, (half + 1) * ROWS)
    row = lax.broadcasted_iota(jnp.int32, shape, 0) + half * ROWS
    col = lax.broadcasted_iota(jnp.int32, shape, 1)
    row_request = jnp.zeros(shape, jnp.int32)
    col_request = jnp.zeros(shape, jnp.int32)
    end = jnp.int32(0)
    for k in range(lens.shape[1]):
        end = end + lens[0, k]
        row_request += (row >= end).astype(jnp.int32)
        col_request += (col >= end).astype(jnp.int32)
    keep = (row_request == col_request) & (row >= col)
    queries = [turned_heads(acc[:, h * HD : (h + 1) * HD], cos, sin) for h in range(heads)]
    scores = contract(jnp.concatenate(queries, axis=0), key) * (1.0 / math.sqrt(HD))
    scores = jnp.where(keep[None], scores.reshape(heads, *shape), -1e30)
    weights = jnp.exp(scores - jnp.max(scores, axis=2, keepdims=True))
    probs = (weights / jnp.sum(weights, axis=2, keepdims=True)).astype(jnp.bfloat16)
    probs = probs.reshape(heads * ROWS, shape[1])
    out = jnp.dot(probs, value, preferred_element_type=jnp.float32).astype(jnp.bfloat16)
    for h in range(heads):
        attended[:, h * HD : (h + 1) * HD] = out[h * ROWS : (h + 1) * ROWS, :]


def stream_units(xs, *streams):
    for s, units in enumerate(streams):
        for n, unit in enumerate(units):
            xs[n, stream_rows(s), :] = unit[...]


def out_early_kernel(a0, a1, a2, a3, b0, b1, b2, b3, w0, w1, acc, xs):
    stream_units(xs, (a0, a1, a2, a3), (b0, b1, b2, b3))
    acc[...] = jnp.zeros_like(acc)
    add_units(xs, acc, (w0,), (w1,), 0, 4)


def out_middle_kernel(a4, a5, b4, b5, acc_in, hidden, w0, w1, acc, xs):
    stream_units(xs, (a4, a5), (b4, b5))
    acc[...] = acc_in[...] + hidden[...].astype(jnp.float32)
    add_units(xs, acc, (w0,), (w1,), 4, 2)


def out_first_kernel(a6, a7, b6, acc_in, w0, w1, out, second, acc, first, xs, late):
    stream_units(xs, (a6,), (b6,))
    stream_units(late, (a7,))
    acc[...] = acc_in[...]
    add_units(xs, acc, (w0,), (w1,), 6, 1)
    first[...] = acc[:ROWS, :]
    second[...] = acc[ROWS:, :]
    add_units(late, first, (w0,), (w1,), 7, 1)
    out[...] = first[...].astype(jnp.bfloat16)


def out_second_kernel(b7, acc_in, w0, w1, partial, out, acc, late):
    stream_units(late, (b7,))
    acc[...] = acc_in[...]
    add_units(late, acc, (w0,), (w1,), 7, 1)
    out[...] = acc[...].astype(jnp.bfloat16)


def summed_over_tp(value):
    for bits in ((1, 2), (2, 1), (4, 4)):
        pairs = [(t * 2 + p, (t ^ bits[p]) * 2 + p) for t in range(RING) for p in range(2)]
        value = value + lax.ppermute(value, ("tp", "pair"), pairs)
    return value


def kernel_call(kernel, **options):
    return pl.pallas_call(kernel, **options)


def in_vmem(value):
    return pltpu.with_memory_space_constraint(value, pltpu.VMEM)


def in_hbm(value):
    return pltpu.with_memory_space_constraint(value, pltpu.HBM)


def angle_kernel(lens, freq, angle):
    place = lax.broadcasted_iota(jnp.int32, angle.shape, 0)
    position = place
    end = jnp.int32(0)
    for k in range(lens.shape[1]):
        end = end + lens[0, k]
        position = position - jnp.where(end <= place, lens[0, k], 0)
    angle[...] = position.astype(jnp.float32) * freq[...]


def after(value, *others):
    return lax.optimization_barrier((value, *others))


def ring_body(*args):
    return ring_layer(*args)


def ring_layer(hidden_in, norm_gain, query_weight, key_weight, value_weight, output_weight, lengths):
    f32, bf16 = jnp.float32, jnp.bfloat16
    a0, b0 = hidden_in[:ROWS], hidden_in[ROWS:]
    a1, b1 = swapped(a0, 0), swapped(b0, 0)
    a2, b2 = swapped(a0, 1), swapped(b0, 1)
    projections = (query_weight, key_weight, value_weight)
    others = []
    for w in projections:
        others.append(in_vmem(partner(w, "pair", 0)))
    qkv = sum(w.shape[0] for w in projections)
    stream = hidden_in.astype(f32)
    squares = jnp.sum(stream * stream, axis=1).reshape(2, 128)
    squares = summed_over_tp(squares)
    factor = lax.rsqrt(squares / (RING * UNIT) + 1e-05)
    factor = jnp.broadcast_to(factor.reshape(STRETCH, 1), (STRETCH, 128))
    gain = norm_gain.reshape(RING * UNIT // 128, 128)
    lane = jnp.arange(HD, dtype=jnp.int32)
    angle = kernel_call(
        angle_kernel,
        out_shape=jax.ShapeDtypeStruct((STRETCH, HD), f32),
        in_specs=[SM, VM],
        out_specs=VM,
        compiler_params=params(2),
    )(lengths, scaled_freq(lane - lane % 2)[None, :])
    cosine = jnp.cos(angle)
    sine = jnp.sin(angle) * jnp.where(lane % 2 == 0, -1.0, 1.0)[None, :]
    a3, b3 = swapped(a1, 1), swapped(b1, 1)
    a4, b4 = swapped(a2, 0), swapped(b2, 0)
    other_output = in_vmem(partner(output_weight, "pair", 0))
    a5, b5 = swapped(a3, 0), swapped(b3, 0)
    a6, b6 = swapped(a4, 1), swapped(b4, 1)
    factor, cosine, sine, lengths = after(factor, cosine, sine, lengths)
    acc_shape = jax.ShapeDtypeStruct((STRETCH, qkv), f32)
    columns = query_weight.shape[1]
    half_query = jax.ShapeDtypeStruct((query_weight.shape[0] // 2, columns), bf16)
    both = jax.ShapeDtypeStruct((qkv - query_weight.shape[0], columns), bf16)
    acc, *own = kernel_call(
        early_kernel,
        out_shape=(acc_shape, half_query, half_query, both),
        in_specs=[VM] * 10 + [HBM] * 3 + [VM] * 3,
        out_specs=(VM,) * 4,
        scratch_shapes=[
            pltpu.VMEM((4, STRETCH, UNIT), bf16),
            pltpu.SemaphoreType.DMA((4, RING)),
        ],
        compiler_params=params(10),
        cost_estimate=cost(STRETCH, 4, qkv),
    )(
        *(a0, a1, a2, a3, b0, b1, b2, b3, gain, factor),
        *(in_hbm(w) for w in projections),
        *others,
    )
    weights = (*own, *others)
    a5, acc = after(a5, acc)
    a7, b7 = swapped(a5, 1), swapped(b5, 1)
    acc = kernel_call(
        middle_kernel,
        out_shape=acc_shape,
        in_specs=[VM] * 13,
        out_specs=VM,
        scratch_shapes=[pltpu.VMEM((2, STRETCH, UNIT), bf16)],
        compiler_params=params(8),
        cost_estimate=cost(STRETCH, 2, qkv),
    )(a4, a5, b4, b5, gain, factor, acc, *weights)
    half_shape = jax.ShapeDtypeStruct((ROWS, qkv), f32)
    first, second = kernel_call(
        project_first_kernel,
        out_shape=(half_shape, half_shape),
        in_specs=[VM] * 12,
        out_specs=(VM, VM),
        scratch_shapes=[
            pltpu.VMEM((STRETCH, qkv), f32),
            pltpu.VMEM((1, STRETCH, UNIT), bf16),
            pltpu.VMEM((1, ROWS, UNIT), bf16),
        ],
        compiler_params=params(8),
        cost_estimate=cost(STRETCH, 2, qkv),
    )(a6, a7, b6, gain, factor, acc, *weights)

    def attend_stream(half, projected, early):
        kv = jax.ShapeDtypeStruct((ROWS, HD), bf16)
        return kernel_call(
            lambda *refs: attend_kernel(half, *refs),
            out_shape=(jax.ShapeDtypeStruct((ROWS, UNIT), bf16), kv, kv),
            in_specs=[SM] + [VM] * (3 + len(early)),
            out_specs=(VM, VM, VM),
            compiler_params=params(8),
            cost_estimate=cost(ROWS, 2, qkv),
        )(lengths, projected, cosine, sine, *early)

    a0, key_a, value_a = attend_stream(0, first, ())
    a1, a2 = swapped(a0, 0), swapped(a0, 1)
    projected = kernel_call(
        project_second_kernel,
        out_shape=half_shape,
        in_specs=[VM] * 10,
        out_specs=VM,
        scratch_shapes=[pltpu.VMEM((1, ROWS, UNIT), bf16)],
        compiler_params=params(10),
        cost_estimate=cost(ROWS, 1, qkv),
    )(b7, gain, factor, second, *weights)
    a1, projected = after(a1, projected)
    a3 = swapped(a1, 1)
    b0, _, _ = attend_stream(1, projected, (key_a, value_a))
    b1, b2 = swapped(b0, 0), swapped(b0, 1)
    a4, b3 = swapped(a2, 0), swapped(b1, 1)
    a5, b4 = swapped(a3, 0), swapped(b2, 0)
    a6, b5 = swapped(a4, 1), swapped(b3, 0)
    width = output_weight.shape[0]
    acc_shape = jax.ShapeDtypeStruct((STRETCH, width), f32)
    acc = kernel_call(
        out_early_kernel,
        out_shape=acc_shape,
        in_specs=[VM] * 10,
        out_specs=VM,
        scratch_shapes=[pltpu.VMEM((4, STRETCH, UNIT), bf16)],
        compiler_params=params(10),
        cost_estimate=cost(STRETCH, 4, width),
    )(a0, a1, a2, a3, b0, b1, b2, b3, output_weight, other_output)
    a5, acc = after(a5, acc)
    a7, b6, b7 = swapped(a5, 1), swapped(b4, 1), swapped(b5, 1)
    acc = kernel_call(
        out_middle_kernel,
        out_shape=acc_shape,
        in_specs=[VM] * 8,
        out_specs=VM,
        scratch_shapes=[pltpu.VMEM((2, STRETCH, UNIT), bf16)],
        compiler_params=params(8),
        cost_estimate=cost(STRETCH, 2, width),
    )(a4, a5, b4, b5, acc, hidden_in, output_weight, other_output)

    out_shape = jax.ShapeDtypeStruct((STRETCH, UNIT), bf16)
    half_shape = jax.ShapeDtypeStruct((ROWS, width), f32)
    half = pltpu.VMEM((ROWS, width), f32)
    late = pltpu.VMEM((1, ROWS, UNIT), bf16)
    out, acc = kernel_call(
        out_first_kernel,
        grid=(1,),
        out_shape=(out_shape, half_shape),
        in_specs=[VM] * 6,
        out_specs=(pl.BlockSpec((ROWS, UNIT), lambda i: (0, 0)), VM),
        scratch_shapes=[
            pltpu.VMEM((STRETCH, width), f32),
            half,
            pltpu.VMEM((1, STRETCH, UNIT), bf16),
            late,
        ],
        compiler_params=params(8),
        cost_estimate=cost(STRETCH, 2, width),
    )(a6, a7, b6, acc, output_weight, other_output)
    return kernel_call(
        out_second_kernel,
        grid=(1,),
        out_shape=out_shape,
        in_specs=[VM] * 4 + [HBM],
        out_specs=pl.BlockSpec((ROWS, UNIT), lambda i: (1, 0)),
        scratch_shapes=[half, late],
        input_output_aliases={4: 0},
        compiler_params=params(8),
        cost_estimate=cost(ROWS, 1, width),
    )(b7, acc, output_weight, other_output, out)


def fits_ring(mesh):
    return dict(mesh.shape)["tp"] == RING and dict(mesh.shape)["pair"] == 2


def solution(mesh):
    placed = (
        P(("group", "pair"), "tp"),
        P(),
        P("tp", "pair"),
        P("tp", "pair"),
        P("tp", "pair"),
        P("tp", "pair"),
        P(("group", "pair"), None),
    )
    body = ring_body if fits_ring(mesh) else general_body
    step = jax.shard_map(
        body, mesh=mesh, in_specs=placed, out_specs=P(("group", "pair"), "tp"), check_vma=False
    )
    if not fits_ring(mesh):
        return step
    return step
```

```python
import math

import jax
import jax.numpy as jnp
from jax import lax
from jax.experimental import pallas as pl
from jax.experimental.pallas import tpu as pltpu

from jax.sharding import PartitionSpec as P

HQ = 64
KVH = 8
HD = 128
STRETCH = 256


THETA = 500000.0


def shortened(shard):

    def short(part):
        return part.astype(jnp.bfloat16) if part.dtype == jnp.float32 else part

    return jax.tree.map(short, shard)


def partner(shard, axis, apart):
    return lax.ppermute(shard, axis, [(i, i ^ 1 << apart) for i in range(lax.axis_size(axis))])


def token_layout(lengths):
    ends = jnp.cumsum(lengths, axis=1)
    offsets = jnp.arange(STRETCH, dtype=jnp.int32)
    finished = ends[:, None, :] <= offsets[None, :, None]
    request = jnp.sum(finished.astype(jnp.int32), axis=2)
    position = offsets[None, :] - jnp.sum(jnp.where(finished, lengths[:, None, :], 0), axis=2)
    return (request, position)


def scaled_freq(dims):
    freq = jnp.exp(dims.astype(jnp.float32) * (-math.log(THETA) / HD))
    wavelen = 2.0 * math.pi / freq
    smooth = (8192.0 / wavelen - 1.0) / 3.0
    middle = (1.0 - smooth) * freq / 8.0 + smooth * freq
    return jnp.where(wavelen < 2048.0, freq, jnp.where(wavelen > 8192.0, freq / 8.0, middle))


def rotary(projected, position, dims):
    freq = scaled_freq(dims[0::2])
    angle = position.astype(jnp.float32)[:, None] * freq[None, :]
    cosine = jnp.cos(angle)
    sine = jnp.sin(angle)
    first = projected[:, 0::2]
    second = projected[:, 1::2]
    turned = jnp.stack([first * cosine - second * sine, first * sine + second * cosine], axis=-1)
    return turned.reshape(projected.shape)


def attend(query, key, value, request, stretches, heads, groups):
    repeat = heads // groups
    query_blocks = query.reshape(stretches, STRETCH, groups, repeat, HD)
    key_blocks = key.reshape(stretches, STRETCH, groups, HD)
    value_blocks = value.reshape(stretches, STRETCH, groups, HD)
    scores = jnp.einsum(
        "cqgrd,ckgd->cgrqk", query_blocks, key_blocks, preferred_element_type=jnp.float32
    ) * (1.0 / math.sqrt(HD))
    offsets = jnp.arange(STRETCH, dtype=jnp.int32)
    keep = (request[:, :, None] == request[:, None, :]) & (offsets[:, None] >= offsets[None, :])[
        None
    ]
    scores = jnp.where(keep[:, None, None], scores, -1e30)
    top = jnp.max(scores, axis=-1, keepdims=True)
    weights = jnp.exp(scores - top)
    probs = (weights / jnp.sum(weights, axis=-1, keepdims=True)).astype(jnp.bfloat16)
    attended = jnp.einsum(
        "cgrqk,ckgd->cqgrd", probs, value_blocks, preferred_element_type=jnp.float32
    )
    return attended.reshape(stretches * STRETCH, heads * HD).astype(jnp.bfloat16)


def contract(left, right):
    return lax.dot_general(
        left, right, (((1,), (1,)), ((), ())), preferred_element_type=jnp.float32
    )


def bit_count(number):
    return number.bit_length() - 1


def assemble(parts, needed_bits, device, axis):
    for bit_index in range(max(needed_bits)):
        moving = [piece for piece, needed in zip(parts, needed_bits) if bit_index < needed]
        widths = [piece.shape[axis] for piece in moving]
        sent = jnp.concatenate(moving, axis=axis)
        arrived = partner(shortened(sent), "tp", bit_index).astype(sent.dtype)
        upper = device // 2**bit_index % 2 == 1
        cuts = []
        running = 0
        for width in widths[:-1]:
            running = running + width
            cuts.append(running)
        received = jnp.split(arrived, cuts, axis=axis)
        joined = []
        counter = 0
        for piece, needed in zip(parts, needed_bits):
            if bit_index < needed:
                other = received[counter]
                counter = counter + 1
                piece = jnp.where(
                    upper,
                    jnp.concatenate([other, piece], axis=axis),
                    jnp.concatenate([piece, other], axis=axis),
                )
            joined.append(piece)
        parts = joined
    return parts


def project(normed, query_rows, key_rows, value_rows, output_rows):
    query_full, key_full, value_full, output_full = (
        lax.all_gather(query_rows, "pair", axis=1, tiled=True),
        lax.all_gather(key_rows, "pair", axis=1, tiled=True),
        lax.all_gather(value_rows, "pair", axis=1, tiled=True),
        lax.all_gather(output_rows, "pair", axis=1, tiled=True),
    )
    query_pre = contract(normed, query_full)
    key_pre = contract(normed, key_full)
    value_pre = contract(normed, value_full)
    return (query_pre, key_pre, value_pre, output_full)


def general_body(hidden_in, norm_gain, query_weight, key_weight, value_weight, output_weight, lengths):
    tp_count = lax.axis_size("tp")
    device = lax.axis_index("tp")
    query_bits = bit_count(max(1, tp_count // HQ))
    group_bits = bit_count(max(1, tp_count // KVH))
    needed_bits = [query_bits, group_bits, group_bits]
    query_cols = query_weight.shape[0]
    stretches = lengths.shape[0]
    request, position = token_layout(lengths)
    position = position.reshape(-1)
    full_rows = lax.all_gather(hidden_in, "tp", axis=1, tiled=True)
    stream = full_rows.astype(jnp.float32)
    mean_square = jnp.mean(stream * stream, axis=1, keepdims=True)
    normed = (stream * lax.rsqrt(mean_square + 1e-05) * norm_gain[None, :]).astype(jnp.bfloat16)
    query_block, key_block, value_block = assemble(
        [query_weight, key_weight, value_weight], needed_bits, device, 0
    )
    query_pre, key_pre, value_pre, output_full = project(
        normed, query_block, key_block, value_block, output_weight
    )
    query_dims = jnp.arange(query_pre.shape[1], dtype=jnp.int32) % HD
    key_dims = jnp.arange(key_pre.shape[1], dtype=jnp.int32) % HD
    query = rotary(query_pre, position, query_dims).astype(jnp.bfloat16)
    key = rotary(key_pre, position, key_dims).astype(jnp.bfloat16)
    value = value_pre.astype(jnp.bfloat16)
    heads = query.shape[1] // HD
    groups = key.shape[1] // HD
    attended = attend(query, key, value, request, stretches, heads, groups)
    own_start = device * query_cols % (heads * HD)
    own_columns = lax.dynamic_slice_in_dim(attended, own_start, query_cols, 1)
    projected = contract(lax.all_gather(own_columns, "tp", axis=1, tiled=True), output_full)
    return (hidden_in.astype(jnp.float32) + projected).astype(jnp.bfloat16)


RING = 8
ROWS = STRETCH // 2
UNIT = 1024
ORDER = (0, 1, -1, -2, 2, 3, -3, -4)


def ring_place(t):
    return t // 2 if t % 2 == 0 else RING - 1 - t // 2


def ring_member(place):
    return 2 * place if place < RING // 2 else 2 * RING - 1 - 2 * place


def ring_swap(later):
    pairs = []
    for t in range(RING):
        for p in range(2):
            place = ring_place(t)
            step = 1 if (place + p + later) % 2 == 0 else -1
            pairs.append((t * 2 + p, ring_member((place + step) % RING) * 2 + p))
    return pairs


def swapped(shard, later):
    return lax.ppermute(shard, ("tp", "pair"), ring_swap(later))


def unit_of(index):
    t = lax.axis_index("tp")
    place = jnp.where(t % 2 == 0, t // 2, RING - 1 - t // 2)
    step = 1 - 2 * ((place + lax.axis_index("pair")) % 2)
    offset = jnp.int32(ORDER[0])
    for k in range(1, len(ORDER)):
        offset = jnp.where(index == k, ORDER[k], offset)
    where = (place + offset * step + RING) % RING
    return jnp.where(where < RING // 2, 2 * where, 2 * RING - 1 - 2 * where)


def columns_of(index):
    t = unit_of(index)
    mine = t // (RING // 2) == lax.axis_index("pair")
    return mine, pl.ds(pl.multiple_of(t % (RING // 2) * UNIT, UNIT), UNIT)


def add_units(xs, acc, own, others, first, count, ready=None):
    def unit_step(u, carry):
        mine, cols = columns_of(first + u)
        for here, parts in ((mine, own), (jnp.logical_not(mine), others)):

            @pl.when(here)
            def _(parts=parts):
                if ready is not None and parts is own:
                    ready(first + u)
                at = 0
                for part in parts:
                    rows = part.shape[0]
                    acc[:, at : at + rows] += contract(xs[u], part[:, cols])
                    at += rows

        return carry

    lax.fori_loop(0, count, unit_step, 0)


def fetch_unit(moves, sems, index, go):
    _, cols = columns_of(index)
    for n, (source, target) in enumerate(moves):
        copy = pltpu.make_async_copy(source.at[:, cols], target.at[:, cols], sems.at[n, index])
        copy.start() if go else copy.wait()


def each_own_unit(first, count, action):
    def unit_step(u, carry):
        mine, _ = columns_of(u)

        @pl.when(mine)
        def _():
            action(u)

        return carry

    lax.fori_loop(first, first + count, unit_step, 0)


def normed_unit(part, factor, gain_ref, index):
    base = unit_of(index) * (UNIT // 128)
    stream = part.astype(jnp.float32)
    lanes = []
    for k in range(UNIT // 128):
        gain = gain_ref[pl.ds(base + k, 1), :]
        lanes.append((stream[:, k * 128 : (k + 1) * 128] * factor * gain).astype(jnp.bfloat16))
    return lanes


def place_unit(xs, rows, n, part, factor, gain, index):
    for k, lane in enumerate(normed_unit(part, factor, gain, index)):
        xs[n, rows, k * 128 : (k + 1) * 128] = lane


VM = pl.BlockSpec(memory_space=pltpu.VMEM)
HBM = pl.BlockSpec(memory_space=pl.ANY)
SM = pl.BlockSpec(memory_space=pltpu.SMEM)


def params(mib):
    return pltpu.CompilerParams(vmem_limit_bytes=mib * 2**20)


def cost(rows, units, width):
    return pl.CostEstimate(
        flops=2 * rows * units * UNIT * width,
        bytes_accessed=2 * units * UNIT * width + 4 * rows * width,
        transcendentals=0,
    )


def stream_rows(s):
    return slice(s * ROWS, (s + 1) * ROWS)


def normed_units(xs, gain, factor, first, *streams):
    for s, units in enumerate(streams):
        for n, unit in enumerate(units):
            place_unit(xs, stream_rows(s), n, unit[...], factor[stream_rows(s), :], gain, first + n)


def early_kernel(a0, a1, a2, a3, b0, b1, b2, b3, gain, factor, *refs):
    query, key, value = refs[:3]
    others = refs[3:6]
    acc, top, bottom, both, xs, sems = refs[6:]
    rows, kv = top.shape[0], key.shape[0]
    moves = (
        (query.at[pl.ds(0, rows), :], top),
        (query.at[pl.ds(rows, rows), :], bottom),
        (key, both.at[pl.ds(0, kv), :]),
        (value, both.at[pl.ds(kv, kv), :]),
    )
    each_own_unit(0, RING, lambda u: fetch_unit(moves, sems, u, True))
    normed_units(xs, gain, factor, 0, (a0, a1, a2, a3), (b0, b1, b2, b3))
    acc[...] = jnp.zeros_like(acc)
    wait = lambda u: fetch_unit(moves, sems, u, False)
    add_units(xs, acc, (top, bottom, both), others, 0, 4, wait)
    each_own_unit(4, 4, wait)


def middle_kernel(a4, a5, b4, b5, gain, factor, acc_in, *refs):
    *weights, acc, xs = refs
    normed_units(xs, gain, factor, 4, (a4, a5), (b4, b5))
    acc[...] = acc_in[...]
    add_units(xs, acc, weights[:3], weights[3:], 4, 2)


def project_first_kernel(a6, a7, b6, gain, factor, acc_in, *refs):
    *weights, first, second, acc, xs, late = refs
    normed_units(xs, gain, factor, 6, (a6,), (b6,))
    normed_units(late, gain, factor, 7, (a7,))
    acc[...] = acc_in[...]
    add_units(xs, acc, weights[:3], weights[3:], 6, 1)
    first[...] = acc[:ROWS, :]
    second[...] = acc[ROWS:, :]
    add_units(late, first, weights[:3], weights[3:], 7, 1)


def project_second_kernel(b7, gain, factor, acc_in, *refs):
    *weights, acc, late = refs
    place_unit(late, slice(0, ROWS), 0, b7[...], factor[ROWS:, :], gain, 7)
    acc[...] = acc_in[...]
    add_units(late, acc, weights[:3], weights[3:], 7, 1)


def turned_heads(part, cosine, sine):
    lane = lax.broadcasted_iota(jnp.int32, part.shape, 1)
    other = jnp.where(lane % 2 == 0, pltpu.roll(part, HD - 1, 1), pltpu.roll(part, 1, 1))
    return (part * cosine + other * sine).astype(jnp.bfloat16)


def attend_kernel(half, lens, acc, cosine, sine, *refs):
    if half:
        key_early, value_early = refs[:2]
    attended, key_out, value_out = refs[-3:]
    rows = stream_rows(half)
    heads = UNIT // HD
    cos, sin = cosine[rows, :], sine[rows, :]
    key = turned_heads(acc[:, UNIT : UNIT + HD], cos, sin)
    value = acc[:, UNIT + HD :].astype(jnp.bfloat16)
    key_out[...] = key
    value_out[...] = value
    if half:
        key = jnp.concatenate([key_early[...], key], axis=0)
        value = jnp.concatenate([value_early[...], value], axis=0)
    shape = (ROWS, (half + 1) * ROWS)
    row = lax.broadcasted_iota(jnp.int32, shape, 0) + half * ROWS
    col = lax.broadcasted_iota(jnp.int32, shape, 1)
    row_request = jnp.zeros(shape, jnp.int32)
    col_request = jnp.zeros(shape, jnp.int32)
    end = jnp.int32(0)
    for k in range(lens.shape[1]):
        end = end + lens[0, k]
        row_request += (row >= end).astype(jnp.int32)
        col_request += (col >= end).astype(jnp.int32)
    keep = (row_request == col_request) & (row >= col)
    queries = [turned_heads(acc[:, h * HD : (h + 1) * HD], cos, sin) for h in range(heads)]
    scores = contract(jnp.concatenate(queries, axis=0), key) * (1.0 / math.sqrt(HD))
    scores = jnp.where(keep[None], scores.reshape(heads, *shape), -1e30)
    weights = jnp.exp(scores - jnp.max(scores, axis=2, keepdims=True))
    probs = (weights / jnp.sum(weights, axis=2, keepdims=True)).astype(jnp.bfloat16)
    probs = probs.reshape(heads * ROWS, shape[1])
    out = jnp.dot(probs, value, preferred_element_type=jnp.float32).astype(jnp.bfloat16)
    for h in range(heads):
        attended[:, h * HD : (h + 1) * HD] = out[h * ROWS : (h + 1) * ROWS, :]


def stream_units(xs, *streams):
    for s, units in enumerate(streams):
        for n, unit in enumerate(units):
            xs[n, stream_rows(s), :] = unit[...]


def out_early_kernel(a0, a1, a2, a3, b0, b1, b2, b3, w0, w1, acc, xs):
    stream_units(xs, (a0, a1, a2, a3), (b0, b1, b2, b3))
    acc[...] = jnp.zeros_like(acc)
    add_units(xs, acc, (w0,), (w1,), 0, 4)


def out_middle_kernel(a4, a5, b4, b5, acc_in, hidden, w0, w1, acc, xs):
    stream_units(xs, (a4, a5), (b4, b5))
    acc[...] = acc_in[...] + hidden[...].astype(jnp.float32)
    add_units(xs, acc, (w0,), (w1,), 4, 2)


def out_first_kernel(a6, a7, b6, acc_in, w0, w1, out, second, acc, first, xs, late):
    stream_units(xs, (a6,), (b6,))
    stream_units(late, (a7,))
    acc[...] = acc_in[...]
    add_units(xs, acc, (w0,), (w1,), 6, 1)
    first[...] = acc[:ROWS, :]
    second[...] = acc[ROWS:, :]
    add_units(late, first, (w0,), (w1,), 7, 1)
    out[...] = first[...].astype(jnp.bfloat16)


def out_second_kernel(b7, acc_in, w0, w1, partial, out, acc, late):
    stream_units(late, (b7,))
    acc[...] = acc_in[...]
    add_units(late, acc, (w0,), (w1,), 7, 1)
    out[...] = acc[...].astype(jnp.bfloat16)


def summed_over_tp(value):
    for bits in ((1, 2), (2, 1), (4, 4)):
        pairs = [(t * 2 + p, (t ^ bits[p]) * 2 + p) for t in range(RING) for p in range(2)]
        value = value + lax.ppermute(value, ("tp", "pair"), pairs)
    return value


def kernel_call(kernel, **options):
    return pl.pallas_call(kernel, **options)


def in_vmem(value):
    return pltpu.with_memory_space_constraint(value, pltpu.VMEM)


def in_hbm(value):
    return pltpu.with_memory_space_constraint(value, pltpu.HBM)


def split_kernel(hidden, first, second, sems):
    copies = [
        pltpu.make_async_copy(hidden.at[pl.ds(s * ROWS, ROWS), :], target, sems.at[s])
        for s, target in enumerate((first, second))
    ]
    for copy in copies:
        copy.start()
    for copy in copies:
        copy.wait()


def angle_kernel(lens, freq, angle):
    place = lax.broadcasted_iota(jnp.int32, angle.shape, 0)
    position = place
    end = jnp.int32(0)
    for k in range(lens.shape[1]):
        end = end + lens[0, k]
        position = position - jnp.where(end <= place, lens[0, k], 0)
    angle[...] = position.astype(jnp.float32) * freq[...]


def after(value, *others):
    return lax.optimization_barrier((value, *others))


def ring_body(*args):
    return ring_layer(*args)


def ring_layer(hidden_in, norm_gain, query_weight, key_weight, value_weight, output_weight, lengths):
    f32, bf16 = jnp.float32, jnp.bfloat16
    rows_shape = jax.ShapeDtypeStruct((ROWS, UNIT), bf16)
    a0, b0 = kernel_call(
        split_kernel,
        out_shape=(rows_shape, rows_shape),
        in_specs=[HBM],
        out_specs=(VM, VM),
        scratch_shapes=[pltpu.SemaphoreType.DMA((2,))],
        compiler_params=params(2),
    )(in_hbm(hidden_in))
    a1, b1 = swapped(a0, 0), swapped(b0, 0)
    a2, b2 = swapped(a0, 1), swapped(b0, 1)
    projections = (query_weight, key_weight, value_weight)
    others = []
    for w in projections:
        others.append(in_vmem(partner(w, "pair", 0)))
    qkv = sum(w.shape[0] for w in projections)
    stream = hidden_in.astype(f32)
    squares = jnp.sum(stream * stream, axis=1).reshape(2, 128)
    squares = summed_over_tp(squares)
    factor = lax.rsqrt(squares / (RING * UNIT) + 1e-05)
    factor = jnp.broadcast_to(factor.reshape(STRETCH, 1), (STRETCH, 128))
    gain = norm_gain.reshape(RING * UNIT // 128, 128)
    lane = jnp.arange(HD, dtype=jnp.int32)
    angle = kernel_call(
        angle_kernel,
        out_shape=jax.ShapeDtypeStruct((STRETCH, HD), f32),
        in_specs=[SM, VM],
        out_specs=VM,
        compiler_params=params(2),
    )(lengths, scaled_freq(lane - lane % 2)[None, :])
    cosine = jnp.cos(angle)
    sine = jnp.sin(angle) * jnp.where(lane % 2 == 0, -1.0, 1.0)[None, :]
    a3, b3 = swapped(a1, 1), swapped(b1, 1)
    a4, b4 = swapped(a2, 0), swapped(b2, 0)
    other_output = in_vmem(partner(output_weight, "pair", 0))
    a5, b5 = swapped(a3, 0), swapped(b3, 0)
    a6, b6 = swapped(a4, 1), swapped(b4, 1)
    factor, cosine, sine, lengths = after(factor, cosine, sine, lengths)
    acc_shape = jax.ShapeDtypeStruct((STRETCH, qkv), f32)
    columns = query_weight.shape[1]
    half_query = jax.ShapeDtypeStruct((query_weight.shape[0] // 2, columns), bf16)
    both = jax.ShapeDtypeStruct((qkv - query_weight.shape[0], columns), bf16)
    acc, *own = kernel_call(
        early_kernel,
        out_shape=(acc_shape, half_query, half_query, both),
        in_specs=[VM] * 10 + [HBM] * 3 + [VM] * 3,
        out_specs=(VM,) * 4,
        scratch_shapes=[
            pltpu.VMEM((4, STRETCH, UNIT), bf16),
            pltpu.SemaphoreType.DMA((4, RING)),
        ],
        compiler_params=params(10),
        cost_estimate=cost(STRETCH, 4, qkv),
    )(
        *(a0, a1, a2, a3, b0, b1, b2, b3, gain, factor),
        *(in_hbm(w) for w in projections),
        *others,
    )
    weights = (*own, *others)
    a5, acc = after(a5, acc)
    a7, b7 = swapped(a5, 1), swapped(b5, 1)
    acc = kernel_call(
        middle_kernel,
        out_shape=acc_shape,
        in_specs=[VM] * 13,
        out_specs=VM,
        scratch_shapes=[pltpu.VMEM((2, STRETCH, UNIT), bf16)],
        compiler_params=params(8),
        cost_estimate=cost(STRETCH, 2, qkv),
    )(a4, a5, b4, b5, gain, factor, acc, *weights)
    half_shape = jax.ShapeDtypeStruct((ROWS, qkv), f32)
    first, second = kernel_call(
        project_first_kernel,
        out_shape=(half_shape, half_shape),
        in_specs=[VM] * 12,
        out_specs=(VM, VM),
        scratch_shapes=[
            pltpu.VMEM((STRETCH, qkv), f32),
            pltpu.VMEM((1, STRETCH, UNIT), bf16),
            pltpu.VMEM((1, ROWS, UNIT), bf16),
        ],
        compiler_params=params(8),
        cost_estimate=cost(STRETCH, 2, qkv),
    )(a6, a7, b6, gain, factor, acc, *weights)

    def attend_stream(half, projected, early):
        kv = jax.ShapeDtypeStruct((ROWS, HD), bf16)
        return kernel_call(
            lambda *refs: attend_kernel(half, *refs),
            out_shape=(jax.ShapeDtypeStruct((ROWS, UNIT), bf16), kv, kv),
            in_specs=[SM] + [VM] * (3 + len(early)),
            out_specs=(VM, VM, VM),
            compiler_params=params(8),
            cost_estimate=cost(ROWS, 2, qkv),
        )(lengths, projected, cosine, sine, *early)

    a0, key_a, value_a = attend_stream(0, first, ())
    a1, a2 = swapped(a0, 0), swapped(a0, 1)
    projected = kernel_call(
        project_second_kernel,
        out_shape=half_shape,
        in_specs=[VM] * 10,
        out_specs=VM,
        scratch_shapes=[pltpu.VMEM((1, ROWS, UNIT), bf16)],
        compiler_params=params(10),
        cost_estimate=cost(ROWS, 1, qkv),
    )(b7, gain, factor, second, *weights)
    a3 = swapped(a1, 1)
    b0, _, _ = attend_stream(1, projected, (key_a, value_a))
    b1, b2 = swapped(b0, 0), swapped(b0, 1)
    a4, b3 = swapped(a2, 0), swapped(b1, 1)
    a5, b4 = swapped(a3, 0), swapped(b2, 0)
    a6, b5 = swapped(a4, 1), swapped(b3, 0)
    width = output_weight.shape[0]
    acc_shape = jax.ShapeDtypeStruct((STRETCH, width), f32)
    acc = kernel_call(
        out_early_kernel,
        out_shape=acc_shape,
        in_specs=[VM] * 10,
        out_specs=VM,
        scratch_shapes=[pltpu.VMEM((4, STRETCH, UNIT), bf16)],
        compiler_params=params(10),
        cost_estimate=cost(STRETCH, 4, width),
    )(a0, a1, a2, a3, b0, b1, b2, b3, output_weight, other_output)
    a5, acc = after(a5, acc)
    a7, b6, b7 = swapped(a5, 1), swapped(b4, 1), swapped(b5, 1)
    acc = kernel_call(
        out_middle_kernel,
        out_shape=acc_shape,
        in_specs=[VM] * 8,
        out_specs=VM,
        scratch_shapes=[pltpu.VMEM((2, STRETCH, UNIT), bf16)],
        compiler_params=params(8),
        cost_estimate=cost(STRETCH, 2, width),
    )(a4, a5, b4, b5, acc, hidden_in, output_weight, other_output)

    out_shape = jax.ShapeDtypeStruct((STRETCH, UNIT), bf16)
    half_shape = jax.ShapeDtypeStruct((ROWS, width), f32)
    half = pltpu.VMEM((ROWS, width), f32)
    late = pltpu.VMEM((1, ROWS, UNIT), bf16)
    out, acc = kernel_call(
        out_first_kernel,
        grid=(1,),
        out_shape=(out_shape, half_shape),
        in_specs=[VM] * 6,
        out_specs=(pl.BlockSpec((ROWS, UNIT), lambda i: (0, 0)), VM),
        scratch_shapes=[
            pltpu.VMEM((STRETCH, width), f32),
            half,
            pltpu.VMEM((1, STRETCH, UNIT), bf16),
            late,
        ],
        compiler_params=params(8),
        cost_estimate=cost(STRETCH, 2, width),
    )(a6, a7, b6, acc, output_weight, other_output)
    return kernel_call(
        out_second_kernel,
        grid=(1,),
        out_shape=out_shape,
        in_specs=[VM] * 4 + [HBM],
        out_specs=pl.BlockSpec((ROWS, UNIT), lambda i: (1, 0)),
        scratch_shapes=[half, late],
        input_output_aliases={4: 0},
        compiler_params=params(8),
        cost_estimate=cost(ROWS, 1, width),
    )(b7, acc, output_weight, other_output, out)


def fits_ring(mesh):
    return dict(mesh.shape)["tp"] == RING and dict(mesh.shape)["pair"] == 2


def solution(mesh):
    placed = (
        P(("group", "pair"), "tp"),
        P(),
        P("tp", "pair"),
        P("tp", "pair"),
        P("tp", "pair"),
        P("tp", "pair"),
        P(("group", "pair"), None),
    )
    body = ring_body if fits_ring(mesh) else general_body
    step = jax.shard_map(
        body, mesh=mesh, in_specs=placed, out_specs=P(("group", "pair"), "tp"), check_vma=False
    )
    if not fits_ring(mesh):
        return step
    return step
```

```python
import math

import jax
import jax.numpy as jnp
from jax import lax
from jax.experimental import pallas as pl
from jax.experimental.pallas import tpu as pltpu

from jax.sharding import PartitionSpec as P

HQ = 64
KVH = 8
HD = 128
STRETCH = 256


THETA = 500000.0


def shortened(shard):

    def short(part):
        return part.astype(jnp.bfloat16) if part.dtype == jnp.float32 else part

    return jax.tree.map(short, shard)


def partner(shard, axis, apart):
    return lax.ppermute(shard, axis, [(i, i ^ 1 << apart) for i in range(lax.axis_size(axis))])


def token_layout(lengths):
    ends = jnp.cumsum(lengths, axis=1)
    offsets = jnp.arange(STRETCH, dtype=jnp.int32)
    finished = ends[:, None, :] <= offsets[None, :, None]
    request = jnp.sum(finished.astype(jnp.int32), axis=2)
    position = offsets[None, :] - jnp.sum(jnp.where(finished, lengths[:, None, :], 0), axis=2)
    return (request, position)


def scaled_freq(dims):
    freq = jnp.exp(dims.astype(jnp.float32) * (-math.log(THETA) / HD))
    wavelen = 2.0 * math.pi / freq
    smooth = (8192.0 / wavelen - 1.0) / 3.0
    middle = (1.0 - smooth) * freq / 8.0 + smooth * freq
    return jnp.where(wavelen < 2048.0, freq, jnp.where(wavelen > 8192.0, freq / 8.0, middle))


def rotary(projected, position, dims):
    freq = scaled_freq(dims[0::2])
    angle = position.astype(jnp.float32)[:, None] * freq[None, :]
    cosine = jnp.cos(angle)
    sine = jnp.sin(angle)
    first = projected[:, 0::2]
    second = projected[:, 1::2]
    turned = jnp.stack([first * cosine - second * sine, first * sine + second * cosine], axis=-1)
    return turned.reshape(projected.shape)


def attend(query, key, value, request, stretches, heads, groups):
    repeat = heads // groups
    query_blocks = query.reshape(stretches, STRETCH, groups, repeat, HD)
    key_blocks = key.reshape(stretches, STRETCH, groups, HD)
    value_blocks = value.reshape(stretches, STRETCH, groups, HD)
    scores = jnp.einsum(
        "cqgrd,ckgd->cgrqk", query_blocks, key_blocks, preferred_element_type=jnp.float32
    ) * (1.0 / math.sqrt(HD))
    offsets = jnp.arange(STRETCH, dtype=jnp.int32)
    keep = (request[:, :, None] == request[:, None, :]) & (offsets[:, None] >= offsets[None, :])[
        None
    ]
    scores = jnp.where(keep[:, None, None], scores, -1e30)
    top = jnp.max(scores, axis=-1, keepdims=True)
    weights = jnp.exp(scores - top)
    probs = (weights / jnp.sum(weights, axis=-1, keepdims=True)).astype(jnp.bfloat16)
    attended = jnp.einsum(
        "cgrqk,ckgd->cqgrd", probs, value_blocks, preferred_element_type=jnp.float32
    )
    return attended.reshape(stretches * STRETCH, heads * HD).astype(jnp.bfloat16)


def contract(left, right):
    return lax.dot_general(
        left, right, (((1,), (1,)), ((), ())), preferred_element_type=jnp.float32
    )


def bit_count(number):
    return number.bit_length() - 1


def assemble(parts, needed_bits, device, axis):
    for bit_index in range(max(needed_bits)):
        moving = [piece for piece, needed in zip(parts, needed_bits) if bit_index < needed]
        widths = [piece.shape[axis] for piece in moving]
        sent = jnp.concatenate(moving, axis=axis)
        arrived = partner(shortened(sent), "tp", bit_index).astype(sent.dtype)
        upper = device // 2**bit_index % 2 == 1
        cuts = []
        running = 0
        for width in widths[:-1]:
            running = running + width
            cuts.append(running)
        received = jnp.split(arrived, cuts, axis=axis)
        joined = []
        counter = 0
        for piece, needed in zip(parts, needed_bits):
            if bit_index < needed:
                other = received[counter]
                counter = counter + 1
                piece = jnp.where(
                    upper,
                    jnp.concatenate([other, piece], axis=axis),
                    jnp.concatenate([piece, other], axis=axis),
                )
            joined.append(piece)
        parts = joined
    return parts


def project(normed, query_rows, key_rows, value_rows, output_rows):
    query_full, key_full, value_full, output_full = (
        lax.all_gather(query_rows, "pair", axis=1, tiled=True),
        lax.all_gather(key_rows, "pair", axis=1, tiled=True),
        lax.all_gather(value_rows, "pair", axis=1, tiled=True),
        lax.all_gather(output_rows, "pair", axis=1, tiled=True),
    )
    query_pre = contract(normed, query_full)
    key_pre = contract(normed, key_full)
    value_pre = contract(normed, value_full)
    return (query_pre, key_pre, value_pre, output_full)


def general_body(hidden_in, norm_gain, query_weight, key_weight, value_weight, output_weight, lengths):
    tp_count = lax.axis_size("tp")
    device = lax.axis_index("tp")
    query_bits = bit_count(max(1, tp_count // HQ))
    group_bits = bit_count(max(1, tp_count // KVH))
    needed_bits = [query_bits, group_bits, group_bits]
    query_cols = query_weight.shape[0]
    stretches = lengths.shape[0]
    request, position = token_layout(lengths)
    position = position.reshape(-1)
    full_rows = lax.all_gather(hidden_in, "tp", axis=1, tiled=True)
    stream = full_rows.astype(jnp.float32)
    mean_square = jnp.mean(stream * stream, axis=1, keepdims=True)
    normed = (stream * lax.rsqrt(mean_square + 1e-05) * norm_gain[None, :]).astype(jnp.bfloat16)
    query_block, key_block, value_block = assemble(
        [query_weight, key_weight, value_weight], needed_bits, device, 0
    )
    query_pre, key_pre, value_pre, output_full = project(
        normed, query_block, key_block, value_block, output_weight
    )
    query_dims = jnp.arange(query_pre.shape[1], dtype=jnp.int32) % HD
    key_dims = jnp.arange(key_pre.shape[1], dtype=jnp.int32) % HD
    query = rotary(query_pre, position, query_dims).astype(jnp.bfloat16)
    key = rotary(key_pre, position, key_dims).astype(jnp.bfloat16)
    value = value_pre.astype(jnp.bfloat16)
    heads = query.shape[1] // HD
    groups = key.shape[1] // HD
    attended = attend(query, key, value, request, stretches, heads, groups)
    own_start = device * query_cols % (heads * HD)
    own_columns = lax.dynamic_slice_in_dim(attended, own_start, query_cols, 1)
    projected = contract(lax.all_gather(own_columns, "tp", axis=1, tiled=True), output_full)
    return (hidden_in.astype(jnp.float32) + projected).astype(jnp.bfloat16)


RING = 8
ROWS = STRETCH // 2
UNIT = 1024
ORDER = (0, 1, -1, -2, 2, 3, -3, -4)


def ring_place(t):
    return t // 2 if t % 2 == 0 else RING - 1 - t // 2


def ring_member(place):
    return 2 * place if place < RING // 2 else 2 * RING - 1 - 2 * place


def ring_swap(later):
    pairs = []
    for t in range(RING):
        for p in range(2):
            place = ring_place(t)
            step = 1 if (place + p + later) % 2 == 0 else -1
            pairs.append((t * 2 + p, ring_member((place + step) % RING) * 2 + p))
    return pairs


def swapped(shard, later):
    return lax.ppermute(shard, ("tp", "pair"), ring_swap(later))


def unit_of(index):
    t = lax.axis_index("tp")
    place = jnp.where(t % 2 == 0, t // 2, RING - 1 - t // 2)
    step = 1 - 2 * ((place + lax.axis_index("pair")) % 2)
    offset = jnp.int32(ORDER[0])
    for k in range(1, len(ORDER)):
        offset = jnp.where(index == k, ORDER[k], offset)
    where = (place + offset * step + RING) % RING
    return jnp.where(where < RING // 2, 2 * where, 2 * RING - 1 - 2 * where)


def columns_of(index):
    t = unit_of(index)
    mine = t // (RING // 2) == lax.axis_index("pair")
    return mine, pl.ds(pl.multiple_of(t % (RING // 2) * UNIT, UNIT), UNIT)


def add_units(xs, acc, own, others, first, count, ready=None):
    def unit_step(u, carry):
        mine, cols = columns_of(first + u)
        for here, parts in ((mine, own), (jnp.logical_not(mine), others)):

            @pl.when(here)
            def _(parts=parts):
                if ready is not None and parts is own:
                    ready(first + u)
                at = 0
                for part in parts:
                    rows = part.shape[0]
                    acc[:, at : at + rows] += contract(xs[u], part[:, cols])
                    at += rows

        return carry

    lax.fori_loop(0, count, unit_step, 0)


def fetch_unit(moves, sems, index, go):
    _, cols = columns_of(index)
    for n, (source, target) in enumerate(moves):
        copy = pltpu.make_async_copy(source.at[:, cols], target.at[:, cols], sems.at[n, index])
        copy.start() if go else copy.wait()


def each_own_unit(first, count, action):
    def unit_step(u, carry):
        mine, _ = columns_of(u)

        @pl.when(mine)
        def _():
            action(u)

        return carry

    lax.fori_loop(first, first + count, unit_step, 0)


def normed_unit(part, factor, gain_ref, index):
    base = unit_of(index) * (UNIT // 128)
    stream = part.astype(jnp.float32)
    lanes = []
    for k in range(UNIT // 128):
        gain = gain_ref[pl.ds(base + k, 1), :]
        lanes.append((stream[:, k * 128 : (k + 1) * 128] * factor * gain).astype(jnp.bfloat16))
    return lanes


def place_unit(xs, rows, n, part, factor, gain, index):
    for k, lane in enumerate(normed_unit(part, factor, gain, index)):
        xs[n, rows, k * 128 : (k + 1) * 128] = lane


VM = pl.BlockSpec(memory_space=pltpu.VMEM)
HBM = pl.BlockSpec(memory_space=pl.ANY)
SM = pl.BlockSpec(memory_space=pltpu.SMEM)


def params(mib):
    return pltpu.CompilerParams(vmem_limit_bytes=mib * 2**20)


def cost(rows, units, width):
    return pl.CostEstimate(
        flops=2 * rows * units * UNIT * width,
        bytes_accessed=2 * units * UNIT * width + 4 * rows * width,
        transcendentals=0,
    )


def stream_rows(s):
    return slice(s * ROWS, (s + 1) * ROWS)


def normed_units(xs, gain, factor, first, *streams):
    for s, units in enumerate(streams):
        for n, unit in enumerate(units):
            place_unit(xs, stream_rows(s), n, unit[...], factor[stream_rows(s), :], gain, first + n)


def early_kernel(a0, a1, a2, a3, b0, b1, b2, b3, gain, factor, *refs):
    query, key, value = refs[:3]
    others = refs[3:6]
    acc, top, bottom, both, xs, sems = refs[6:]
    rows, kv = top.shape[0], key.shape[0]
    moves = (
        (query.at[pl.ds(0, rows), :], top),
        (query.at[pl.ds(rows, rows), :], bottom),
        (key, both.at[pl.ds(0, kv), :]),
        (value, both.at[pl.ds(kv, kv), :]),
    )
    each_own_unit(0, RING, lambda u: fetch_unit(moves, sems, u, True))
    normed_units(xs, gain, factor, 0, (a0, a1, a2, a3), (b0, b1, b2, b3))
    acc[...] = jnp.zeros_like(acc)
    wait = lambda u: fetch_unit(moves, sems, u, False)
    add_units(xs, acc, (top, bottom, both), others, 0, 4, wait)
    each_own_unit(4, 4, wait)


def middle_kernel(a4, a5, a6, b4, b5, b6, gain, factor, acc_in, *refs):
    *weights, first, second, acc, xs = refs
    normed_units(xs, gain, factor, 4, (a4, a5, a6), (b4, b5, b6))
    acc[...] = acc_in[...]
    add_units(xs, acc, weights[:3], weights[3:], 4, 3)
    first[...] = acc[:ROWS, :]
    second[...] = acc[ROWS:, :]


def project_kernel(half, unit, gain, factor, acc_in, *refs):
    *weights, acc, late = refs
    place_unit(late, slice(0, ROWS), 0, unit[...], factor[stream_rows(half), :], gain, 7)
    acc[...] = acc_in[...]
    add_units(late, acc, weights[:3], weights[3:], 7, 1)


def turned_heads(part, cosine, sine):
    lane = lax.broadcasted_iota(jnp.int32, part.shape, 1)
    other = jnp.where(lane % 2 == 0, pltpu.roll(part, HD - 1, 1), pltpu.roll(part, 1, 1))
    return (part * cosine + other * sine).astype(jnp.bfloat16)


def attend_kernel(half, lens, acc, cosine, sine, *refs):
    if half:
        key_early, value_early = refs[:2]
    attended, key_out, value_out = refs[-3:]
    rows = stream_rows(half)
    heads = UNIT // HD
    cos, sin = cosine[rows, :], sine[rows, :]
    key = turned_heads(acc[:, UNIT : UNIT + HD], cos, sin)
    value = acc[:, UNIT + HD :].astype(jnp.bfloat16)
    key_out[...] = key
    value_out[...] = value
    if half:
        key = jnp.concatenate([key_early[...], key], axis=0)
        value = jnp.concatenate([value_early[...], value], axis=0)
    shape = (ROWS, (half + 1) * ROWS)
    row = lax.broadcasted_iota(jnp.int32, shape, 0) + half * ROWS
    col = lax.broadcasted_iota(jnp.int32, shape, 1)
    row_request = jnp.zeros(shape, jnp.int32)
    col_request = jnp.zeros(shape, jnp.int32)
    end = jnp.int32(0)
    for k in range(lens.shape[1]):
        end = end + lens[0, k]
        row_request += (row >= end).astype(jnp.int32)
        col_request += (col >= end).astype(jnp.int32)
    keep = (row_request == col_request) & (row >= col)
    queries = [turned_heads(acc[:, h * HD : (h + 1) * HD], cos, sin) for h in range(heads)]
    scores = contract(jnp.concatenate(queries, axis=0), key) * (1.0 / math.sqrt(HD))
    scores = jnp.where(keep[None], scores.reshape(heads, *shape), -1e30)
    weights = jnp.exp(scores - jnp.max(scores, axis=2, keepdims=True))
    probs = (weights / jnp.sum(weights, axis=2, keepdims=True)).astype(jnp.bfloat16)
    probs = probs.reshape(heads * ROWS, shape[1])
    out = jnp.dot(probs, value, preferred_element_type=jnp.float32).astype(jnp.bfloat16)
    for h in range(heads):
        attended[:, h * HD : (h + 1) * HD] = out[h * ROWS : (h + 1) * ROWS, :]


def stream_units(xs, *streams):
    for s, units in enumerate(streams):
        for n, unit in enumerate(units):
            xs[n, stream_rows(s), :] = unit[...]


def out_early_kernel(a0, a1, a2, a3, b0, b1, b2, b3, w0, w1, acc, xs):
    stream_units(xs, (a0, a1, a2, a3), (b0, b1, b2, b3))
    acc[...] = jnp.zeros_like(acc)
    add_units(xs, acc, (w0,), (w1,), 0, 4)


def out_middle_kernel(a4, a5, a6, b4, b5, b6, acc_in, hidden, w0, w1, acc, xs):
    stream_units(xs, (a4, a5, a6), (b4, b5, b6))
    acc[...] = acc_in[...] + hidden[...].astype(jnp.float32)
    add_units(xs, acc, (w0,), (w1,), 4, 3)


def out_last_kernel(a7, b7, acc, w0, w1, out, xs):
    width = out.shape[1]
    block = pl.ds(pl.multiple_of(pl.program_id(0) * width, width), width)
    stream_units(xs, (a7,), (b7,))
    mine, cols = columns_of(7)
    for here, part in ((mine, w0), (jnp.logical_not(mine), w1)):

        @pl.when(here)
        def _(part=part):
            total = acc[:, block] + contract(xs[0], part[block, cols])
            out[...] = total.astype(jnp.bfloat16)


def summed_over_tp(value):
    for bits in ((1, 2), (2, 1), (4, 4)):
        pairs = [(t * 2 + p, (t ^ bits[p]) * 2 + p) for t in range(RING) for p in range(2)]
        value = value + lax.ppermute(value, ("tp", "pair"), pairs)
    return value


def kernel_call(kernel, **options):
    return pl.pallas_call(kernel, **options)


def in_vmem(value):
    return pltpu.with_memory_space_constraint(value, pltpu.VMEM)


def in_hbm(value):
    return pltpu.with_memory_space_constraint(value, pltpu.HBM)


def split_kernel(hidden, first, second, sems):
    copies = [
        pltpu.make_async_copy(hidden.at[pl.ds(s * ROWS, ROWS), :], target, sems.at[s])
        for s, target in enumerate((first, second))
    ]
    for copy in copies:
        copy.start()
    for copy in copies:
        copy.wait()


def angle_kernel(lens, freq, angle):
    place = lax.broadcasted_iota(jnp.int32, angle.shape, 0)
    position = place
    end = jnp.int32(0)
    for k in range(lens.shape[1]):
        end = end + lens[0, k]
        position = position - jnp.where(end <= place, lens[0, k], 0)
    angle[...] = position.astype(jnp.float32) * freq[...]


def after(value, *others):
    return lax.optimization_barrier((value, *others))


def ring_body(*args):
    return ring_layer(*args)


def ring_layer(hidden_in, norm_gain, query_weight, key_weight, value_weight, output_weight, lengths):
    f32, bf16 = jnp.float32, jnp.bfloat16
    rows_shape = jax.ShapeDtypeStruct((ROWS, UNIT), bf16)
    a0, b0 = kernel_call(
        split_kernel,
        out_shape=(rows_shape, rows_shape),
        in_specs=[HBM],
        out_specs=(VM, VM),
        scratch_shapes=[pltpu.SemaphoreType.DMA((2,))],
        compiler_params=params(2),
    )(in_hbm(hidden_in))
    a1, b1 = swapped(a0, 0), swapped(b0, 0)
    a2, b2 = swapped(a0, 1), swapped(b0, 1)
    projections = (query_weight, key_weight, value_weight)
    others = []
    for w in projections:
        others.append(in_vmem(partner(w, "pair", 0)))
    qkv = sum(w.shape[0] for w in projections)
    stream = hidden_in.astype(f32)
    squares = jnp.sum(stream * stream, axis=1).reshape(2, 128)
    squares = summed_over_tp(squares)
    factor = lax.rsqrt(squares / (RING * UNIT) + 1e-05)
    factor = jnp.broadcast_to(factor.reshape(STRETCH, 1), (STRETCH, 128))
    gain = norm_gain.reshape(RING * UNIT // 128, 128)
    lane = jnp.arange(HD, dtype=jnp.int32)
    angle = kernel_call(
        angle_kernel,
        out_shape=jax.ShapeDtypeStruct((STRETCH, HD), f32),
        in_specs=[SM, VM],
        out_specs=VM,
        compiler_params=params(2),
    )(lengths, scaled_freq(lane - lane % 2)[None, :])
    cosine = jnp.cos(angle)
    sine = jnp.sin(angle) * jnp.where(lane % 2 == 0, -1.0, 1.0)[None, :]
    a3, b3 = swapped(a1, 1), swapped(b1, 1)
    a4, b4 = swapped(a2, 0), swapped(b2, 0)
    other_output = in_vmem(partner(output_weight, "pair", 0))
    a5, b5 = swapped(a3, 0), swapped(b3, 0)
    a6, b6 = swapped(a4, 1), swapped(b4, 1)
    factor, cosine, sine, lengths = after(factor, cosine, sine, lengths)
    acc_shape = jax.ShapeDtypeStruct((STRETCH, qkv), f32)
    columns = query_weight.shape[1]
    half_query = jax.ShapeDtypeStruct((query_weight.shape[0] // 2, columns), bf16)
    both = jax.ShapeDtypeStruct((qkv - query_weight.shape[0], columns), bf16)
    acc, *own = kernel_call(
        early_kernel,
        out_shape=(acc_shape, half_query, half_query, both),
        in_specs=[VM] * 10 + [HBM] * 3 + [VM] * 3,
        out_specs=(VM,) * 4,
        scratch_shapes=[
            pltpu.VMEM((4, STRETCH, UNIT), bf16),
            pltpu.SemaphoreType.DMA((4, RING)),
        ],
        compiler_params=params(10),
        cost_estimate=cost(STRETCH, 4, qkv),
    )(
        *(a0, a1, a2, a3, b0, b1, b2, b3, gain, factor),
        *(in_hbm(w) for w in projections),
        *others,
    )
    weights = (*own, *others)
    a5, acc = after(a5, acc)
    a7, b7 = swapped(a5, 1), swapped(b5, 1)
    half_shape = jax.ShapeDtypeStruct((ROWS, qkv), f32)
    first, second = kernel_call(
        middle_kernel,
        out_shape=(half_shape, half_shape),
        in_specs=[VM] * 15,
        out_specs=(VM, VM),
        scratch_shapes=[pltpu.VMEM((STRETCH, qkv), f32), pltpu.VMEM((3, STRETCH, UNIT), bf16)],
        compiler_params=params(10),
        cost_estimate=cost(STRETCH, 3, qkv),
    )(a4, a5, a6, b4, b5, b6, gain, factor, acc, *weights)

    def project(half, unit, partial):
        return kernel_call(
            lambda *refs: project_kernel(half, *refs),
            out_shape=half_shape,
            in_specs=[VM] * 10,
            out_specs=VM,
            scratch_shapes=[pltpu.VMEM((1, ROWS, UNIT), bf16)],
            compiler_params=params(8),
            cost_estimate=cost(ROWS, 1, qkv),
        )(unit, gain, factor, partial, *weights)

    def attend_stream(half, projected, early):
        kv = jax.ShapeDtypeStruct((ROWS, HD), bf16)
        return kernel_call(
            lambda *refs: attend_kernel(half, *refs),
            out_shape=(jax.ShapeDtypeStruct((ROWS, UNIT), bf16), kv, kv),
            in_specs=[SM] + [VM] * (3 + len(early)),
            out_specs=(VM, VM, VM),
            compiler_params=params(8),
            cost_estimate=cost(ROWS, 2, qkv),
        )(lengths, projected, cosine, sine, *early)

    a0, key_a, value_a = attend_stream(0, project(0, a7, first), ())
    a1, a2 = swapped(a0, 0), swapped(a0, 1)
    projected = project(1, b7, second)
    a3 = swapped(a1, 1)
    b0, _, _ = attend_stream(1, projected, (key_a, value_a))
    b1, b2 = swapped(b0, 0), swapped(b0, 1)
    a4, b3 = swapped(a2, 0), swapped(b1, 1)
    a5, b4 = swapped(a3, 0), swapped(b2, 0)
    a6, b5 = swapped(a4, 1), swapped(b3, 0)
    width = output_weight.shape[0]
    acc_shape = jax.ShapeDtypeStruct((STRETCH, width), f32)
    acc = kernel_call(
        out_early_kernel,
        out_shape=acc_shape,
        in_specs=[VM] * 10,
        out_specs=VM,
        scratch_shapes=[pltpu.VMEM((4, STRETCH, UNIT), bf16)],
        compiler_params=params(10),
        cost_estimate=cost(STRETCH, 4, width),
    )(a0, a1, a2, a3, b0, b1, b2, b3, output_weight, other_output)
    a5, acc = after(a5, acc)
    a7, b6, b7 = swapped(a5, 1), swapped(b4, 1), swapped(b5, 1)
    acc = kernel_call(
        out_middle_kernel,
        out_shape=acc_shape,
        in_specs=[VM] * 10,
        out_specs=VM,
        scratch_shapes=[pltpu.VMEM((3, STRETCH, UNIT), bf16)],
        compiler_params=params(10),
        cost_estimate=cost(STRETCH, 3, width),
    )(a4, a5, a6, b4, b5, b6, acc, hidden_in, output_weight, other_output)
    return kernel_call(
        out_last_kernel,
        grid=(2,),
        out_shape=jax.ShapeDtypeStruct((STRETCH, width), bf16),
        in_specs=[VM] * 5,
        out_specs=pl.BlockSpec((STRETCH, width // 2), lambda n: (0, n)),
        scratch_shapes=[pltpu.VMEM((1, STRETCH, UNIT), bf16)],
        compiler_params=params(8),
        cost_estimate=cost(STRETCH, 1, width),
    )(a7, b7, acc, output_weight, other_output)


def fits_ring(mesh):
    return dict(mesh.shape)["tp"] == RING and dict(mesh.shape)["pair"] == 2


def solution(mesh):
    placed = (
        P(("group", "pair"), "tp"),
        P(),
        P("tp", "pair"),
        P("tp", "pair"),
        P("tp", "pair"),
        P("tp", "pair"),
        P(("group", "pair"), None),
    )
    body = ring_body if fits_ring(mesh) else general_body
    step = jax.shard_map(
        body, mesh=mesh, in_specs=placed, out_specs=P(("group", "pair"), "tp"), check_vma=False
    )
    if not fits_ring(mesh):
        return step
    return step
```
